128 devices in a mesh: pts: 32 (over x, y, core), top: 4 (over z).
Axes of the slice: x: 4, y: 4, z: 4, core: 2. Of those that a mesh axis runs over, the one named last changes fastest.
Arguments:
- local_pos: float32 [3, 131072], P(None, ('pts', 'top')), may hold values from -1 to 1
- densities: float32 [8, 131072], P(None, ('pts', 'top')), may hold values from -6 to 6
- morton_slot: int32 [131072], P(('pts', 'top')), may hold values from 0 to 131071, as said below
- slot_leaf: int32 [131072], P(('pts', 'top')), may hold values from 0 to 4095, as said below
- uc2e: float32 [152, 152], replicated, may hold values from -0.5 to 0.5
- m2m: float32 [184832], replicated, may hold values from -0.15625 to 0.15625
- m2l_ops: bfloat16 [7300864], replicated, may hold values from -0.02734375 to 0.02734375
- dc2e: float32 [152, 152], replicated, may hold values from -0.5 to 0.5
- lattice: float32 [152, 152], replicated, may hold values from -0.5 to 0.5
- l2l: float32 [184832], replicated, may hold values from -0.5 to 0.5
Outputs:
- potentials: float32 [8, 131072], P(None, ('pts', 'top'))
The draws below stay inside these ranges and needn't reach their ends.
Inputs may be any that keep to these rules, and one draw needn't show every extreme that they name: `morton_slot`: every slot 0 to 131071 appears once. The points of one device go to at most 16 slots of any one device of the Morton layout (slot // 1024). `slot_leaf`: Non-decreasing. The leaves of the 4096 slots of one owner (slot // 4096) lie in at most 32 consecutive boxes of level 3 (leaf // 8).
All inputs are finite; a program needn't handle non-finite values.
Results may differ from the reference program's by a relative error of at most 0.003.
Values may be sent and summed in bfloat16 or wider, within the bound.
A program may use at most 192 MiB of HBM per device.

```python
import math
import jax
import jax.numpy as jnp
import numpy as np
from jax import lax

PTS_DEV = 1024
LEVEL = 3
EDGE = 6
DENS = 8
OFFSETS = 316
COEF = 152
BOXES4 = 512
LEAVES = 4096
POINTS = 131072
BOX_CAP = 32
N_PTS = 32
N_TOP = 4
DEVICES = 128


def draw_slot_leaf(key, part):
    owners = N_PTS
    mean_boxes = BOXES4 // owners
    key_perm, key_pair, key_flip, key_edge, key_leaf = jax.random.split(key, 5)
    owner_order = jax.random.permutation(key_perm, owners)
    shifts = jax.random.randint(key_pair, (owners // 2,), 0, mean_boxes).astype(jnp.int32)
    shifts = shifts.at[0].set(mean_boxes - 1)
    flip_vals = jax.random.randint(key_flip, (owners // 2,), 0, 2).astype(jnp.int32)
    flip_vals = flip_vals.at[0].set(jnp.where(owner_order[0] == owners - 1, 1, 0))
    upper_own = jnp.where(flip_vals == 0, owner_order[0::2], owner_order[1::2])
    lower_own = jnp.where(flip_vals == 0, owner_order[1::2], owner_order[0::2])
    counts = jnp.zeros((owners,), jnp.int32).at[upper_own].add(mean_boxes + shifts).at[lower_own].add(mean_boxes - shifts)
    box_first = jnp.concatenate([jnp.zeros((1,), jnp.int32), jnp.cumsum(counts)[:-1].astype(jnp.int32)])
    edge_vals = jax.random.randint(key_edge, (owners,), 1, 8).astype(jnp.int32).at[0].set(0)
    leaf_first = 8 * box_first + edge_vals
    leaf_end = jnp.concatenate([leaf_first[1:], jnp.full((1,), LEAVES, jnp.int32)])
    span_len = leaf_end - leaf_first
    per_owner = POINTS // owners
    offsets = jax.random.randint(key_leaf, (owners, per_owner), 0, span_len[:, None]).astype(jnp.int32)
    leaves = jnp.sort(leaf_first[:, None] + offsets, axis=1)
    leaves = leaves.at[:, 0].set(leaf_first).at[:, per_owner - 1].set(leaf_end - 1)
    return leaves.reshape(-1).astype(jnp.int32)


def draw_morton_slot(key, part):
    devices = DEVICES
    mean_send = PTS_DEV // devices
    key_perm, key_pair, key_dest, key_slot, key_body = jax.random.split(key, 5)
    block_order = jax.random.permutation(key_perm, devices)
    shifts = jax.random.randint(key_pair, (devices // 2,), 0, mean_send + 1).astype(jnp.int32)
    shifts = shifts.at[0].set(mean_send)
    size_vals = jnp.zeros((devices,), jnp.int32).at[block_order[0::2]].add(mean_send + shifts).at[block_order[1::2]].add(mean_send - shifts)
    bounds = jnp.cumsum(size_vals).astype(jnp.int32)
    rank_vals = jnp.arange(PTS_DEV, dtype=jnp.int32)
    block_of = jnp.sum((rank_vals[:, None] >= bounds[None, :]).astype(jnp.int32), axis=1)
    dest_shift = jax.random.permutation(key_dest, devices).astype(jnp.int32)
    slot_keys = jax.random.split(key_slot, devices)
    slot_perm = jax.vmap(lambda one_key: jax.random.permutation(one_key, PTS_DEV))(slot_keys).astype(jnp.int32)
    source = (dest_shift[:, None] + block_of[None, :]) % devices
    slot_value = jnp.arange(devices, dtype=jnp.int32)[:, None] * PTS_DEV + slot_perm
    tiebreak = jax.random.permutation(key_body, POINTS).astype(jnp.int32).reshape(devices, PTS_DEV)
    score_vals = (source * POINTS + tiebreak).reshape(-1)
    body_order = jnp.argsort(score_vals, stable=True)
    return slot_value.reshape(-1)[body_order].astype(jnp.int32)


def level_of(stream_key, shape, cuts, smallest, top_value):
    gain, own = 1.0, jax.random.fold_in(stream_key, 6)
    for position, parts in cuts:
        steps = jnp.exp(jax.random.uniform(jax.random.fold_in(own, position), (parts,), jnp.float32, smallest / len(cuts), top_value / len(cuts)))
        gain = gain * jnp.repeat(steps, shape[position] // parts).reshape([-1 if axis == position else 1 for axis in range(len(shape))])
    return gain


def bell_draw(rng, extent, scale, reach, pieces=(), kind=jnp.bfloat16):
    values = scale * jax.random.normal(rng, extent, jnp.float32)
    if pieces:
        values = values * level_of(rng, extent, pieces, -0.22, 0.18)
    return jnp.clip(values, -reach, reach).astype(kind)


def setup_inputs(seed: int = 0) -> dict:
    streams_of = jax.random.split(jax.random.key(seed), 11)
    local_pos = jnp.clip(jax.random.uniform(streams_of[0], (3, POINTS), jnp.float32, -1.0, 1.0) * level_of(streams_of[0], (3, POINTS), ((1, 128),), -0.4, 0.0), -1.0, 1.0)
    densities = bell_draw(streams_of[1], (DENS, POINTS), 1.0, 6.0, ((1, 128),), jnp.float32)
    morton_slot = draw_morton_slot(jax.random.fold_in(streams_of[10], 71), 0)
    slot_leaf = draw_slot_leaf(jax.random.fold_in(streams_of[10], 71), 0)
    uc2e = bell_draw(streams_of[4], (COEF, COEF), COEF ** -0.5, 0.5, (), jnp.float32)
    m2m = bell_draw(streams_of[5], (8 * COEF * COEF,), (8 * COEF) ** -0.5, 0.15625, (), jnp.float32)
    m2l_ops = bell_draw(streams_of[6], (COEF * OFFSETS * COEF,), (OFFSETS * COEF) ** -0.5, 0.02734375)
    dc2e = bell_draw(streams_of[7], (COEF, COEF), COEF ** -0.5, 0.5, (), jnp.float32)
    lattice = bell_draw(streams_of[8], (COEF, COEF), COEF ** -0.5, 0.5, (), jnp.float32)
    l2l = bell_draw(streams_of[9], (8 * COEF * COEF,), COEF ** -0.5, 0.5, (), jnp.float32)
    return dict(local_pos=local_pos, densities=densities, morton_slot=morton_slot, slot_leaf=slot_leaf, uc2e=uc2e, m2m=m2m, m2l_ops=m2l_ops, dc2e=dc2e, lattice=lattice, l2l=l2l)


def surface_table():
    grid_vals = np.linspace(-1.0, 1.0, EDGE)
    points_list = []
    for index_a in range(EDGE):
        for index_b in range(EDGE):
            for index_c in range(EDGE):
                if min(index_a, index_b, index_c) == 0 or max(index_a, index_b, index_c) == EDGE - 1:
                    points_list.append([grid_vals[index_a], grid_vals[index_b], grid_vals[index_c]])
    return np.array(points_list, dtype=np.float32).T

def offset_table():
    points_list = []
    for shift_x in range(-3, 4):
        for shift_y in range(-3, 4):
            for shift_z in range(-3, 4):
                if max(abs(shift_x), abs(shift_y), abs(shift_z)) >= 2:
                    points_list.append([shift_x, shift_y, shift_z])
    return np.array(points_list, dtype=np.int32)

def morton_decode(number, bit_count):
    coord_x = jnp.zeros_like(number)
    coord_y = jnp.zeros_like(number)
    coord_z = jnp.zeros_like(number)
    for level_idx in range(bit_count):
        digit_val = number // 8 ** level_idx % 8
        coord_x = coord_x + digit_val // 4 * 2 ** level_idx
        coord_y = coord_y + digit_val // 2 % 2 * 2 ** level_idx
        coord_z = coord_z + digit_val % 2 * 2 ** level_idx
    return (coord_x, coord_y, coord_z)

def morton_encode(coord_x, coord_y, coord_z, bit_count):
    number = jnp.zeros_like(coord_x)
    for level_idx in range(bit_count):
        digit_val = coord_x // 2 ** level_idx % 2 * 4 + coord_y // 2 ** level_idx % 2 * 2 + coord_z // 2 ** level_idx % 2
        number = number + digit_val * 8 ** level_idx
    return number

def source_boxes(targets):
    side_len = 2 ** LEVEL
    coord_x, coord_y, coord_z = morton_decode(targets, LEVEL)
    shift_table = jnp.asarray(offset_table())
    return morton_encode((coord_x[None, :] + shift_table[:, 0:1]) % side_len, (coord_y[None, :] + shift_table[:, 1:2]) % side_len, (coord_z[None, :] + shift_table[:, 2:3]) % side_len, LEVEL).astype(jnp.int32)

def kernel_tile(local_pos):
    surface = surface_table()
    squared = jnp.zeros((local_pos.shape[1], surface.shape[1]), jnp.float32)
    for dim_index in range(3):
        spacing = 1.25 * jnp.asarray(surface[dim_index])[None, :] - local_pos[dim_index][:, None]
        squared = squared + spacing * spacing
    return 1.0 / (4.0 * math.pi * jnp.sqrt(squared))

def upward(level_mult, m2m):
    current = level_mult
    for level_idx in range(LEVEL):
        parents = current.shape[2] // 8
        current = jnp.einsum('oce,ekpo->ckp', m2m, current.reshape(current.shape[0], current.shape[1], parents, 8), precision=lax.Precision.HIGHEST)
    return current

def downward(root_local, l2l, levels):
    current = root_local
    for level_idx in range(levels):
        current = jnp.einsum('oce,ekp->ckpo', l2l, current, precision=lax.Precision.HIGHEST)
        current = current.reshape(current.shape[0], current.shape[1], -1)
    return current

def reference(local_pos, densities, morton_slot, slot_leaf, uc2e, m2m, m2l_ops, dc2e, lattice, l2l):
    m2m = m2m.reshape(8, COEF, COEF)
    l2l = l2l.reshape(8, COEF, COEF)
    m2l_ops = m2l_ops.reshape(COEF, OFFSETS, COEF)
    own_pts = PTS_DEV * N_TOP
    inverse = jnp.zeros((POINTS,), jnp.int32).at[morton_slot].set(jnp.arange(POINTS, dtype=jnp.int32))
    sorted_pos = local_pos[:, inverse]
    sorted_dens = densities[:, inverse]
    owner_pos = sorted_pos.reshape(3, N_PTS, own_pts).transpose(1, 0, 2)
    owner_dens = sorted_dens.reshape(DENS, N_PTS, own_pts).transpose(1, 0, 2)
    owner_leaf = slot_leaf.reshape(N_PTS, own_pts)

    def owner_partial(packed):
        pos_block, dens_block, leaf_block = packed
        first_box = (leaf_block[0] // 8).astype(jnp.int32)
        kernel = kernel_tile(pos_block)
        contrib = (dens_block.T[:, :, None] * kernel[:, None, :]).reshape(own_pts, DENS * COEF)
        checks = jax.ops.segment_sum(contrib, (leaf_block - 8 * first_box).astype(jnp.int32), num_segments=8 * BOX_CAP)
        checks = checks.reshape(BOX_CAP, 8, DENS, COEF)
        leaf_mult = jnp.einsum('ef,bokf->boke', uc2e, checks, precision=lax.Precision.HIGHEST)
        partial_value = jnp.einsum('oce,boke->ckb', m2m, leaf_mult, precision=lax.Precision.HIGHEST)
        rounded = lax.optimization_barrier(partial_value.astype(jnp.bfloat16)).astype(jnp.float32)
        return (rounded, first_box)
    partials, first_boxes = lax.map(owner_partial, (owner_pos, owner_dens, owner_leaf))
    box_ids = (first_boxes[:, None] + jnp.arange(BOX_CAP, dtype=jnp.int32)[None, :]).astype(jnp.int32)
    spread = partials.transpose(1, 2, 0, 3).reshape(COEF, DENS, N_PTS * BOX_CAP)
    level4 = jnp.zeros((COEF, DENS, BOXES4), jnp.float32).at[:, :, box_ids.reshape(-1)].add(spread, mode='drop')
    level4_low = level4.astype(jnp.bfloat16)
    root_mult = upward(level4, m2m)
    root_local = jnp.einsum('ce,ekp->ckp', lattice, root_mult, precision=lax.Precision.HIGHEST)
    lattice4 = downward(root_local, l2l, LEVEL)
    ops_wide = m2l_ops.astype(jnp.float32)
    low_wide = level4_low.astype(jnp.float32)
    block_len = math.gcd(BOXES4, 32)

    def m2l_block(targets):
        sources = source_boxes(targets)
        return jnp.einsum('cds,skdt->ckt', ops_wide, low_wide[:, :, sources], precision=lax.Precision.HIGHEST)
    target_blocks = jnp.arange(BOXES4, dtype=jnp.int32).reshape(-1, block_len)
    checks4 = lax.map(m2l_block, target_blocks)
    checks4 = checks4.transpose(1, 2, 0, 3).reshape(COEF, DENS, BOXES4)
    locals4 = jnp.einsum('cd,dkt->ckt', dc2e, checks4, precision=lax.Precision.HIGHEST) + lattice4
    leaf_local = jnp.einsum('oce,ekb->ckbo', l2l, locals4, precision=lax.Precision.HIGHEST).reshape(COEF, DENS, LEAVES)

    def owner_potential(packed):
        pos_block, leaf_block = packed
        kernel = kernel_tile(pos_block)
        return jnp.einsum('sc,cks->ks', kernel, leaf_local[:, :, leaf_block], precision=lax.Precision.HIGHEST)
    owner_pot = lax.map(owner_potential, (owner_pos, owner_leaf))
    sorted_pot = owner_pot.transpose(1, 0, 2).reshape(DENS, POINTS)
    return sorted_pot[:, morton_slot]
```

```python
import functools
import math

import jax
import jax.numpy as jnp
import numpy as np
from jax import lax
from jax.experimental import pallas as pl
from jax.experimental.pallas import tpu as pltpu
from jax.sharding import PartitionSpec as P

LEVEL = 3
EDGE = 6
COEF = 152
OFFSETS = 316
PTS = 1024
OWN = 4096
CAP = 64
OWNERS = 32
TOP = 4
DEVS = 128
COLS = DEVS * CAP
BOXES = 512
WIN = 32
GROUPS = 38
CHUNKS = 1501
GPAD = 48
CPAD = 1536
CLASS = 80
BROWS = CLASS * COEF
CHUNK = 512

F32 = jnp.float32
BF16 = jnp.bfloat16
VM = pltpu.MemorySpace.VMEM


def surface_table():
    grid_vals = np.linspace(-1.0, 1.0, EDGE)
    points_list = []
    for a in range(EDGE):
        for b in range(EDGE):
            for c in range(EDGE):
                if min(a, b, c) == 0 or max(a, b, c) == EDGE - 1:
                    points_list.append([grid_vals[a], grid_vals[b], grid_vals[c]])
    return np.array(points_list, dtype=np.float32).T


def surface_columns():
    table = np.zeros((COEF, 8), np.float32)
    table[:, :3] = (np.float32(1.25) * surface_table()).T
    return jnp.asarray(table)


def offset_table():
    points_list = []
    for dx in range(-3, 4):
        for dy in range(-3, 4):
            for dz in range(-3, 4):
                if max(abs(dx), abs(dy), abs(dz)) >= 2:
                    points_list.append([dx, dy, dz])
    return np.array(points_list, dtype=np.int32)


def morton_decode(number):
    x = y = z = jnp.zeros_like(number)
    for bit in range(LEVEL):
        digit = number >> (3 * bit)
        x = x | (((digit >> 2) & 1) << bit)
        y = y | (((digit >> 1) & 1) << bit)
        z = z | ((digit & 1) << bit)
    return x, y, z


def morton_encode(x, y, z):
    number = jnp.zeros_like(x)
    for bit in range(LEVEL):
        digit = (((x >> bit) & 1) << 2) | (((y >> bit) & 1) << 1) | ((z >> bit) & 1)
        number = number | (digit << (3 * bit))
    return number


def split2(x):
    hi = x.astype(BF16)
    lo = (x - hi.astype(F32)).astype(BF16)
    return hi, lo


def split3(x):
    hi = x.astype(BF16)
    rest = x - hi.astype(F32)
    mid = rest.astype(BF16)
    lo = (rest - mid.astype(F32)).astype(BF16)
    return hi, mid, lo


def dot_nn(a, b):
    return lax.dot_general(a, b, (((1,), (0,)), ((), ())), preferred_element_type=F32)


def dot_nt(a, b):
    return lax.dot_general(a, b, (((1,), (1,)), ((), ())), preferred_element_type=F32)


def nt3(x, w):
    xh, xl = split2(x)
    wh, wl = split2(w)
    return dot_nt(xh, wh) + dot_nt(xl, wh) + dot_nt(xh, wl)


def iota(shape, dim):
    return lax.broadcasted_iota(jnp.int32, shape, dim)


def onehot(mask):
    return jnp.where(mask, 1.0, 0.0).astype(BF16)


def pack_kernel(pos_ref, dens_ref, slot_ref, out_ref, where_ref, load_ref):
    slot = slot_ref[...]
    owner = slot >> 12
    code = (slot & (OWN - 1)) + 1
    member = jnp.where(iota((OWNERS, PTS), 0) == owner, 1.0, 0.0)
    before = onehot(iota((PTS, PTS), 0) < iota((PTS, PTS), 1))
    prefix = dot_nn(member.astype(BF16), before)
    rank = jnp.sum(member * prefix, axis=0, keepdims=True)
    position = owner * CAP + rank.astype(jnp.int32)
    where_ref[...] = position
    load_ref[...] = jnp.zeros_like(load_ref)
    pos = pos_ref[...]
    hi = pos.astype(BF16).astype(F32)
    rest = pos - hi
    mid = rest.astype(BF16).astype(F32)
    load_ref[0:3] = hi
    load_ref[8:11] = mid
    load_ref[16:19] = rest - mid
    load_ref[3:4] = (code >> 6).astype(F32)
    load_ref[4:5] = (code & 63).astype(F32)
    dens = dens_ref[...]
    hi = dens.astype(BF16).astype(F32)
    rest = dens - hi
    mid = rest.astype(BF16).astype(F32)
    load_ref[24:32] = hi
    load_ref[32:40] = mid
    load_ref[40:48] = rest - mid
    payload = load_ref[...].astype(BF16)
    for block in range(8):
        pick = onehot(iota((256, PTS), 0) + 256 * block == position)
        res = dot_nt(payload, pick)
        head = res[0:8] + res[8:16] + res[16:24]
        slots = head[3:4] * 64.0 + head[4:5]
        dens_out = res[24:32] + res[32:40] + res[40:48]
        for part in range(4):
            own = 4 * block + part
            lanes = slice(CAP * part, CAP * part + CAP)
            for top in range(TOP):
                out_ref[TOP * own + top, 0:3, :] = head[0:3, lanes]
                out_ref[TOP * own + top, 3:4, :] = slots[:, lanes]
                out_ref[TOP * own + top, 4:6, :] = dens_out[2 * top : 2 * top + 2, lanes]


def green(recv_ref, surf_ref, cols):
    squared = None
    for dim in range(3):
        gap = surf_ref[:, dim : dim + 1] - recv_ref[dim : dim + 1, cols]
        squared = gap * gap if squared is None else squared + gap * gap
    return lax.rsqrt(squared) * (1.0 / (4.0 * math.pi))


def p2m_kernel(recv_ref, leaf_ref, surf_ref, uc2e_ref, m2m_ref, part_ref, code_ref, acc_ref):
    acc_ref[...] = jnp.zeros_like(acc_ref)
    table = leaf_ref[...].astype(BF16)

    def step(index, carry):
        cols = pl.ds(pl.multiple_of(index * CHUNK, CHUNK), CHUNK)
        slot = recv_ref[3:4, cols].astype(jnp.int32) - 1
        high = onehot(iota((64, CHUNK), 0) == (slot >> 6))
        rows = dot_nn(table, high)
        leaf = jnp.sum(
            jnp.where(iota((64, CHUNK), 0) == (slot & 63), rows, 0.0), axis=0, keepdims=True
        ).astype(jnp.int32)
        code = (leaf & 7) * WIN + (leaf >> 3)
        code_ref[:, cols] = code
        pick = onehot(iota((256, CHUNK), 0) == code)
        kernel = green(recv_ref, surf_ref, cols)
        for dens in range(2):
            hi, lo = split2(kernel * recv_ref[4 + dens : 5 + dens, cols])
            total = dot_nt(pick, hi) + dot_nt(pick, lo)
            acc_ref[:, dens] += total.reshape(8, WIN, COEF)
        return carry

    lax.fori_loop(0, COLS // CHUNK, step, 0)
    leaf_mult = nt3(acc_ref[...].reshape(2 * 256, COEF), uc2e_ref[...])
    part = nt3(leaf_mult[0:64], m2m_ref[0])
    for octant in range(1, 8):
        part = part + nt3(leaf_mult[64 * octant : 64 * octant + 64], m2m_ref[octant])
    part_ref[...] = part.astype(BF16)


def relayout_kernel(flat_ref, out_ref, stage_ref, wide_ref, sem):
    rows = 2048
    total = GROUPS * CHUNKS
    blocks = total // rows
    tail = total - blocks * rows

    def fetch(index, slot):
        return pltpu.make_async_copy(
            flat_ref.at[pl.ds(index * rows, rows)], stage_ref.at[slot], sem.at[slot]
        )

    @pl.when(pl.program_id(0) == 0)
    def _():
        fetch(0, 0).start()

        def body(index, carry):
            slot = index % 2

            @pl.when(index + 1 < blocks)
            def _():
                fetch(index + 1, 1 - slot).start()

            fetch(index, slot).wait()
            wide_ref[pl.ds(pl.multiple_of(index * rows, rows), rows)] = stage_ref[slot].astype(F32)
            return carry

        lax.fori_loop(0, blocks, body, 0)
        last = pltpu.make_async_copy(
            flat_ref.at[pl.ds(blocks * rows, tail)], stage_ref.at[0, pl.ds(0, tail)], sem.at[0]
        )
        last.start()
        last.wait()
        wide_ref[pl.ds(blocks * rows, tail)] = stage_ref[0, 0:tail].astype(F32)

    base = pl.program_id(0) * 64

    def move(index, carry):
        for part in range(8):
            chunk = base + index * 8 + part
            source = jnp.minimum(chunk, CHUNKS - 1)
            value = wide_ref[pl.ds(source, GROUPS, stride=CHUNKS), :]
            value = jnp.where(chunk < CHUNKS, value, 0.0)
            lanes = pl.ds(pl.multiple_of((index * 8 + part) * 128, 128), 128)
            out_ref[0:GROUPS, lanes] = value.astype(BF16)
        return carry

    lax.fori_loop(0, 8, move, 0)


def far_kernel(
    fb_ref,
    parts_ref,
    tbox_ref,
    nbr_ref,
    wide_hbm,
    m2m_ref,
    l2l_ref,
    lattice_ref,
    dc2e_ref,
    hi_ref,
    lo_ref,
    wide_ref,
    src_ref,
    acc_ref,
    check_ref,
    sem,
):
    bring = pltpu.make_async_copy(wide_hbm, wide_ref, sem)
    bring.start()
    row = iota((BOXES, 1), 0)
    box = ((row & 7) << 6) + (row & 56) + (row >> 6)
    place = onehot(box == tbox_ref[...])
    eye = onehot(iota((COEF, COEF), 0) == iota((COEF, COEF), 1))
    level = []
    low = []
    for dens in range(2):
        parts = parts_ref[:, dens].reshape(OWNERS * WIN, COEF)
        value = dot_nn(place, parts)
        level.append(value)
        low.append(dot_nt(eye, value.astype(BF16)).astype(BF16))
    src_ref[0:128] = jnp.zeros((128, 256), BF16)
    src_ref[128 + BROWS : 384 + BROWS] = jnp.zeros((256, 256), BF16)

    def build(pair, carry):
        pick = onehot(box == nbr_ref[pair])
        first = dot_nn(low[0], pick)
        second = dot_nn(low[1], pick)
        top = jnp.concatenate([first[:, 0:128], second[:, 0:128]], axis=1)
        bottom = jnp.concatenate([first[:, 128:256], second[:, 128:256]], axis=1)
        both = jnp.concatenate([top, bottom], axis=0).astype(BF16)
        src_ref[pl.ds(pl.multiple_of(128 + pair * 304, 16), 304)] = both
        return carry

    lax.fori_loop(0, CLASS // 2, build, 0)

    up = None
    for o in range(8):
        rows = jnp.concatenate(
            [level[0][64 * o : 64 * o + 64], level[1][64 * o : 64 * o + 64]], axis=0
        )
        term = nt3(rows, m2m_ref[o])
        up = term if up is None else up + term
    up2 = None
    for o in range(8):
        rows = jnp.concatenate([up[8 * o : 8 * o + 8], up[64 + 8 * o : 72 + 8 * o]], axis=0)
        term = nt3(rows, m2m_ref[o])
        up2 = term if up2 is None else up2 + term
    row16 = iota((16, 1), 0)
    up3 = None
    for o in range(8):
        term = nt3(jnp.where((row16 & 7) == o, up2, 0.0), m2m_ref[o])
        up3 = term if up3 is None else up3 + term
    root0 = jnp.sum(up3[0:8], axis=0, keepdims=True)
    root1 = jnp.sum(up3[8:16], axis=0, keepdims=True)
    root = jnp.where(row16 < 8, root0, root1)
    down = nt3(root, lattice_ref[...])
    down1 = None
    for o in range(8):
        term = nt3(jnp.where((row16 & 7) == o, down, 0.0), l2l_ref[o])
        down1 = term if down1 is None else down1 + term
    down2 = jnp.concatenate([nt3(down1, l2l_ref[o]) for o in range(8)], axis=0)
    row64 = iota((64, 1), 0)
    target = (fb_ref[0] + (row64 & 31)) & (BOXES - 1)
    parent = ((target >> 3) & 7) * 16 + (row64 >> 5) * 8 + (target >> 6)
    choose = onehot(iota((64, 128), 1) == parent)
    hi, mid, rest = split3(down2)
    parents = dot_nn(choose, hi) + dot_nn(choose, mid) + dot_nn(choose, rest)
    far = None
    for o in range(8):
        term = nt3(jnp.where((target & 7) == o, parents, 0.0), l2l_ref[o])
        far = term if far is None else far + term

    bring.wait()
    acc_ref[...] = jnp.zeros_like(acc_ref)
    width = 1024

    def mult(index, carry):
        for r in range(4):
            lhs = []
            for m in range(4):
                lane = pl.multiple_of(128 * (375 * r + 95 * m) + index * width, 128)
                lhs.append(wide_ref[:, pl.ds(lane, width)])
            start = pl.multiple_of(128 - 32 * r + index * width, 32)
            acc_ref[r] += dot_nn(jnp.concatenate(lhs, axis=0), src_ref[pl.ds(start, width)])
        return carry

    lax.fori_loop(0, 12, mult, 0)
    block = (iota((1, 256), 1) >> 5) & 3
    for r in range(4):
        value = None
        for m in range(4):
            term = jnp.where(block == m, acc_ref[r, GPAD * m : GPAD * m + GROUPS], 0.0)
            value = term if value is None else value + term
        for half in range(2):
            lanes = slice(128 * half, 128 * half + 128)
            check_ref[half, pl.ds(r, GROUPS, stride=4), :] = value[:, lanes]
    lane = iota((64, 256), 1)
    fold = onehot(((lane & 31) == (row64 & 31)) & ((lane >> 7) == (row64 >> 5)))
    hi, mid, rest = split3(jnp.concatenate([check_ref[0], check_ref[1]], axis=1))
    checks = dot_nt(fold, hi) + dot_nt(fold, mid) + dot_nt(fold, rest)
    local = nt3(checks, dc2e_ref[...]) + far
    leaves = [nt3(local, l2l_ref[o]) for o in range(8)]
    for dens in range(2):
        value = jnp.concatenate([leaf[WIN * dens : WIN * dens + WIN] for leaf in leaves], axis=0)
        hi, lo = split2(value)
        hi_ref[dens] = dot_nt(eye, hi).astype(BF16)
        lo_ref[dens] = dot_nt(eye, lo).astype(BF16)


def l2p_kernel(recv_ref, code_ref, surf_ref, hi_ref, lo_ref, out_ref):
    def step(index, carry):
        cols = pl.ds(pl.multiple_of(index * CHUNK, CHUNK), CHUNK)
        pick = onehot(iota((256, CHUNK), 0) == code_ref[:, cols])
        kernel = green(recv_ref, surf_ref, cols)
        for dens in range(2):
            value = dot_nn(hi_ref[dens], pick) + dot_nn(lo_ref[dens], pick)
            out_ref[dens : dens + 1, cols] = jnp.sum(kernel * value, axis=0, keepdims=True)
        return carry

    lax.fori_loop(0, COLS // CHUNK, step, 0)


def unpack_kernel(back_ref, where_ref, out_ref):
    pieces = split3(back_ref[...])
    position = where_ref[...]
    total = jnp.zeros((8, PTS), F32)
    for block in range(8):
        pick = onehot(iota((256, PTS), 0) + 256 * block == position)
        cols = slice(256 * block, 256 * block + 256)
        for piece in pieces:
            total = total + dot_nn(piece[:, cols], pick)
    out_ref[...] = total


def whole(count):
    return [pl.BlockSpec(memory_space=VM)] * count


def limits(mib):
    return pltpu.CompilerParams(vmem_limit_bytes=mib * 1024 * 1024)


def per_device(
    local_pos, densities, morton_slot, slot_leaf, uc2e, m2m, m2l_ops, dc2e, lattice, l2l
):
    m2m = m2m.reshape(8, COEF, COEF)
    l2l = l2l.reshape(8, COEF, COEF)
    surf = surface_columns()
    leaves = lax.all_gather(slot_leaf, "top", axis=0, tiled=True)
    starts = lax.all_gather(slot_leaf[:1], ("pts", "top"), axis=0, tiled=True)
    first_box = leaves[0] // 8
    leaf_table = (leaves - 8 * first_box).reshape(64, 64).T.astype(F32)
    first_all = starts.reshape(OWNERS, TOP)[:, 0] // 8
    slide = jnp.arange(WIN, dtype=jnp.int32)
    tbox = (first_all[:, None] + slide[None, :]).reshape(1, OWNERS * WIN)
    targets = (first_box + slide) & (BOXES - 1)
    tx, ty, tz = morton_decode(targets)
    offsets = np.zeros((4 * CLASS, 3), np.int32)
    offsets[:OFFSETS] = offset_table()
    offsets = jnp.asarray(offsets.reshape(4, CLASS, 3).transpose(1, 0, 2))
    known = jnp.asarray((np.arange(4 * CLASS) < OFFSETS).reshape(4, CLASS).T)
    nbr = morton_encode(
        (tx + offsets[:, :, 0:1]) & 7, (ty + offsets[:, :, 1:2]) & 7, (tz + offsets[:, :, 2:3]) & 7
    )
    nbr = jnp.where(known[:, :, None], nbr, -1).reshape(CLASS // 2, 1, 256)

    flat = m2l_ops.reshape(GROUPS * CHUNKS, 128)
    wide = pl.pallas_call(
        relayout_kernel,
        grid=(CPAD // 64,),
        out_shape=jax.ShapeDtypeStruct((GPAD, CPAD * 128), BF16),
        in_specs=[pl.BlockSpec(memory_space=pl.ANY)],
        out_specs=pl.BlockSpec((GPAD, 64 * 128), lambda i: (0, i)),
        scratch_shapes=[
            pltpu.VMEM((2, 2048, 128), BF16),
            pltpu.VMEM((GROUPS * CHUNKS, 128), F32),
            pltpu.SemaphoreType.DMA((2,)),
        ],
        compiler_params=limits(60),
        name="relayout",
    )(flat)

    send, position = pl.pallas_call(
        pack_kernel,
        out_shape=(
            jax.ShapeDtypeStruct((DEVS, 6, CAP), F32),
            jax.ShapeDtypeStruct((1, PTS), jnp.int32),
        ),
        in_specs=whole(3),
        out_specs=tuple(whole(2)),
        scratch_shapes=[pltpu.VMEM((48, PTS), F32)],
        compiler_params=limits(32),
        name="pack",
    )(local_pos, densities, morton_slot.reshape(1, PTS))

    recv = lax.all_to_all(send, ("pts", "top"), split_axis=0, concat_axis=0, tiled=True)
    recv = recv.transpose(1, 0, 2).reshape(6, COLS)

    part, code = pl.pallas_call(
        p2m_kernel,
        out_shape=(
            jax.ShapeDtypeStruct((2 * WIN, COEF), BF16),
            jax.ShapeDtypeStruct((1, COLS), jnp.int32),
        ),
        in_specs=whole(5),
        out_specs=tuple(whole(2)),
        scratch_shapes=[pltpu.VMEM((8, 2, WIN, COEF), F32)],
        compiler_params=limits(32),
        name="p2m",
    )(recv, leaf_table, surf, uc2e, m2m)

    parts = lax.all_gather(part, "pts", axis=0, tiled=False).reshape(OWNERS, 2, WIN, COEF)

    hi, lo = pl.pallas_call(
        far_kernel,
        out_shape=(
            jax.ShapeDtypeStruct((2, COEF, 256), BF16),
            jax.ShapeDtypeStruct((2, COEF, 256), BF16),
        ),
        in_specs=[pl.BlockSpec(memory_space=pltpu.MemorySpace.SMEM)]
        + whole(3)
        + [pl.BlockSpec(memory_space=pl.ANY)]
        + whole(4),
        out_specs=tuple(whole(2)),
        scratch_shapes=[
            pltpu.VMEM((GPAD, CPAD * 128), BF16),
            pltpu.VMEM((BROWS + 384, 256), BF16),
            pltpu.VMEM((4, 4 * GPAD, 256), F32),
            pltpu.VMEM((2, COEF, 128), F32),
            pltpu.SemaphoreType.DMA,
        ],
        compiler_params=limits(60),
        name="far",
    )(first_box.reshape(1), parts, tbox, nbr, wide, m2m, l2l, lattice, dc2e)

    pot = pl.pallas_call(
        l2p_kernel,
        out_shape=jax.ShapeDtypeStruct((2, COLS), F32),
        in_specs=whole(5),
        out_specs=whole(1)[0],
        compiler_params=limits(32),
        name="l2p",
    )(recv, code, surf, hi, lo)

    reply = pot.reshape(2, DEVS, CAP).transpose(1, 0, 2)
    back = lax.all_to_all(reply, ("pts", "top"), split_axis=0, concat_axis=0, tiled=True)
    back = back.reshape(OWNERS, TOP, 2, CAP).transpose(1, 2, 0, 3).reshape(8, OWNERS * CAP)
    return pl.pallas_call(
        unpack_kernel,
        out_shape=jax.ShapeDtypeStruct((8, PTS), F32),
        in_specs=whole(2),
        out_specs=whole(1)[0],
        compiler_params=limits(32),
        name="unpack",
    )(back, position)


def solution(mesh):
    placed = (
        P(None, ("pts", "top")),
        P(None, ("pts", "top")),
        P(("pts", "top")),
        P(("pts", "top")),
        P(),
        P(),
        P(),
        P(),
        P(),
        P(),
    )
    return jax.shard_map(
        per_device, mesh=mesh, in_specs=placed, out_specs=P(None, ("pts", "top")), check_vma=False
    )
```

```python
import functools
import math

import jax
import jax.numpy as jnp
import numpy as np
from jax import lax
from jax.experimental import pallas as pl
from jax.experimental.pallas import tpu as pltpu
from jax.sharding import PartitionSpec as P

LEVEL = 3
EDGE = 6
COEF = 152
OFFSETS = 316
PTS = 1024
OWN = 4096
CAP = 64
OWNERS = 32
TOP = 4
DEVS = 128
COLS = DEVS * CAP
BOXES = 512
WIN = 32
GROUPS = 38
CHUNKS = 1501
GPAD = 40
WIDE = 60048
PIECE = 1440
PIECES = 40
DEPTH = 8
TAIL = COEF - 128
CLASS = 80
BROWS = CLASS * COEF
CHUNK = 512

F32 = jnp.float32
BF16 = jnp.bfloat16
VM = pltpu.MemorySpace.VMEM
MESH = pl.DeviceIdType.MESH


def surface_table():
    grid_vals = np.linspace(-1.0, 1.0, EDGE)
    points_list = []
    for a in range(EDGE):
        for b in range(EDGE):
            for c in range(EDGE):
                if min(a, b, c) == 0 or max(a, b, c) == EDGE - 1:
                    points_list.append([grid_vals[a], grid_vals[b], grid_vals[c]])
    return np.array(points_list, dtype=np.float32).T


def surface_columns():
    table = np.zeros((COEF, 8), np.float32)
    table[:, :3] = (np.float32(1.25) * surface_table()).T
    return jnp.asarray(table)


def offset_table():
    points_list = []
    for dx in range(-3, 4):
        for dy in range(-3, 4):
            for dz in range(-3, 4):
                if max(abs(dx), abs(dy), abs(dz)) >= 2:
                    points_list.append([dx, dy, dz])
    return np.array(points_list, dtype=np.int32)


def morton_decode(number):
    x = y = z = jnp.zeros_like(number)
    for bit in range(LEVEL):
        digit = number >> (3 * bit)
        x = x | (((digit >> 2) & 1) << bit)
        y = y | (((digit >> 1) & 1) << bit)
        z = z | ((digit & 1) << bit)
    return x, y, z


def morton_encode(x, y, z):
    number = jnp.zeros_like(x)
    for bit in range(LEVEL):
        digit = (((x >> bit) & 1) << 2) | (((y >> bit) & 1) << 1) | ((z >> bit) & 1)
        number = number | (digit << (3 * bit))
    return number


def split2(x):
    hi = x.astype(BF16)
    lo = (x - hi.astype(F32)).astype(BF16)
    return hi, lo


def split3(x):
    hi = x.astype(BF16)
    rest = x - hi.astype(F32)
    mid = rest.astype(BF16)
    lo = (rest - mid.astype(F32)).astype(BF16)
    return hi, mid, lo


def dot_nn(a, b):
    return lax.dot_general(a, b, (((1,), (0,)), ((), ())), preferred_element_type=F32)


def dot_nt(a, b):
    return lax.dot_general(a, b, (((1,), (1,)), ((), ())), preferred_element_type=F32)


def nt3(x, w):
    rows = x.shape[0]
    xh, xl = split2(x)
    wh, wl = split2(w)
    both = dot_nt(jnp.concatenate([xh, xl], axis=0), wh)
    return both[:rows] + both[rows:] + dot_nt(xh, wl)


def iota(shape, dim):
    return lax.broadcasted_iota(jnp.int32, shape, dim)


def onehot(mask):
    return jnp.where(mask, 1.0, 0.0).astype(BF16)


def pack_kernel(pos_ref, dens_ref, slot_ref, out_ref, where_ref, load_ref):
    slot = slot_ref[...]
    owner = slot >> 12
    code = (slot & (OWN - 1)) + 1
    member = jnp.where(iota((OWNERS, PTS), 0) == owner, 1.0, 0.0)
    before = onehot(iota((PTS, PTS), 0) < iota((PTS, PTS), 1))
    prefix = dot_nn(member.astype(BF16), before)
    rank = jnp.sum(member * prefix, axis=0, keepdims=True)
    position = owner * CAP + rank.astype(jnp.int32)
    where_ref[...] = position
    load_ref[...] = jnp.zeros_like(load_ref)
    pos = pos_ref[...]
    hi = pos.astype(BF16).astype(F32)
    rest = pos - hi
    mid = rest.astype(BF16).astype(F32)
    load_ref[0:3] = hi
    load_ref[8:11] = mid
    load_ref[16:19] = rest - mid
    load_ref[3:4] = (code >> 6).astype(F32)
    load_ref[4:5] = (code & 63).astype(F32)
    dens = dens_ref[...]
    hi = dens.astype(BF16).astype(F32)
    rest = dens - hi
    mid = rest.astype(BF16).astype(F32)
    load_ref[24:32] = hi
    load_ref[32:40] = mid
    load_ref[40:48] = rest - mid
    payload = load_ref[...].astype(BF16)
    for block in range(8):
        pick = onehot(iota((256, PTS), 0) + 256 * block == position)
        res = dot_nt(payload, pick)
        head = res[0:8] + res[8:16] + res[16:24]
        slots = head[3:4] * 64.0 + head[4:5]
        dens_out = res[24:32] + res[32:40] + res[40:48]
        for part in range(4):
            own = 4 * block + part
            lanes = slice(CAP * part, CAP * part + CAP)
            for top in range(TOP):
                out_ref[TOP * own + top, 0:3, :] = head[0:3, lanes]
                out_ref[TOP * own + top, 3:4, :] = slots[:, lanes]
                out_ref[TOP * own + top, 4:6, :] = dens_out[2 * top : 2 * top + 2, lanes]


def green(recv_ref, surf_ref, cols):
    squared = None
    for dim in range(3):
        gap = surf_ref[:, dim : dim + 1] - recv_ref[dim : dim + 1, cols]
        squared = gap * gap if squared is None else squared + gap * gap
    return lax.rsqrt(squared) * (1.0 / (4.0 * math.pi))


def p2m_kernel(
    fb_ref,
    recv_ref,
    leaf_ref,
    surf_ref,
    uc2e_ref,
    m2m_ref,
    gath_ref,
    code_ref,
    acc_ref,
    pad_ref,
    send_sem,
    recv_sem,
    pass_sem,
    take_sem,
):
    me = lax.axis_index("pts")
    x, y, core = me // 8, (me // 2) % 4, me % 2
    partner = me + 1 - 2 * core

    def other(step, sign, side):
        return ((x + sign * (step // 4) + 4) % 4) * 8 + ((y + sign * (step % 4) + 4) % 4) * 2 + side

    barrier = pltpu.get_barrier_semaphore()
    for step in range(1, 16):
        pl.semaphore_signal(
            barrier, inc=1, device_id={"pts": other(step, 1, core)}, device_id_type=MESH
        )
    pl.semaphore_signal(barrier, inc=1, device_id={"pts": partner}, device_id_type=MESH)

    acc_ref[...] = jnp.zeros_like(acc_ref)
    pad_ref[...] = jnp.zeros_like(pad_ref)
    table = leaf_ref[...].astype(BF16)

    def step(index, carry):
        cols = pl.ds(pl.multiple_of(index * CHUNK, CHUNK), CHUNK)
        slot = recv_ref[3:4, cols].astype(jnp.int32) - 1
        high = onehot(iota((64, CHUNK), 0) == (slot >> 6))
        rows = dot_nn(table, high)
        leaf = jnp.sum(
            jnp.where(iota((64, CHUNK), 0) == (slot & 63), rows, 0.0), axis=0, keepdims=True
        ).astype(jnp.int32)
        code = (leaf & 7) * WIN + (leaf >> 3)
        code_ref[:, cols] = code
        pick = onehot(iota((256, CHUNK), 0) == code)
        kernel = green(recv_ref, surf_ref, cols)
        for dens in range(2):
            hi, lo = split2(kernel * recv_ref[4 + dens : 5 + dens, cols])
            total = dot_nt(pick, hi) + dot_nt(pick, lo)
            acc_ref[:, dens] += total.reshape(8, WIN, COEF)
        return carry

    lax.fori_loop(0, COLS // CHUNK, step, 0)
    leaf_mult = nt3(acc_ref[...].reshape(2 * 256, COEF), uc2e_ref[...])
    part = nt3(leaf_mult[0:64], m2m_ref[0])
    for octant in range(1, 8):
        part = part + nt3(leaf_mult[64 * octant : 64 * octant + 64], m2m_ref[octant])
    pad_ref[:, 0:COEF] = part
    first = fb_ref[0]
    lane = iota((16, 128), 1)
    tail = jnp.where(
        lane == 96,
        (first >> 3).astype(F32),
        jnp.where(lane == 97, (first & 7).astype(F32), 0.0),
    )
    for group in range(4):
        piece = pad_ref[16 * group : 16 * group + 16, 128:256]
        tail = tail + (pltpu.roll(piece, TAIL * group, 1) if group else piece)
    gath_ref[me, 0:64] = pad_ref[:, 0:128].astype(BF16)
    gath_ref[me, 64:80] = tail.astype(BF16)

    pl.semaphore_wait(barrier, 16)

    def copy(slot, sems, index, target):
        return pltpu.make_async_remote_copy(
            src_ref=gath_ref.at[slot],
            dst_ref=gath_ref.at[slot],
            send_sem=sems[0].at[index],
            recv_sem=sems[1].at[index],
            device_id={"pts": target},
            device_id_type=MESH,
        )

    far = (send_sem, recv_sem)
    near = (pass_sem, take_sem)
    copy(me, near, 0, partner).start()
    for step in range(1, 16):
        copy(me, far, step, other(step, 1, core)).start()
    for step in range(1, 16):
        slot = other(step, -1, core)
        copy(slot, far, step, partner).wait_recv()
        copy(slot, near, step, partner).start()
    copy(partner, near, 0, partner).wait_recv()
    for step in range(1, 16):
        copy(other(step, -1, 1 - core), near, step, partner).wait_recv()
    copy(me, near, 0, partner).wait_send()
    for step in range(1, 16):
        copy(me, far, step, partner).wait_send()
        copy(other(step, -1, core), near, step, partner).wait_send()


def far_kernel(
    fb_ref,
    parts_ref,
    nbr_ref,
    flat_hbm,
    m2m_ref,
    l2l_ref,
    lattice_ref,
    dc2e_ref,
    hi_ref,
    lo_ref,
    stage_ref,
    wide_ref,
    src_ref,
    acc_ref,
    check_ref,
    sem,
):
    def fetch(index, size):
        return pltpu.make_async_copy(
            flat_hbm.at[pl.ds(index * PIECE, size)],
            stage_ref.at[index % DEPTH, pl.ds(0, size)],
            sem.at[index % DEPTH],
        )

    last = GROUPS * CHUNKS - (PIECES - 1) * PIECE
    for index in range(DEPTH):
        fetch(index, PIECE).start()
    row = iota((BOXES, 1), 0)
    box = ((row & 7) << 6) + (row & 56) + (row >> 6)
    eye = onehot(iota((COEF, COEF), 0) == iota((COEF, COEF), 1))
    codes = parts_ref[:, 64, :].astype(F32)
    lane = iota((OWNERS, 128), 1)
    first = jnp.sum(
        jnp.where(lane == 96, 8.0 * codes, jnp.where(lane == 97, codes, 0.0)),
        axis=1,
        keepdims=True,
    )
    spread = jnp.where(iota((OWNERS, 512), 0) == (iota((OWNERS, 512), 1) >> 4), first, 0.0)
    start = jnp.sum(spread, axis=0, keepdims=True).astype(jnp.int32)
    start = start + (iota((1, 512), 1) & 15)
    halves = []
    for half in range(2):
        place = onehot(box == start + 16 * half)
        pieces = [
            parts_ref[:, 32 * dens + 16 * half : 32 * dens + 16 * half + 16, :].reshape(512, 128)
            for dens in range(2)
        ]
        pieces.append(parts_ref[:, 64:80, :].reshape(512, 128))
        halves.append(dot_nn(place, jnp.concatenate(pieces, axis=1)))
    level = []
    for dens in range(2):
        main = slice(128 * dens, 128 * dens + 128)
        tail = 256 + 2 * TAIL * dens
        value = jnp.concatenate(
            [
                halves[0][:, main] + halves[1][:, main],
                halves[0][:, tail : tail + TAIL] + halves[1][:, tail + TAIL : tail + 2 * TAIL],
            ],
            axis=1,
        )
        level.append(value)
    low = jnp.concatenate([dot_nt(eye, value.astype(BF16)) for value in level], axis=0)
    low = low.astype(BF16)
    src_ref[0:128] = jnp.zeros((128, 256), BF16)
    src_ref[128 + BROWS : 384 + BROWS] = jnp.zeros((256, 256), BF16)
    wide_ref[PIECES * PIECE : WIDE] = jnp.zeros((WIDE - PIECES * PIECE, 128), F32)

    def build(pair, carry):
        pick = onehot(box == nbr_ref[pair])
        found = dot_nn(low, pick)
        top = jnp.concatenate([found[0:COEF, 0:128], found[COEF:, 0:128]], axis=1)
        bottom = jnp.concatenate([found[0:COEF, 128:256], found[COEF:, 128:256]], axis=1)
        both = jnp.concatenate([top, bottom], axis=0).astype(BF16)
        src_ref[pl.ds(pl.multiple_of(128 + pair * 304, 16), 304)] = both

        @pl.when(pair < PIECES - 1)
        def _():
            fetch(pair, PIECE).wait()

        @pl.when(pair == PIECES - 1)
        def _():
            fetch(pair, last).wait()

        wide_ref[pl.ds(pl.multiple_of(pair * PIECE, 32), PIECE)] = stage_ref[pair % DEPTH].astype(
            F32
        )

        @pl.when(pair + DEPTH < PIECES - 1)
        def _():
            fetch(pair + DEPTH, PIECE).start()

        @pl.when(pair + DEPTH == PIECES - 1)
        def _():
            fetch(pair + DEPTH, last).start()

        return carry

    lax.fori_loop(0, PIECES, build, 0)

    up = None
    for o in range(8):
        rows = jnp.concatenate(
            [level[0][64 * o : 64 * o + 64], level[1][64 * o : 64 * o + 64]], axis=0
        )
        term = nt3(rows, m2m_ref[o])
        up = term if up is None else up + term
    up2 = None
    for o in range(8):
        rows = jnp.concatenate([up[8 * o : 8 * o + 8], up[64 + 8 * o : 72 + 8 * o]], axis=0)
        term = nt3(rows, m2m_ref[o])
        up2 = term if up2 is None else up2 + term
    row16 = iota((16, 1), 0)
    up3 = None
    for o in range(8):
        term = nt3(jnp.where((row16 & 7) == o, up2, 0.0), m2m_ref[o])
        up3 = term if up3 is None else up3 + term
    root0 = jnp.sum(up3[0:8], axis=0, keepdims=True)
    root1 = jnp.sum(up3[8:16], axis=0, keepdims=True)
    root = jnp.where(row16 < 8, root0, root1)
    down = nt3(root, lattice_ref[...])
    down1 = None
    for o in range(8):
        term = nt3(jnp.where((row16 & 7) == o, down, 0.0), l2l_ref[o])
        down1 = term if down1 is None else down1 + term
    down2 = jnp.concatenate([nt3(down1, l2l_ref[o]) for o in range(8)], axis=0)
    row64 = iota((64, 1), 0)
    target = (fb_ref[0] + (row64 & 31)) & (BOXES - 1)
    parent = ((target >> 3) & 7) * 16 + (row64 >> 5) * 8 + (target >> 6)
    choose = onehot(iota((64, 128), 1) == parent)
    hi, mid, rest = split3(down2)
    parents = dot_nn(choose, hi) + dot_nn(choose, mid) + dot_nn(choose, rest)
    far = None
    for o in range(8):
        term = nt3(jnp.where((target & 7) == o, parents, 0.0), l2l_ref[o])
        far = term if far is None else far + term

    acc_ref[...] = jnp.zeros_like(acc_ref)

    def mult(index, carry):
        for r in range(4):
            lhs = []
            for m in range(4):
                chunk = 375 * r + 95 * m + index * 8
                lhs.append(
                    jnp.concatenate(
                        [wide_ref[pl.ds(chunk + q, GPAD, stride=CHUNKS), :] for q in range(8)],
                        axis=1,
                    )
                )
            begin = pl.multiple_of(128 - 32 * r + index * 1024, 32)
            acc_ref[r] += dot_nn(
                jnp.concatenate(lhs, axis=0).astype(BF16), src_ref[pl.ds(begin, 1024)]
            )
        return carry

    lax.fori_loop(0, 12, mult, 0)
    block = (iota((1, 256), 1) >> 5) & 3
    for r in range(4):
        value = None
        for m in range(4):
            term = jnp.where(block == m, acc_ref[r, GPAD * m : GPAD * m + GROUPS], 0.0)
            value = term if value is None else value + term
        for half in range(2):
            lanes = slice(128 * half, 128 * half + 128)
            check_ref[half, pl.ds(r, GROUPS, stride=4), :] = value[:, lanes]
    lane = iota((64, 256), 1)
    fold = onehot(((lane & 31) == (row64 & 31)) & ((lane >> 7) == (row64 >> 5)))
    hi, mid, rest = split3(jnp.concatenate([check_ref[0], check_ref[1]], axis=1))
    checks = dot_nt(fold, hi) + dot_nt(fold, mid) + dot_nt(fold, rest)
    local = nt3(checks, dc2e_ref[...]) + far
    leaves = [nt3(local, l2l_ref[o]) for o in range(8)]
    for dens in range(2):
        value = jnp.concatenate([leaf[WIN * dens : WIN * dens + WIN] for leaf in leaves], axis=0)
        hi, lo = split2(value)
        hi_ref[dens] = dot_nt(eye, hi).astype(BF16)
        lo_ref[dens] = dot_nt(eye, lo).astype(BF16)


def l2p_kernel(recv_ref, code_ref, surf_ref, hi_ref, lo_ref, out_ref):
    def step(index, carry):
        cols = pl.ds(pl.multiple_of(index * CHUNK, CHUNK), CHUNK)
        pick = onehot(iota((256, CHUNK), 0) == code_ref[:, cols])
        kernel = green(recv_ref, surf_ref, cols)
        for dens in range(2):
            value = dot_nn(hi_ref[dens], pick) + dot_nn(lo_ref[dens], pick)
            out_ref[dens : dens + 1, cols] = jnp.sum(kernel * value, axis=0, keepdims=True)
        return carry

    lax.fori_loop(0, COLS // CHUNK, step, 0)


def unpack_kernel(back_ref, where_ref, out_ref):
    pieces = split3(back_ref[...])
    position = where_ref[...]
    total = jnp.zeros((8, PTS), F32)
    for block in range(8):
        pick = onehot(iota((256, PTS), 0) + 256 * block == position)
        cols = slice(256 * block, 256 * block + 256)
        for piece in pieces:
            total = total + dot_nn(piece[:, cols], pick)
    out_ref[...] = total


def whole(count):
    return [pl.BlockSpec(memory_space=VM)] * count


def limits(mib):
    return pltpu.CompilerParams(vmem_limit_bytes=mib * 1024 * 1024)


def per_device(
    local_pos, densities, morton_slot, slot_leaf, uc2e, m2m, m2l_ops, dc2e, lattice, l2l
):
    m2m = m2m.reshape(8, COEF, COEF)
    l2l = l2l.reshape(8, COEF, COEF)
    surf = surface_columns()
    leaves = lax.all_gather(slot_leaf, "top", axis=0, tiled=True)
    first_box = leaves[0] >> 3
    leaf_table = (leaves - 8 * first_box).reshape(64, 64).T.astype(F32)
    slide = jnp.arange(WIN, dtype=jnp.int32)
    targets = (first_box + slide) & (BOXES - 1)
    tx, ty, tz = morton_decode(targets)
    offsets = np.zeros((4 * CLASS, 3), np.int32)
    offsets[:OFFSETS] = offset_table()
    offsets = jnp.asarray(offsets.reshape(4, CLASS, 3).transpose(1, 0, 2))
    known = jnp.asarray((np.arange(4 * CLASS) < OFFSETS).reshape(4, CLASS).T)
    nbr = morton_encode(
        (tx + offsets[:, :, 0:1]) & 7, (ty + offsets[:, :, 1:2]) & 7, (tz + offsets[:, :, 2:3]) & 7
    )
    nbr = jnp.where(known[:, :, None], nbr, -1).reshape(CLASS // 2, 1, 256)

    flat = m2l_ops.reshape(GROUPS * CHUNKS, 128)
    send, position = pl.pallas_call(
        pack_kernel,
        out_shape=(
            jax.ShapeDtypeStruct((DEVS, 6, CAP), F32),
            jax.ShapeDtypeStruct((1, PTS), jnp.int32),
        ),
        in_specs=whole(3),
        out_specs=tuple(whole(2)),
        scratch_shapes=[pltpu.VMEM((48, PTS), F32)],
        compiler_params=limits(32),
        name="pack",
    )(local_pos, densities, morton_slot.reshape(1, PTS))

    recv = lax.all_to_all(send, ("pts", "top"), split_axis=0, concat_axis=0, tiled=True)
    recv = recv.transpose(1, 0, 2).reshape(6, COLS)

    fb = first_box.reshape(1)
    smem = [pl.BlockSpec(memory_space=pltpu.MemorySpace.SMEM)]
    parts, code = pl.pallas_call(
        p2m_kernel,
        out_shape=(
            jax.ShapeDtypeStruct((OWNERS, 80, 128), BF16),
            jax.ShapeDtypeStruct((1, COLS), jnp.int32),
        ),
        in_specs=smem + whole(5),
        out_specs=tuple(whole(2)),
        scratch_shapes=[
            pltpu.VMEM((8, 2, WIN, COEF), F32),
            pltpu.VMEM((2 * WIN, 256), F32),
            pltpu.SemaphoreType.DMA((16,)),
            pltpu.SemaphoreType.DMA((16,)),
            pltpu.SemaphoreType.DMA((16,)),
            pltpu.SemaphoreType.DMA((16,)),
        ],
        compiler_params=pltpu.CompilerParams(
            vmem_limit_bytes=32 * 1024 * 1024, collective_id=0, has_side_effects=True
        ),
        name="p2m",
    )(fb, recv, leaf_table, surf, uc2e, m2m)

    hi, lo = pl.pallas_call(
        far_kernel,
        out_shape=(
            jax.ShapeDtypeStruct((2, COEF, 256), BF16),
            jax.ShapeDtypeStruct((2, COEF, 256), BF16),
        ),
        in_specs=smem + whole(2) + [pl.BlockSpec(memory_space=pl.ANY)] + whole(4),
        out_specs=tuple(whole(2)),
        scratch_shapes=[
            pltpu.VMEM((DEPTH, PIECE, 128), BF16),
            pltpu.VMEM((WIDE, 128), F32),
            pltpu.VMEM((BROWS + 384, 256), BF16),
            pltpu.VMEM((4, 4 * GPAD, 256), F32),
            pltpu.VMEM((2, COEF, 128), F32),
            pltpu.SemaphoreType.DMA((DEPTH,)),
        ],
        compiler_params=limits(60),
        name="far",
    )(fb, parts, nbr, flat, m2m, l2l, lattice, dc2e)

    pot = pl.pallas_call(
        l2p_kernel,
        out_shape=jax.ShapeDtypeStruct((2, COLS), F32),
        in_specs=whole(5),
        out_specs=whole(1)[0],
        compiler_params=limits(32),
        name="l2p",
    )(recv, code, surf, hi, lo)

    reply = pot.reshape(2, DEVS, CAP).transpose(1, 0, 2)
    back = lax.all_to_all(reply, ("pts", "top"), split_axis=0, concat_axis=0, tiled=True)
    back = back.reshape(OWNERS, TOP, 2, CAP).transpose(1, 2, 0, 3).reshape(8, OWNERS * CAP)
    return pl.pallas_call(
        unpack_kernel,
        out_shape=jax.ShapeDtypeStruct((8, PTS), F32),
        in_specs=whole(2),
        out_specs=whole(1)[0],
        compiler_params=limits(32),
        name="unpack",
    )(back, position)


def solution(mesh):
    placed = (
        P(None, ("pts", "top")),
        P(None, ("pts", "top")),
        P(("pts", "top")),
        P(("pts", "top")),
        P(),
        P(),
        P(),
        P(),
        P(),
        P(),
    )
    return jax.shard_map(
        per_device, mesh=mesh, in_specs=placed, out_specs=P(None, ("pts", "top")), check_vma=False
    )
```

```python
import functools
import math

import jax
import jax.numpy as jnp
import numpy as np
from jax import lax
from jax.experimental import pallas as pl
from jax.experimental.pallas import tpu as pltpu
from jax.sharding import PartitionSpec as P

LEVEL = 3
EDGE = 6
COEF = 152
OFFSETS = 316
PTS = 1024
OWN = 4096
CAP = 64
OWNERS = 32
TOP = 4
DEVS = 128
COLS = DEVS * CAP
BOXES = 512
WIN = 32
GROUPS = 38
CHUNKS = 1501
GPAD = 40
WIDE = 60048
PIECE = 1440
PIECES = 40
DEPTH = 8
TAIL = COEF - 128
CLASS = 80
BROWS = CLASS * COEF
CHUNK = 512

F32 = jnp.float32
BF16 = jnp.bfloat16
VM = pltpu.MemorySpace.VMEM
MESH = pl.DeviceIdType.MESH


def surface_table():
    grid_vals = np.linspace(-1.0, 1.0, EDGE)
    points_list = []
    for a in range(EDGE):
        for b in range(EDGE):
            for c in range(EDGE):
                if min(a, b, c) == 0 or max(a, b, c) == EDGE - 1:
                    points_list.append([grid_vals[a], grid_vals[b], grid_vals[c]])
    return np.array(points_list, dtype=np.float32).T


def surface_columns():
    table = np.zeros((COEF, 8), np.float32)
    table[:, :3] = (np.float32(1.25) * surface_table()).T
    return jnp.asarray(table)


def offset_table():
    points_list = []
    for dx in range(-3, 4):
        for dy in range(-3, 4):
            for dz in range(-3, 4):
                if max(abs(dx), abs(dy), abs(dz)) >= 2:
                    points_list.append([dx, dy, dz])
    return np.array(points_list, dtype=np.int32)


def dilate(value):
    return sum(((value >> bit) & 1) << (3 * bit) for bit in range(LEVEL))


def shift_rows():
    rows = np.zeros((CLASS // 2, 4, 256), np.int32)
    table = offset_table()
    lane = np.arange(256)
    for pair in range(CLASS // 2):
        offset = CLASS * ((lane >> 5) & 3) + 2 * pair + (lane >> 7)
        known = offset < OFFSETS
        steps = table[np.minimum(offset, OFFSETS - 1)] % 8
        for dim in range(3):
            rows[pair, dim] = [dilate(int(v)) << (2 - dim) for v in steps[:, dim]]
        rows[pair, 3] = np.where(known, 0, -1)
    return jnp.asarray(rows)


def split2(x):
    hi = x.astype(BF16)
    lo = (x - hi.astype(F32)).astype(BF16)
    return hi, lo


def split3(x):
    hi = x.astype(BF16)
    rest = x - hi.astype(F32)
    mid = rest.astype(BF16)
    lo = (rest - mid.astype(F32)).astype(BF16)
    return hi, mid, lo


def dot_nn(a, b):
    return lax.dot_general(a, b, (((1,), (0,)), ((), ())), preferred_element_type=F32)


def dot_nt(a, b):
    return lax.dot_general(a, b, (((1,), (1,)), ((), ())), preferred_element_type=F32)


def nt3(x, w):
    rows = x.shape[0]
    xh, xl = split2(x)
    wh, wl = split2(w)
    both = dot_nt(jnp.concatenate([xh, xl], axis=0), wh)
    return both[:rows] + both[rows:] + dot_nt(xh, wl)


def iota(shape, dim):
    return lax.broadcasted_iota(jnp.int32, shape, dim)


def onehot(mask):
    return jnp.where(mask, 1.0, 0.0).astype(BF16)


def matrices(flat_ref, main_ref, tail_ref):
    lane = iota((76, 128), 1)
    for r in range(16):
        chunk, shift = divmod(COEF * r, 128)
        count = 3 if shift + COEF > 256 else 2
        turned = []
        for c in range(count):
            value = flat_ref[pl.ds(chunk + c, 76, stride=19), :]
            turned.append(pltpu.roll(value, 128 - shift, 1) if shift else value)
        keep = lane < 128 - shift
        main = jnp.where(keep, turned[0], turned[1])
        tail = jnp.where(keep, turned[1], turned[2]) if count == 3 else turned[1]
        main_ref[pl.ds(r, 76, stride=16), :] = main
        tail_ref[pl.ds(r, 76, stride=16), :] = tail


def matrix(main_ref, tail_ref, octant):
    rows = slice(COEF * octant, COEF * octant + COEF)
    return jnp.concatenate([main_ref[rows], tail_ref[rows, 0:TAIL]], axis=1)


def mix(first, second):
    left = iota(first.shape, 1) % 128 < CAP
    even = jnp.where(left, first, pltpu.roll(second, CAP, 1))
    odd = jnp.where(left, pltpu.roll(first, CAP, 1), second)
    return even, odd


def place_of(index):
    return {"pts": index // TOP, "top": index % TOP}


def greet(barrier, me):
    def hello(step, carry):
        pl.semaphore_signal(
            barrier, inc=1, device_id=place_of((me + step) % DEVS), device_id_type=MESH
        )
        return carry

    lax.fori_loop(1, DEVS, hello, 0)


def trade(me, source_ref, target_ref, sems):
    def block(slot, target):
        return pltpu.make_async_remote_copy(
            src_ref=source_ref.at[target],
            dst_ref=target_ref.at[slot],
            send_sem=sems[0],
            recv_sem=sems[1],
            device_id=place_of(target),
            device_id_type=MESH,
        )

    def push(step, carry):
        block(me, (me + step) % DEVS).start()
        return carry

    lax.fori_loop(1, DEVS, push, 0)
    target_ref[me] = source_ref[me]
    return pltpu.make_async_remote_copy(
        src_ref=source_ref.at[pl.ds(0, DEVS - 1)],
        dst_ref=target_ref.at[pl.ds(0, DEVS - 1)],
        send_sem=sems[0],
        recv_sem=sems[1],
        device_id=place_of((me + 1) % DEVS),
        device_id_type=MESH,
    )


def pack_kernel(
    pos_ref,
    dens_ref,
    slot_ref,
    leaf_ref,
    m2m_ref,
    l2l_ref,
    recv_ref,
    where_ref,
    leaves_ref,
    m2m_main,
    m2m_tail,
    l2l_main,
    l2l_tail,
    load_ref,
    send_ref,
    send_sem,
    recv_sem,
    push_sem,
    pull_sem,
):
    top = lax.axis_index("top")
    me = TOP * lax.axis_index("pts") + top
    barrier = pltpu.get_barrier_semaphore()
    greet(barrier, me)
    slot = slot_ref[...]
    owner = slot >> 12
    member = jnp.where(iota((OWNERS, PTS), 0) == owner, 1.0, 0.0)
    before = onehot(iota((PTS, PTS), 0) < iota((PTS, PTS), 1))
    prefix = dot_nn(member.astype(BF16), before)
    rank = jnp.sum(member * prefix, axis=0, keepdims=True)
    position = owner * CAP + rank.astype(jnp.int32)
    where_ref[...] = position
    load_ref[...] = jnp.zeros_like(load_ref)
    load_ref[0:1] = pos_ref[0:1]
    load_ref[1:2] = pos_ref[2:3]
    load_ref[8:9] = pos_ref[1:2]
    load_ref[9:10] = ((slot & (OWN - 1)) + 1).astype(F32)
    for pair in range(4):
        load_ref[2 + pair : 3 + pair] = dens_ref[2 * pair : 2 * pair + 1]
        load_ref[10 + pair : 11 + pair] = dens_ref[2 * pair + 1 : 2 * pair + 2]
    payload = jnp.concatenate(split3(load_ref[...]), axis=0)
    for block in range(8):
        pick = onehot(iota((256, PTS), 0) + 256 * block == position)
        res = dot_nt(payload, pick)
        value = res[0:16] + res[16:32] + res[32:48]
        for pair in range(2):
            lanes = slice(128 * pair, 128 * pair + 128)
            tiles = mix(value[0:8, lanes], value[8:16, lanes])
            for part, tile in enumerate(tiles):
                own = 4 * block + 2 * pair + part
                for column in range(TOP):
                    send_ref[TOP * own + column, 0:2, :] = tile[0:2]
                    send_ref[TOP * own + column, 2:3, :] = tile[2 + column : 3 + column]
    pl.semaphore_wait(barrier, DEVS - 1)
    waits = trade(me, send_ref, recv_ref, (send_sem, recv_sem))

    def share(step, slot):
        return pltpu.make_async_remote_copy(
            src_ref=leaf_ref,
            dst_ref=leaves_ref.at[slot],
            send_sem=push_sem.at[step],
            recv_sem=pull_sem.at[step],
            device_id={"top": (top + step) % TOP},
            device_id_type=MESH,
        )

    for step in range(1, TOP):
        share(step, top).start()
    leaves_ref[top] = leaf_ref[...]
    matrices(m2m_ref, m2m_main, m2m_tail)
    matrices(l2l_ref, l2l_main, l2l_tail)
    for step in range(1, TOP):
        share(step, (top + TOP - step) % TOP).wait_recv()
        share(step, top).wait_send()
    waits.wait_recv()
    waits.wait_send()


def row_of(tab_ref, index, start):
    rows = [tab_ref[index, pl.ds(start + q, 1), :] for q in range(CHUNK // 128)]
    return jnp.concatenate(rows, axis=1)


def green(tab_ref, surf_ref, start):
    squared = None
    for dim in range(3):
        gap = surf_ref[:, dim : dim + 1] - row_of(tab_ref, dim, start)
        squared = gap * gap if squared is None else squared + gap * gap
    return lax.rsqrt(squared)


FACTOR = 1.0 / (4.0 * math.pi)


def p2m_kernel(
    recv_ref,
    leaves_ref,
    surf_ref,
    uc2e_ref,
    m2m_main,
    m2m_tail,
    gath_ref,
    code_ref,
    tab_ref,
    acc_ref,
    order_ref,
    pad_ref,
    tmp_ref,
    send_sem,
    recv_sem,
    pass_sem,
    take_sem,
):
    me = lax.axis_index("pts")
    x, y, core = me // 8, (me // 2) % 4, me % 2
    partner = me + 1 - 2 * core

    def other(step, sign, side):
        return ((x + sign * (step // 4) + 4) % 4) * 8 + ((y + sign * (step % 4) + 4) % 4) * 2 + side

    barrier = pltpu.get_barrier_semaphore()
    for step in range(1, 16):
        pl.semaphore_signal(
            barrier, inc=1, device_id={"pts": other(step, 1, core)}, device_id_type=MESH
        )
    pl.semaphore_signal(barrier, inc=1, device_id={"pts": partner}, device_id_type=MESH)

    acc_ref[...] = jnp.zeros_like(acc_ref)
    pad_ref[...] = jnp.zeros_like(pad_ref)
    for pair in range(3):
        tmp_ref[...] = recv_ref[:, pair, :]
        tiles = mix(tmp_ref[pl.ds(0, 64, stride=2), :], tmp_ref[pl.ds(1, 64, stride=2), :])
        tab_ref[2 * pair] = tiles[0]
        tab_ref[2 * pair + 1] = tiles[1]
    first = leaves_ref[0, 0:1, 0:1] >> 3
    table = (leaves_ref[...].reshape(32, 128) - 8 * first).astype(F32).astype(BF16)
    eye = onehot(iota((128, 128), 0) == iota((128, 128), 1))
    table = dot_nt(eye, table).astype(BF16)

    def step(index, carry):
        cols = pl.ds(pl.multiple_of(index * CHUNK, CHUNK), CHUNK)
        start = index * (CHUNK // 128)
        slot = row_of(tab_ref, 3, start).astype(jnp.int32) - 1
        high = onehot(iota((32, CHUNK), 0) == (slot >> 7))
        rows = dot_nn(table, high)
        leaf = jnp.sum(
            jnp.where(iota((128, CHUNK), 0) == (slot & 127), rows, 0.0), axis=0, keepdims=True
        ).astype(jnp.int32)
        code = (leaf & 7) * WIN + (leaf >> 3)
        code_ref[:, cols] = code
        pick = onehot(iota((256, CHUNK), 0) == code)
        kernel = green(tab_ref, surf_ref, start)
        weighted = []
        for dens in range(2):
            value = kernel * (row_of(tab_ref, 4 + dens, start) * FACTOR)
            high = value.astype(BF16).astype(F32)
            weighted += [high, value - high]
        acc_ref[...] += dot_nt(jnp.concatenate(weighted, axis=0).astype(BF16), pick)
        return carry

    lax.fori_loop(0, COLS // CHUNK, step, 0)
    eye = onehot(iota((256, 256), 0) == iota((256, 256), 1))
    for dens in range(2):
        base = 2 * COEF * dens
        total = acc_ref[base : base + COEF] + acc_ref[base + COEF : base + 2 * COEF]
        hi, mid, rest = split3(total)
        turned = dot_nt(eye, hi) + dot_nt(eye, mid) + dot_nt(eye, rest)
        order_ref[:, dens] = turned.reshape(8, WIN, COEF)
    leaf_mult = nt3(order_ref[...].reshape(2 * 256, COEF), uc2e_ref[...])
    part = nt3(leaf_mult[0:64], matrix(m2m_main, m2m_tail, 0))
    for octant in range(1, 8):
        part = part + nt3(
            leaf_mult[64 * octant : 64 * octant + 64], matrix(m2m_main, m2m_tail, octant)
        )
    pad_ref[:, 0:COEF] = part
    lane = iota((16, 128), 1)
    tail = jnp.where(
        lane == 96,
        (first >> 3).astype(F32),
        jnp.where(lane == 97, (first & 7).astype(F32), 0.0),
    )
    for group in range(4):
        piece = pad_ref[16 * group : 16 * group + 16, 128:256]
        tail = tail + (pltpu.roll(piece, TAIL * group, 1) if group else piece)
    gath_ref[me, 0:64] = pad_ref[:, 0:128].astype(BF16)
    gath_ref[me, 64:80] = tail.astype(BF16)

    pl.semaphore_wait(barrier, 16)

    def copy(slot, sems, index, target):
        return pltpu.make_async_remote_copy(
            src_ref=gath_ref.at[slot],
            dst_ref=gath_ref.at[slot],
            send_sem=sems[0].at[index],
            recv_sem=sems[1].at[index],
            device_id={"pts": target},
            device_id_type=MESH,
        )

    far = (send_sem, recv_sem)
    near = (pass_sem, take_sem)
    copy(me, near, 0, partner).start()
    for step in range(1, 16):
        copy(me, far, step, other(step, 1, core)).start()
    for step in range(1, 16):
        slot = other(step, -1, core)
        copy(slot, far, step, partner).wait_recv()
        copy(slot, near, step, partner).start()
    copy(partner, near, 0, partner).wait_recv()
    for step in range(1, 16):
        copy(other(step, -1, 1 - core), near, step, partner).wait_recv()
    copy(me, near, 0, partner).wait_send()
    for step in range(1, 16):
        copy(me, far, step, partner).wait_send()
        copy(other(step, -1, core), near, step, partner).wait_send()


def far_kernel(
    parts_ref,
    leaves_ref,
    shift_ref,
    flat_hbm,
    m2m_main,
    m2m_tail,
    l2l_main,
    l2l_tail,
    lattice_ref,
    dc2e_ref,
    hi_ref,
    lo_ref,
    stage_ref,
    wide_ref,
    src_ref,
    acc_ref,
    check_ref,
    sem,
):
    def fetch(index, size):
        return pltpu.make_async_copy(
            flat_hbm.at[pl.ds(index * PIECE, size)],
            stage_ref.at[index % DEPTH, pl.ds(0, size)],
            sem.at[index % DEPTH],
        )

    last = GROUPS * CHUNKS - (PIECES - 1) * PIECE
    for index in range(DEPTH):
        fetch(index, PIECE).start()
    row = iota((BOXES, 1), 0)
    box = ((row & 7) << 6) + (row & 56) + (row >> 6)
    eye = onehot(iota((COEF, COEF), 0) == iota((COEF, COEF), 1))
    codes = parts_ref[:, 64, :].astype(F32)
    lane = iota((OWNERS, 128), 1)
    first = jnp.sum(
        jnp.where(lane == 96, 8.0 * codes, jnp.where(lane == 97, codes, 0.0)),
        axis=1,
        keepdims=True,
    )
    spread = jnp.where(iota((OWNERS, 512), 0) == (iota((OWNERS, 512), 1) >> 4), first, 0.0)
    start = jnp.sum(spread, axis=0, keepdims=True).astype(jnp.int32)
    start = start + (iota((1, 512), 1) & 15)
    halves = []
    for half in range(2):
        place = onehot(box == start + 16 * half)
        pieces = [
            parts_ref[:, 32 * dens + 16 * half : 32 * dens + 16 * half + 16, :].reshape(512, 128)
            for dens in range(2)
        ]
        pieces.append(parts_ref[:, 64:80, :].reshape(512, 128))
        halves.append(dot_nn(place, jnp.concatenate(pieces, axis=1)))
    level = []
    for dens in range(2):
        main = slice(128 * dens, 128 * dens + 128)
        tail = 256 + 2 * TAIL * dens
        value = jnp.concatenate(
            [
                halves[0][:, main] + halves[1][:, main],
                halves[0][:, tail : tail + TAIL] + halves[1][:, tail + TAIL : tail + 2 * TAIL],
            ],
            axis=1,
        )
        level.append(value)
    low = jnp.concatenate([dot_nt(eye, value.astype(BF16)) for value in level], axis=0)
    low = low.astype(BF16)
    src_ref[0:128] = jnp.zeros((128, 256), BF16)
    src_ref[128 + BROWS : 384 + BROWS] = jnp.zeros((256, 256), BF16)
    wide_ref[PIECES * PIECE : WIDE] = jnp.zeros((WIDE - PIECES * PIECE, 128), F32)

    window = leaves_ref[0, 0:1, 0:1] >> 3
    spot = (window + (iota((1, 256), 1) & 31)) & (BOXES - 1)
    masks = (0o444, 0o222, 0o111)
    based = [spot | (-1 - mask) for mask in masks]

    def build(pair, carry):
        shifts = shift_ref[pair]
        nbr = shifts[3:4]
        for dim in range(3):
            nbr = nbr | ((based[dim] + shifts[dim : dim + 1]) & masks[dim])
        pick = onehot(box == nbr)
        found = dot_nn(low, pick)
        top = jnp.concatenate([found[0:COEF, 0:128], found[COEF:, 0:128]], axis=1)
        bottom = jnp.concatenate([found[0:COEF, 128:256], found[COEF:, 128:256]], axis=1)
        both = jnp.concatenate([top, bottom], axis=0).astype(BF16)
        src_ref[pl.ds(pl.multiple_of(128 + pair * 304, 16), 304)] = both

        @pl.when(pair < PIECES - 1)
        def _():
            fetch(pair, PIECE).wait()

        @pl.when(pair == PIECES - 1)
        def _():
            fetch(pair, last).wait()

        wide_ref[pl.ds(pl.multiple_of(pair * PIECE, 32), PIECE)] = stage_ref[pair % DEPTH].astype(
            F32
        )

        @pl.when(pair + DEPTH < PIECES - 1)
        def _():
            fetch(pair + DEPTH, PIECE).start()

        @pl.when(pair + DEPTH == PIECES - 1)
        def _():
            fetch(pair + DEPTH, last).start()

        return carry

    lax.fori_loop(0, PIECES, build, 0)

    up = None
    for o in range(8):
        rows = jnp.concatenate(
            [level[0][64 * o : 64 * o + 64], level[1][64 * o : 64 * o + 64]], axis=0
        )
        term = nt3(rows, matrix(m2m_main, m2m_tail, o))
        up = term if up is None else up + term
    up2 = None
    for o in range(8):
        rows = jnp.concatenate([up[8 * o : 8 * o + 8], up[64 + 8 * o : 72 + 8 * o]], axis=0)
        term = nt3(rows, matrix(m2m_main, m2m_tail, o))
        up2 = term if up2 is None else up2 + term
    row16 = iota((16, 1), 0)
    up3 = None
    for o in range(8):
        term = nt3(jnp.where((row16 & 7) == o, up2, 0.0), matrix(m2m_main, m2m_tail, o))
        up3 = term if up3 is None else up3 + term
    root0 = jnp.sum(up3[0:8], axis=0, keepdims=True)
    root1 = jnp.sum(up3[8:16], axis=0, keepdims=True)
    root = jnp.where(row16 < 8, root0, root1)
    down = nt3(root, lattice_ref[...])
    down1 = None
    for o in range(8):
        term = nt3(jnp.where((row16 & 7) == o, down, 0.0), matrix(l2l_main, l2l_tail, o))
        down1 = term if down1 is None else down1 + term
    down2 = jnp.concatenate([nt3(down1, matrix(l2l_main, l2l_tail, o)) for o in range(8)], axis=0)
    row64 = iota((64, 1), 0)
    target = (window + (row64 & 31)) & (BOXES - 1)
    parent = ((target >> 3) & 7) * 16 + (row64 >> 5) * 8 + (target >> 6)
    choose = onehot(iota((64, 128), 1) == parent)
    hi, mid, rest = split3(down2)
    parents = dot_nn(choose, hi) + dot_nn(choose, mid) + dot_nn(choose, rest)
    far = None
    for o in range(8):
        term = nt3(jnp.where((target & 7) == o, parents, 0.0), matrix(l2l_main, l2l_tail, o))
        far = term if far is None else far + term

    acc_ref[...] = jnp.zeros_like(acc_ref)

    def mult(index, carry):
        for r in range(4):
            lhs = []
            for m in range(4):
                chunk = 375 * r + 95 * m + index * 8
                lhs.append(
                    jnp.concatenate(
                        [wide_ref[pl.ds(chunk + q, GPAD, stride=CHUNKS), :] for q in range(8)],
                        axis=1,
                    )
                )
            begin = pl.multiple_of(128 - 32 * r + index * 1024, 32)
            acc_ref[r] += dot_nn(
                jnp.concatenate(lhs, axis=0).astype(BF16), src_ref[pl.ds(begin, 1024)]
            )
        return carry

    lax.fori_loop(0, 12, mult, 0)
    block = (iota((1, 256), 1) >> 5) & 3
    for r in range(4):
        value = None
        for m in range(4):
            term = jnp.where(block == m, acc_ref[r, GPAD * m : GPAD * m + GROUPS], 0.0)
            value = term if value is None else value + term
        for half in range(2):
            lanes = slice(128 * half, 128 * half + 128)
            check_ref[half, pl.ds(r, GROUPS, stride=4), :] = value[:, lanes]
    lane = iota((64, 256), 1)
    fold = onehot(((lane & 31) == (row64 & 31)) & ((lane >> 7) == (row64 >> 5)))
    hi, mid, rest = split3(jnp.concatenate([check_ref[0], check_ref[1]], axis=1))
    checks = dot_nt(fold, hi) + dot_nt(fold, mid) + dot_nt(fold, rest)
    local = nt3(checks, dc2e_ref[...]) + far
    leaves = [nt3(local, matrix(l2l_main, l2l_tail, o)) for o in range(8)]
    for dens in range(2):
        value = jnp.concatenate([leaf[WIN * dens : WIN * dens + WIN] for leaf in leaves], axis=0)
        hi, lo = split2(value)
        hi_ref[dens] = dot_nt(eye, hi).astype(BF16)
        lo_ref[dens] = dot_nt(eye, lo).astype(BF16)


def l2p_kernel(
    tab_ref,
    code_ref,
    surf_ref,
    hi_ref,
    lo_ref,
    where_ref,
    out_ref,
    pot_ref,
    tmp_ref,
    rows_ref,
    reply_ref,
    back_ref,
    send_sem,
    recv_sem,
):
    me = TOP * lax.axis_index("pts") + lax.axis_index("top")
    barrier = pltpu.get_barrier_semaphore()
    greet(barrier, me)
    wide = jnp.concatenate(
        [hi_ref[0], lo_ref[0], hi_ref[1], lo_ref[1]], axis=0
    )

    def step(index, carry):
        cols = pl.ds(pl.multiple_of(index * CHUNK, CHUNK), CHUNK)
        start = index * (CHUNK // 128)
        pick = onehot(iota((256, CHUNK), 0) == code_ref[:, cols])
        kernel = green(tab_ref, surf_ref, start)
        found = dot_nn(wide, pick)
        for dens in range(2):
            base = 2 * COEF * dens
            value = found[base : base + COEF] + found[base + COEF : base + 2 * COEF]
            row = jnp.sum(kernel * value, axis=0, keepdims=True) * FACTOR
            for q in range(CHUNK // 128):
                pot_ref[dens, pl.ds(start + q, 1), :] = row[:, 128 * q : 128 * q + 128]
        return carry

    lax.fori_loop(0, COLS // CHUNK, step, 0)
    even, odd = mix(pot_ref[0], pot_ref[1])
    tmp_ref[pl.ds(0, 64, stride=2), :] = even
    tmp_ref[pl.ds(1, 64, stride=2), :] = odd
    reply_ref[...] = tmp_ref[...].reshape(DEVS, 1, 128)
    pl.semaphore_wait(barrier, DEVS - 1)
    waits = trade(me, reply_ref, back_ref, (send_sem, recv_sem))
    waits.wait_recv()
    tmp_ref[...] = back_ref[...].reshape(DEVS, 128)
    for top in range(TOP):
        tiles = mix(
            tmp_ref[pl.ds(top, 16, stride=8), :], tmp_ref[pl.ds(TOP + top, 16, stride=8), :]
        )
        for dens in range(2):
            rows_ref[pl.ds(2 * top + dens, 16, stride=8), :] = tiles[dens]
    value = jnp.concatenate([rows_ref[8 * j : 8 * j + 8] for j in range(16)], axis=1)
    hi = value.astype(BF16).astype(F32)
    mid = (value - hi).astype(BF16).astype(F32)
    pieces = jnp.concatenate([hi, mid, value - hi - mid], axis=0).astype(BF16)
    position = where_ref[...]
    total = None
    for block in range(8):
        pick = onehot(iota((256, PTS), 0) + 256 * block == position)
        term = dot_nn(pieces[:, 256 * block : 256 * block + 256], pick)
        total = term if total is None else total + term
    out_ref[...] = total[0:8] + total[8:16] + total[16:24]
    waits.wait_send()


def whole(count):
    return [pl.BlockSpec(memory_space=VM)] * count


def limits(mib):
    return pltpu.CompilerParams(vmem_limit_bytes=mib * 1024 * 1024)


def talking(mib, ident):
    return pltpu.CompilerParams(
        vmem_limit_bytes=mib * 1024 * 1024, collective_id=ident, has_side_effects=True
    )


def per_device(
    local_pos, densities, morton_slot, slot_leaf, uc2e, m2m, m2l_ops, dc2e, lattice, l2l
):
    surf = surface_columns()
    flat = m2l_ops.reshape(GROUPS * CHUNKS, 128)
    smalls = (1216, 128)
    recv, position, leaves, mm, mt, lm, lt = pl.pallas_call(
        pack_kernel,
        out_shape=(
            jax.ShapeDtypeStruct((DEVS, 3, 128), F32),
            jax.ShapeDtypeStruct((1, PTS), jnp.int32),
            jax.ShapeDtypeStruct((TOP, 8, 128), jnp.int32),
        )
        + (jax.ShapeDtypeStruct(smalls, F32),) * 4,
        in_specs=whole(6),
        out_specs=tuple(whole(7)),
        scratch_shapes=[
            pltpu.VMEM((16, PTS), F32),
            pltpu.VMEM((DEVS, 3, 128), F32),
            pltpu.SemaphoreType.DMA,
            pltpu.SemaphoreType.DMA,
            pltpu.SemaphoreType.DMA((TOP,)),
            pltpu.SemaphoreType.DMA((TOP,)),
        ],
        compiler_params=talking(32, 0),
        name="pack",
    )(
        local_pos,
        densities,
        morton_slot.reshape(1, PTS),
        slot_leaf.reshape(8, 128),
        m2m.reshape(1444, 128),
        l2l.reshape(1444, 128),
    )

    parts, code, tab = pl.pallas_call(
        p2m_kernel,
        out_shape=(
            jax.ShapeDtypeStruct((OWNERS, 80, 128), BF16),
            jax.ShapeDtypeStruct((1, COLS), jnp.int32),
            jax.ShapeDtypeStruct((6, 64, 128), F32),
        ),
        in_specs=whole(6),
        out_specs=tuple(whole(3)),
        scratch_shapes=[
            pltpu.VMEM((4 * COEF, 256), F32),
            pltpu.VMEM((8, 2, WIN, COEF), F32),
            pltpu.VMEM((2 * WIN, 256), F32),
            pltpu.VMEM((128, 128), F32),
            pltpu.SemaphoreType.DMA((16,)),
            pltpu.SemaphoreType.DMA((16,)),
            pltpu.SemaphoreType.DMA((16,)),
            pltpu.SemaphoreType.DMA((16,)),
        ],
        compiler_params=talking(32, 1),
        name="p2m",
    )(recv, leaves, surf, uc2e, mm, mt)

    hi, lo = pl.pallas_call(
        far_kernel,
        out_shape=(
            jax.ShapeDtypeStruct((2, COEF, 256), BF16),
            jax.ShapeDtypeStruct((2, COEF, 256), BF16),
        ),
        in_specs=whole(3) + [pl.BlockSpec(memory_space=pl.ANY)] + whole(6),
        out_specs=tuple(whole(2)),
        scratch_shapes=[
            pltpu.VMEM((DEPTH, PIECE, 128), BF16),
            pltpu.VMEM((WIDE, 128), F32),
            pltpu.VMEM((BROWS + 384, 256), BF16),
            pltpu.VMEM((4, 4 * GPAD, 256), F32),
            pltpu.VMEM((2, COEF, 128), F32),
            pltpu.SemaphoreType.DMA((DEPTH,)),
        ],
        compiler_params=limits(60),
        name="far",
    )(parts, leaves, shift_rows(), flat, mm, mt, lm, lt, lattice, dc2e)

    return pl.pallas_call(
        l2p_kernel,
        out_shape=jax.ShapeDtypeStruct((8, PTS), F32),
        in_specs=whole(6),
        out_specs=whole(1)[0],
        scratch_shapes=[
            pltpu.VMEM((2, 64, 128), F32),
            pltpu.VMEM((128, 128), F32),
            pltpu.VMEM((128, 128), F32),
            pltpu.VMEM((DEVS, 1, 128), F32),
            pltpu.VMEM((DEVS, 1, 128), F32),
            pltpu.SemaphoreType.DMA,
            pltpu.SemaphoreType.DMA,
        ],
        compiler_params=talking(32, 2),
        name="l2p",
    )(tab, code, surf, hi, lo, position)


def solution(mesh):
    placed = (
        P(None, ("pts", "top")),
        P(None, ("pts", "top")),
        P(("pts", "top")),
        P(("pts", "top")),
        P(),
        P(),
        P(),
        P(),
        P(),
        P(),
    )
    return jax.shard_map(
        per_device, mesh=mesh, in_specs=placed, out_specs=P(None, ("pts", "top")), check_vma=False
    )
```

```python
import functools
import math

import jax
import jax.numpy as jnp
import numpy as np
from jax import lax
from jax.experimental import pallas as pl
from jax.experimental.pallas import tpu as pltpu
from jax.sharding import PartitionSpec as P

LEVEL = 3
EDGE = 6
COEF = 152
OFFSETS = 316
PTS = 1024
OWN = 4096
CAP = 64
OWNERS = 32
TOP = 4
DEVS = 128
COLS = DEVS * CAP
BOXES = 512
WIN = 32
GROUPS = 38
CHUNKS = 1501
GPAD = 40
WIDE = 60048
PIECE = 1440
PIECES = 40
DEPTH = 8
TAIL = COEF - 128
CLASS = 80
BROWS = CLASS * COEF
CHUNK = 1024

F32 = jnp.float32
BF16 = jnp.bfloat16
VM = pltpu.MemorySpace.VMEM
MESH = pl.DeviceIdType.MESH


def surface_table():
    grid_vals = np.linspace(-1.0, 1.0, EDGE)
    points_list = []
    for a in range(EDGE):
        for b in range(EDGE):
            for c in range(EDGE):
                if min(a, b, c) == 0 or max(a, b, c) == EDGE - 1:
                    points_list.append([grid_vals[a], grid_vals[b], grid_vals[c]])
    return np.array(points_list, dtype=np.float32).T


def surface_columns():
    table = np.zeros((COEF, 8), np.float32)
    table[:, :3] = (np.float32(1.25) * surface_table()).T
    return jnp.asarray(table)


def offset_table():
    points_list = []
    for dx in range(-3, 4):
        for dy in range(-3, 4):
            for dz in range(-3, 4):
                if max(abs(dx), abs(dy), abs(dz)) >= 2:
                    points_list.append([dx, dy, dz])
    return np.array(points_list, dtype=np.int32)


def dilate(value):
    return sum(((value >> bit) & 1) << (3 * bit) for bit in range(LEVEL))


def shift_rows():
    rows = np.zeros((CLASS // 2, 4, 256), np.int32)
    table = offset_table()
    lane = np.arange(256)
    for pair in range(CLASS // 2):
        offset = CLASS * ((lane >> 5) & 3) + 2 * pair + (lane >> 7)
        known = offset < OFFSETS
        steps = table[np.minimum(offset, OFFSETS - 1)] % 8
        for dim in range(3):
            rows[pair, dim] = [dilate(int(v)) << (2 - dim) for v in steps[:, dim]]
        rows[pair, 3] = np.where(known, 0, -1)
    return jnp.asarray(rows)


def split2(x):
    hi = x.astype(BF16)
    lo = (x - hi.astype(F32)).astype(BF16)
    return hi, lo


def split3(x):
    hi = x.astype(BF16)
    rest = x - hi.astype(F32)
    mid = rest.astype(BF16)
    lo = (rest - mid.astype(F32)).astype(BF16)
    return hi, mid, lo


def dot_nn(a, b):
    return lax.dot_general(a, b, (((1,), (0,)), ((), ())), preferred_element_type=F32)


def dot_nt(a, b):
    return lax.dot_general(a, b, (((1,), (1,)), ((), ())), preferred_element_type=F32)


def nt3(x, w):
    rows = x.shape[0]
    xh, xl = split2(x)
    both = dot_nt(jnp.concatenate([xh, xl], axis=0), w[0])
    return both[:rows] + both[rows:] + dot_nt(xh, w[1])


def iota(shape, dim):
    return lax.broadcasted_iota(jnp.int32, shape, dim)


def onehot(mask):
    return jnp.where(mask, 1.0, 0.0).astype(BF16)


def matrices(flat_ref, main_ref, tail_ref):
    lane = iota((76, 128), 1)
    for r in range(16):
        chunk, shift = divmod(COEF * r, 128)
        count = 3 if shift + COEF > 256 else 2
        turned = []
        for c in range(count):
            value = flat_ref[pl.ds(chunk + c, 76, stride=19), :]
            turned.append(pltpu.roll(value, 128 - shift, 1) if shift else value)
        keep = lane < 128 - shift
        main = jnp.where(keep, turned[0], turned[1])
        tail = jnp.where(keep, turned[1], turned[2]) if count == 3 else turned[1]
        main_ref[pl.ds(r, 76, stride=16), :] = main
        tail_ref[pl.ds(r, 76, stride=16), :] = tail


def matrix(main_ref, tail_ref, octant):
    rows = slice(COEF * octant, COEF * octant + COEF)
    return jnp.concatenate([main_ref[rows], tail_ref[rows, 0:TAIL]], axis=1)


def mix(first, second):
    left = iota(first.shape, 1) % 128 < CAP
    even = jnp.where(left, first, pltpu.roll(second, CAP, 1))
    odd = jnp.where(left, pltpu.roll(first, CAP, 1), second)
    return even, odd


def place_of(index):
    return {"pts": index // TOP, "top": index % TOP}


def greet(barrier, me):
    def hello(step, carry):
        pl.semaphore_signal(
            barrier, inc=1, device_id=place_of((me + step) % DEVS), device_id_type=MESH
        )
        return carry

    lax.fori_loop(1, DEVS, hello, 0)


def trade(me, source_ref, target_ref, sems):
    def block(slot, target):
        return pltpu.make_async_remote_copy(
            src_ref=source_ref.at[target],
            dst_ref=target_ref.at[slot],
            send_sem=sems[0],
            recv_sem=sems[1],
            device_id=place_of(target),
            device_id_type=MESH,
        )

    def push(step, carry):
        block(me, (me + step) % DEVS).start()
        return carry

    lax.fori_loop(1, DEVS, push, 0)
    target_ref[me] = source_ref[me]
    return pltpu.make_async_remote_copy(
        src_ref=source_ref.at[pl.ds(0, DEVS - 1)],
        dst_ref=target_ref.at[pl.ds(0, DEVS - 1)],
        send_sem=sems[0],
        recv_sem=sems[1],
        device_id=place_of((me + 1) % DEVS),
        device_id_type=MESH,
    )


def row_of(tab_ref, index, start):
    rows = [tab_ref[index, pl.ds(start + q, 1), :] for q in range(CHUNK // 128)]
    return jnp.concatenate(rows, axis=1)


def green(tab_ref, surf_ref, start):
    squared = None
    for dim in range(3):
        gap = surf_ref[:, dim : dim + 1] - row_of(tab_ref, dim, start)
        squared = gap * gap if squared is None else squared + gap * gap
    return lax.rsqrt(squared)


FACTOR = 1.0 / (4.0 * math.pi)


def fmm_kernel(
    pos_hbm,
    dens_hbm,
    slot_hbm,
    leaf_hbm,
    m2m_hbm,
    l2l_hbm,
    uc2e_hbm,
    dc2e_hbm,
    lattice_hbm,
    surf_hbm,
    shift_hbm,
    flat_hbm,
    out_ref,
    pos_ref,
    dens_ref,
    slot_ref,
    leaf_ref,
    m2m_ref,
    l2l_ref,
    uc2e_ref,
    dc2e_ref,
    lattice_ref,
    surf_ref,
    shift_ref,
    in_sem,
    load_ref,
    send_ref,
    recv_ref,
    leaves_ref,
    main_ref,
    tail_ref,
    up_ref,
    down_ref,
    single_ref,
    stage_ref,
    wide_ref,
    stage_sem,
    tab_ref,
    code_ref,
    green_ref,
    sums_ref,
    order_ref,
    pad_ref,
    tmp_ref,
    gath_ref,
    roots_ref,
    src_ref,
    acc_ref,
    check_ref,
    leaf_mat_ref,
    pot_ref,
    rows_ref,
    reply_ref,
    back_ref,
    points_sems,
    push_sem,
    pull_sem,
    send_sem,
    recv_sem,
    pass_sem,
    take_sem,
    root_sems,
    reply_sems,
):
    own = lax.axis_index("pts")
    top = lax.axis_index("top")
    me = TOP * own + top
    x, y, core = own // 8, (own // 2) % 4, own % 2
    partner = own + 1 - 2 * core

    def other(step, sign, side):
        return ((x + sign * (step // 4) + 4) % 4) * 8 + ((y + sign * (step % 4) + 4) % 4) * 2 + side

    moves = [
        (pos_hbm, pos_ref),
        (dens_hbm, dens_ref),
        (slot_hbm, slot_ref),
        (leaf_hbm, leaf_ref),
        (m2m_hbm, m2m_ref),
        (l2l_hbm, l2l_ref),
        (uc2e_hbm, uc2e_ref),
        (dc2e_hbm, dc2e_ref),
        (lattice_hbm, lattice_ref),
        (surf_hbm, surf_ref),
        (shift_hbm, shift_ref),
    ]
    loads = [
        pltpu.make_async_copy(source, target, in_sem.at[index])
        for index, (source, target) in enumerate(moves)
    ]
    for load in loads:
        load.start()

    def fetch(index, size):
        return pltpu.make_async_copy(
            flat_hbm.at[pl.ds(index * PIECE, size)],
            stage_ref.at[index % DEPTH, pl.ds(0, size)],
            stage_sem.at[index % DEPTH],
        )

    last = GROUPS * CHUNKS - (PIECES - 1) * PIECE
    for index in range(DEPTH):
        fetch(index, PIECE).start()
    barrier = pltpu.get_barrier_semaphore()
    greet(barrier, me)

    for load in loads[:4]:
        load.wait()
    slot = slot_ref[...]
    owner = slot >> 12
    member = jnp.where(iota((OWNERS, PTS), 0) == owner, 1.0, 0.0)
    before = onehot(iota((PTS, PTS), 0) < iota((PTS, PTS), 1))
    prefix = dot_nn(member.astype(BF16), before)
    rank = jnp.sum(member * prefix, axis=0, keepdims=True)
    position = owner * CAP + rank.astype(jnp.int32)
    load_ref[...] = jnp.zeros_like(load_ref)
    load_ref[0:1] = pos_ref[0:1]
    load_ref[1:2] = pos_ref[2:3]
    load_ref[8:9] = pos_ref[1:2]
    load_ref[9:10] = ((slot & (OWN - 1)) + 1).astype(F32)
    for pair in range(4):
        load_ref[2 + pair : 3 + pair] = dens_ref[2 * pair : 2 * pair + 1]
        load_ref[10 + pair : 11 + pair] = dens_ref[2 * pair + 1 : 2 * pair + 2]
    payload = jnp.concatenate(split3(load_ref[...]), axis=0)
    for block in range(8):
        pick = onehot(iota((256, PTS), 0) + 256 * block == position)
        res = dot_nt(payload, pick)
        value = res[0:16] + res[16:32] + res[32:48]
        for pair in range(2):
            lanes = slice(128 * pair, 128 * pair + 128)
            tiles = mix(value[0:8, lanes], value[8:16, lanes])
            for part, tile in enumerate(tiles):
                target = 4 * block + 2 * pair + part
                for column in range(TOP):
                    send_ref[TOP * target + column, 0:2, :] = tile[0:2]
                    send_ref[TOP * target + column, 2:3, :] = tile[2 + column : 3 + column]
    pl.semaphore_wait(barrier, DEVS - 1)
    points = trade(me, send_ref, recv_ref, (points_sems.at[0], points_sems.at[1]))

    def share(step, place):
        return pltpu.make_async_remote_copy(
            src_ref=leaf_ref,
            dst_ref=leaves_ref.at[place],
            send_sem=push_sem.at[step],
            recv_sem=pull_sem.at[step],
            device_id={"top": (top + step) % TOP},
            device_id_type=MESH,
        )

    for step in range(1, TOP):
        share(step, top).start()
    leaves_ref[top] = leaf_ref[...]

    for load in loads[4:]:
        load.wait()
    for flat_ref, split_ref in ((m2m_ref, up_ref), (l2l_ref, down_ref)):
        matrices(flat_ref, main_ref, tail_ref)
        for octant in range(8):
            hi, lo = split2(matrix(main_ref, tail_ref, octant))
            split_ref[octant, 0] = hi
            split_ref[octant, 1] = lo
    for index, ref in enumerate((uc2e_ref, dc2e_ref, lattice_ref)):
        hi, lo = split2(ref[...])
        single_ref[index, 0] = hi
        single_ref[index, 1] = lo
    wide_ref[PIECES * PIECE : WIDE] = jnp.zeros((WIDE - PIECES * PIECE, 128), F32)
    src_ref[0:128] = jnp.zeros((128, 256), BF16)
    src_ref[128 + BROWS : 384 + BROWS] = jnp.zeros((256, 256), BF16)

    def widen(index, carry):
        @pl.when(index < PIECES - 1)
        def _():
            fetch(index, PIECE).wait()

        @pl.when(index == PIECES - 1)
        def _():
            fetch(index, last).wait()

        wide_ref[pl.ds(pl.multiple_of(index * PIECE, 32), PIECE)] = stage_ref[
            index % DEPTH
        ].astype(F32)

        @pl.when(index + DEPTH < PIECES - 1)
        def _():
            fetch(index + DEPTH, PIECE).start()

        @pl.when(index + DEPTH == PIECES - 1)
        def _():
            fetch(index + DEPTH, last).start()

        return carry

    lax.fori_loop(0, PIECES, widen, 0)
    sums_ref[...] = jnp.zeros_like(sums_ref)
    pad_ref[...] = jnp.zeros_like(pad_ref)

    for step in range(1, TOP):
        share(step, (top + TOP - step) % TOP).wait_recv()
        share(step, top).wait_send()
    points.wait_recv()

    for pair in range(3):
        tmp_ref[...] = recv_ref[:, pair, :]
        tiles = mix(tmp_ref[pl.ds(0, 64, stride=2), :], tmp_ref[pl.ds(1, 64, stride=2), :])
        tab_ref[2 * pair] = tiles[0]
        tab_ref[2 * pair + 1] = tiles[1]
    window = leaves_ref[0, 0:1, 0:1] >> 3
    table = (leaves_ref[...].reshape(32, 128) - 8 * window).astype(F32).astype(BF16)
    eye = onehot(iota((128, 128), 0) == iota((128, 128), 1))
    table = dot_nt(eye, table).astype(BF16)

    def gather(index, carry):
        cols = pl.ds(pl.multiple_of(index * CHUNK, CHUNK), CHUNK)
        start = index * (CHUNK // 128)
        place = row_of(tab_ref, 3, start).astype(jnp.int32) - 1
        high = onehot(iota((32, CHUNK), 0) == (place >> 7))
        rows = dot_nn(table, high)
        leaf = jnp.sum(
            jnp.where(iota((128, CHUNK), 0) == (place & 127), rows, 0.0), axis=0, keepdims=True
        ).astype(jnp.int32)
        code = (leaf & 7) * WIN + (leaf >> 3)
        code_ref[:, cols] = code
        pick = onehot(iota((256, CHUNK), 0) == code)
        kernel = green(tab_ref, surf_ref, start)
        green_ref[:, cols] = kernel
        weighted = []
        for dens in range(2):
            value = kernel * (row_of(tab_ref, 4 + dens, start) * FACTOR)
            high = value.astype(BF16).astype(F32)
            weighted += [high, value - high]
        sums_ref[...] += dot_nt(jnp.concatenate(weighted, axis=0).astype(BF16), pick)
        return carry

    lax.fori_loop(0, COLS // CHUNK, gather, 0)
    eye = onehot(iota((256, 256), 0) == iota((256, 256), 1))
    for dens in range(2):
        base = 2 * COEF * dens
        total = sums_ref[base : base + COEF] + sums_ref[base + COEF : base + 2 * COEF]
        hi, mid, rest = split3(total)
        turned = dot_nt(eye, hi) + dot_nt(eye, mid) + dot_nt(eye, rest)
        order_ref[:, dens] = turned.reshape(8, WIN, COEF)
    leaf_mult = nt3(order_ref[...].reshape(2 * 256, COEF), single_ref.at[0])
    part = nt3(leaf_mult[0:64], up_ref.at[0])
    for octant in range(1, 8):
        part = part + nt3(leaf_mult[64 * octant : 64 * octant + 64], up_ref.at[octant])
    pad_ref[:, 0:COEF] = part
    lane = iota((16, 128), 1)
    tail = jnp.where(
        lane == 96,
        (window >> 3).astype(F32),
        jnp.where(lane == 97, (window & 7).astype(F32), 0.0),
    )
    for group in range(4):
        piece = pad_ref[16 * group : 16 * group + 16, 128:256]
        tail = tail + (pltpu.roll(piece, TAIL * group, 1) if group else piece)
    gath_ref[own, 0:64] = pad_ref[:, 0:128].astype(BF16)
    gath_ref[own, 64:80] = tail.astype(BF16)

    def copy(place, sems, index, target):
        return pltpu.make_async_remote_copy(
            src_ref=gath_ref.at[place],
            dst_ref=gath_ref.at[place],
            send_sem=sems[0].at[index],
            recv_sem=sems[1].at[index],
            device_id={"pts": target},
            device_id_type=MESH,
        )

    far = (send_sem, recv_sem)
    near = (pass_sem, take_sem)
    copy(own, near, 0, partner).start()
    for step in range(1, 16):
        copy(own, far, step, other(step, 1, core)).start()

    row64 = iota((64, 1), 0)
    target = (window + (row64 & 31)) & (BOXES - 1)
    digits = [target & 7, (target >> 3) & 7, target >> 6]
    rise = part.astype(BF16).astype(F32)
    for digit in digits:
        total = None
        for o in range(8):
            term = nt3(jnp.where(digit == o, rise, 0.0), up_ref.at[o])
            total = term if total is None else total + term
        rise = total
    pad_ref[:, 0:COEF] = rise
    for dens in range(2):
        total = jnp.sum(pad_ref[WIN * dens : WIN * dens + WIN], axis=0, keepdims=True)
        roots_ref[own, dens : dens + 1, :] = total[:, 0:128]
        roots_ref[own, 2 + dens : 3 + dens, :] = total[:, 128:256]

    def tell(step, carry):
        pltpu.make_async_remote_copy(
            src_ref=roots_ref.at[own],
            dst_ref=roots_ref.at[own],
            send_sem=root_sems.at[0],
            recv_sem=root_sems.at[1],
            device_id={"pts": (own + step) % OWNERS},
            device_id_type=MESH,
        ).start()
        return carry

    lax.fori_loop(1, OWNERS, tell, 0)
    for step in range(1, 16):
        place = other(step, -1, core)
        copy(place, far, step, partner).wait_recv()
        copy(place, near, step, partner).start()
    told = pltpu.make_async_remote_copy(
        src_ref=roots_ref.at[pl.ds(0, OWNERS - 1)],
        dst_ref=roots_ref.at[pl.ds(0, OWNERS - 1)],
        send_sem=root_sems.at[0],
        recv_sem=root_sems.at[1],
        device_id={"pts": partner},
        device_id_type=MESH,
    )
    told.wait_recv()
    root = jnp.sum(roots_ref[...], axis=0)
    root = jnp.concatenate([root[0:2], root[2:4, 0:TAIL]], axis=1)
    fall = jnp.where(row64 < WIN, root[0:1], root[1:2])
    fall = nt3(fall, single_ref.at[2])
    for digit in digits[::-1]:
        total = None
        for o in range(8):
            term = nt3(jnp.where(digit == o, fall, 0.0), down_ref.at[o])
            total = term if total is None else total + term
        fall = total
    copy(partner, near, 0, partner).wait_recv()
    for step in range(1, 16):
        copy(other(step, -1, 1 - core), near, step, partner).wait_recv()

    row = iota((BOXES, 1), 0)
    box = ((row & 7) << 6) + (row & 56) + (row >> 6)
    eye = onehot(iota((COEF, COEF), 0) == iota((COEF, COEF), 1))
    codes = gath_ref[:, 64, :].astype(F32)
    lane = iota((OWNERS, 128), 1)
    first = jnp.sum(
        jnp.where(lane == 96, 8.0 * codes, jnp.where(lane == 97, codes, 0.0)),
        axis=1,
        keepdims=True,
    )
    spread = jnp.where(iota((OWNERS, 512), 0) == (iota((OWNERS, 512), 1) >> 4), first, 0.0)
    start = jnp.sum(spread, axis=0, keepdims=True).astype(jnp.int32)
    start = start + (iota((1, 512), 1) & 15)
    halves = []
    for half in range(2):
        place = onehot(box == start + 16 * half)
        pieces = [
            gath_ref[:, 32 * dens + 16 * half : 32 * dens + 16 * half + 16, :].reshape(512, 128)
            for dens in range(2)
        ]
        pieces.append(gath_ref[:, 64:80, :].reshape(512, 128))
        halves.append(dot_nn(place, jnp.concatenate(pieces, axis=1)))
    low = []
    for dens in range(2):
        main = slice(128 * dens, 128 * dens + 128)
        tail = 256 + 2 * TAIL * dens
        value = jnp.concatenate(
            [
                halves[0][:, main] + halves[1][:, main],
                halves[0][:, tail : tail + TAIL] + halves[1][:, tail + TAIL : tail + 2 * TAIL],
            ],
            axis=1,
        )
        low.append(dot_nt(eye, value.astype(BF16)))
    low = jnp.concatenate(low, axis=0).astype(BF16)

    spot = (window + (iota((1, 256), 1) & 31)) & (BOXES - 1)
    masks = (0o444, 0o222, 0o111)
    based = [spot | (-1 - mask) for mask in masks]

    def build(index, carry):
        for part in range(2):
            pair = 2 * index + part
            shifts = shift_ref[pair]
            nbr = shifts[3:4]
            for dim in range(3):
                nbr = nbr | ((based[dim] + shifts[dim : dim + 1]) & masks[dim])
            pick = onehot(box == nbr)
            found = dot_nn(low, pick)
            upper = jnp.concatenate([found[0:COEF, 0:128], found[COEF:, 0:128]], axis=1)
            lower = jnp.concatenate([found[0:COEF, 128:256], found[COEF:, 128:256]], axis=1)
            both = jnp.concatenate([upper, lower], axis=0).astype(BF16)
            src_ref[pl.ds(pl.multiple_of(128 + pair * 304, 16), 304)] = both
        return carry

    lax.fori_loop(0, CLASS // 4, build, 0)

    acc_ref[...] = jnp.zeros_like(acc_ref)

    def mult(index, carry):
        for r in range(4):
            lhs = []
            for m in range(4):
                chunk = 375 * r + 95 * m + index * 8
                lhs.append(
                    jnp.concatenate(
                        [wide_ref[pl.ds(chunk + q, GPAD, stride=CHUNKS), :] for q in range(8)],
                        axis=1,
                    )
                )
            begin = pl.multiple_of(128 - 32 * r + index * 1024, 32)
            acc_ref[r] += dot_nn(
                jnp.concatenate(lhs, axis=0).astype(BF16), src_ref[pl.ds(begin, 1024)]
            )
        return carry

    lax.fori_loop(0, 12, mult, 0)
    block = (iota((1, 256), 1) >> 5) & 3
    for r in range(4):
        value = None
        for m in range(4):
            term = jnp.where(block == m, acc_ref[r, GPAD * m : GPAD * m + GROUPS], 0.0)
            value = term if value is None else value + term
        for half in range(2):
            lanes = slice(128 * half, 128 * half + 128)
            check_ref[half, pl.ds(r, GROUPS, stride=4), :] = value[:, lanes]
    lane = iota((64, 256), 1)
    fold = onehot(((lane & 31) == (row64 & 31)) & ((lane >> 7) == (row64 >> 5)))
    hi, mid, rest = split3(jnp.concatenate([check_ref[0], check_ref[1]], axis=1))
    checks = dot_nt(fold, hi) + dot_nt(fold, mid) + dot_nt(fold, rest)
    local = nt3(checks, single_ref.at[1]) + fall
    leaves = [nt3(local, down_ref.at[o]) for o in range(8)]
    found = []
    for dens in range(2):
        value = jnp.concatenate([leaf[WIN * dens : WIN * dens + WIN] for leaf in leaves], axis=0)
        for piece in split2(value * FACTOR):
            found.append(dot_nt(eye, piece))
    leaf_mat_ref[...] = jnp.concatenate(found, axis=0).astype(BF16)

    def spread_out(index, carry):
        cols = pl.ds(pl.multiple_of(index * CHUNK, CHUNK), CHUNK)
        start = index * (CHUNK // 128)
        pick = onehot(iota((256, CHUNK), 0) == code_ref[:, cols])
        kernel = green_ref[:, cols]
        found = dot_nn(leaf_mat_ref[...], pick)
        for dens in range(2):
            base = 2 * COEF * dens
            value = found[base : base + COEF] + found[base + COEF : base + 2 * COEF]
            line = jnp.sum(kernel * value, axis=0, keepdims=True)
            for q in range(CHUNK // 128):
                pot_ref[dens, pl.ds(start + q, 1), :] = line[:, 128 * q : 128 * q + 128]
        return carry

    lax.fori_loop(0, COLS // CHUNK, spread_out, 0)
    even, odd = mix(pot_ref[0], pot_ref[1])
    tmp_ref[pl.ds(0, 64, stride=2), :] = even
    tmp_ref[pl.ds(1, 64, stride=2), :] = odd
    reply_ref[...] = tmp_ref[...].reshape(DEVS, 1, 128)
    replies = trade(me, reply_ref, back_ref, (reply_sems.at[0], reply_sems.at[1]))
    replies.wait_recv()
    tmp_ref[...] = back_ref[...].reshape(DEVS, 128)
    for column in range(TOP):
        tiles = mix(
            tmp_ref[pl.ds(column, 16, stride=8), :],
            tmp_ref[pl.ds(TOP + column, 16, stride=8), :],
        )
        for dens in range(2):
            rows_ref[pl.ds(2 * column + dens, 16, stride=8), :] = tiles[dens]
    value = jnp.concatenate([rows_ref[8 * j : 8 * j + 8] for j in range(16)], axis=1)
    hi = value.astype(BF16).astype(F32)
    mid = (value - hi).astype(BF16).astype(F32)
    pieces = jnp.concatenate([hi, mid, value - hi - mid], axis=0).astype(BF16)
    total = None
    for block in range(8):
        pick = onehot(iota((256, PTS), 0) + 256 * block == position)
        term = dot_nn(pieces[:, 256 * block : 256 * block + 256], pick)
        total = term if total is None else total + term
    out_ref[...] = total[0:8] + total[8:16] + total[16:24]

    points.wait_send()
    copy(own, near, 0, partner).wait_send()
    for step in range(1, 16):
        copy(own, far, step, partner).wait_send()
        copy(other(step, -1, core), near, step, partner).wait_send()
    told.wait_send()
    replies.wait_send()


def per_device(
    local_pos, densities, morton_slot, slot_leaf, uc2e, m2m, m2l_ops, dc2e, lattice, l2l
):
    vmem, sem = pltpu.VMEM, pltpu.SemaphoreType.DMA
    return pl.pallas_call(
        fmm_kernel,
        out_shape=jax.ShapeDtypeStruct((8, PTS), F32),
        in_specs=[pl.BlockSpec(memory_space=pl.ANY)] * 12,
        out_specs=pl.BlockSpec(memory_space=VM),
        scratch_shapes=[
            vmem((3, PTS), F32),
            vmem((8, PTS), F32),
            vmem((1, PTS), jnp.int32),
            vmem((8, 128), jnp.int32),
            vmem((1444, 128), F32),
            vmem((1444, 128), F32),
            vmem((COEF, COEF), F32),
            vmem((COEF, COEF), F32),
            vmem((COEF, COEF), F32),
            vmem((COEF, 8), F32),
            vmem((CLASS // 2, 4, 256), jnp.int32),
            sem((11,)),
            vmem((16, PTS), F32),
            vmem((DEVS, 3, 128), F32),
            vmem((DEVS, 3, 128), F32),
            vmem((TOP, 8, 128), jnp.int32),
            vmem((1216, 128), F32),
            vmem((1216, 128), F32),
            vmem((8, 2, COEF, COEF), BF16),
            vmem((8, 2, COEF, COEF), BF16),
            vmem((3, 2, COEF, COEF), BF16),
            vmem((DEPTH, PIECE, 128), BF16),
            vmem((WIDE, 128), F32),
            sem((DEPTH,)),
            vmem((6, 64, 128), F32),
            vmem((1, COLS), jnp.int32),
            vmem((COEF, COLS), F32),
            vmem((4 * COEF, 256), F32),
            vmem((8, 2, WIN, COEF), F32),
            vmem((2 * WIN, 256), F32),
            vmem((128, 128), F32),
            vmem((OWNERS, 80, 128), BF16),
            vmem((OWNERS, 4, 128), F32),
            vmem((BROWS + 384, 256), BF16),
            vmem((4, 4 * GPAD, 256), F32),
            vmem((2, COEF, 128), F32),
            vmem((4 * COEF, 256), BF16),
            vmem((2, 64, 128), F32),
            vmem((128, 128), F32),
            vmem((DEVS, 1, 128), F32),
            vmem((DEVS, 1, 128), F32),
            sem((2,)),
            sem((TOP,)),
            sem((TOP,)),
            sem((16,)),
            sem((16,)),
            sem((16,)),
            sem((16,)),
            sem((2,)),
            sem((2,)),
        ],
        compiler_params=pltpu.CompilerParams(
            vmem_limit_bytes=62 * 1024 * 1024, collective_id=0, has_side_effects=True
        ),
        name="fmm",
    )(
        local_pos,
        densities,
        morton_slot.reshape(1, PTS),
        slot_leaf.reshape(8, 128),
        m2m.reshape(1444, 128),
        l2l.reshape(1444, 128),
        uc2e,
        dc2e,
        lattice,
        surface_columns(),
        shift_rows(),
        m2l_ops.reshape(GROUPS * CHUNKS, 128),
    )


def solution(mesh):
    placed = (
        P(None, ("pts", "top")),
        P(None, ("pts", "top")),
        P(("pts", "top")),
        P(("pts", "top")),
        P(),
        P(),
        P(),
        P(),
        P(),
        P(),
    )
    return jax.shard_map(
        per_device, mesh=mesh, in_specs=placed, out_specs=P(None, ("pts", "top")), check_vma=False
    )
```

```python
import functools
import math

import jax
import jax.numpy as jnp
import numpy as np
from jax import lax
from jax.experimental import pallas as pl
from jax.experimental.pallas import tpu as pltpu
from jax.sharding import PartitionSpec as P

LEVEL = 3
EDGE = 6
COEF = 152
OFFSETS = 316
PTS = 1024
OWN = 4096
CAP = 64
OWNERS = 32
TOP = 4
DEVS = 128
COLS = DEVS * CAP
BOXES = 512
WIN = 32
GROUPS = 38
CHUNKS = 1501
GPAD = 40
WIDE = 60048
PIECE = 1440
PIECES = 40
DEPTH = 5
TAIL = COEF - 128
CLASS = 80
BROWS = CLASS * COEF
CHUNK = 1024

F32 = jnp.float32
BF16 = jnp.bfloat16
VM = pltpu.MemorySpace.VMEM
MESH = pl.DeviceIdType.MESH


def surface_table():
    grid_vals = np.linspace(-1.0, 1.0, EDGE)
    points_list = []
    for a in range(EDGE):
        for b in range(EDGE):
            for c in range(EDGE):
                if min(a, b, c) == 0 or max(a, b, c) == EDGE - 1:
                    points_list.append([grid_vals[a], grid_vals[b], grid_vals[c]])
    return np.array(points_list, dtype=np.float32).T


def surface_picks():
    table = np.zeros((COEF, 80), np.float32)
    steps = np.rint((surface_table().T + 1.0) * (EDGE - 1) / 2.0).astype(int)
    for piece in range(3):
        for dim in range(3):
            table[np.arange(COEF), 24 * piece + 8 * dim + steps[:, dim]] = 1.0
    return jnp.asarray(table).astype(BF16)


def edge_values():
    table = np.zeros((8, 128), np.float32)
    table[:EDGE] = (np.float32(1.25) * np.linspace(-1.0, 1.0, EDGE).astype(np.float32))[:, None]
    return jnp.asarray(table)


def offset_table():
    points_list = []
    for dx in range(-3, 4):
        for dy in range(-3, 4):
            for dz in range(-3, 4):
                if max(abs(dx), abs(dy), abs(dz)) >= 2:
                    points_list.append([dx, dy, dz])
    return np.array(points_list, dtype=np.int32)


def dilate(value):
    return sum(((value >> bit) & 1) << (3 * bit) for bit in range(LEVEL))


def shift_rows():
    rows = np.zeros((CLASS // 2, 4, 256), np.int32)
    table = offset_table()
    lane = np.arange(256)
    for pair in range(CLASS // 2):
        offset = CLASS * ((lane >> 5) & 3) + 2 * pair + (lane >> 7)
        known = offset < OFFSETS
        steps = table[np.minimum(offset, OFFSETS - 1)] % 8
        for dim in range(3):
            rows[pair, dim] = [dilate(int(v)) << (2 - dim) for v in steps[:, dim]]
        rows[pair, 3] = np.where(known, 0, -1)
    return jnp.asarray(rows)


def split2(x):
    hi = x.astype(BF16)
    lo = (x - hi.astype(F32)).astype(BF16)
    return hi, lo


def split3(x):
    hi = x.astype(BF16)
    rest = x - hi.astype(F32)
    mid = rest.astype(BF16)
    lo = (rest - mid.astype(F32)).astype(BF16)
    return hi, mid, lo


def dot_nn(a, b):
    return lax.dot_general(a, b, (((1,), (0,)), ((), ())), preferred_element_type=F32)


def dot_nt(a, b):
    return lax.dot_general(a, b, (((1,), (1,)), ((), ())), preferred_element_type=F32)


def nt3(x, w):
    rows = x.shape[0]
    xh, xl = split2(x)
    both = dot_nt(jnp.concatenate([xh, xl], axis=0), w[0])
    return both[:rows] + both[rows:] + dot_nt(xh, w[1])


def iota(shape, dim):
    return lax.broadcasted_iota(jnp.int32, shape, dim)


def onehot(mask):
    return jnp.where(mask, 1.0, 0.0).astype(BF16)


def equal(left, right):
    shape = jnp.broadcast_shapes(left.shape, right.shape)
    same = jnp.broadcast_to(left, shape) == jnp.broadcast_to(right, shape)
    return jnp.where(same, jnp.bfloat16(1), jnp.bfloat16(0))


def rows_equal(count, line, shift=0):
    line = (line - shift).astype(jnp.int16)
    return equal(iota((count, line.shape[1]), 0).astype(jnp.int16), line)


def matrices(flat_ref, main_ref, tail_ref):
    lane = iota((76, 128), 1)
    for r in range(16):
        chunk, shift = divmod(COEF * r, 128)
        count = 3 if shift + COEF > 256 else 2
        turned = []
        for c in range(count):
            value = flat_ref[pl.ds(chunk + c, 76, stride=19), :]
            turned.append(pltpu.roll(value, 128 - shift, 1) if shift else value)
        keep = lane < 128 - shift
        main = jnp.where(keep, turned[0], turned[1])
        tail = jnp.where(keep, turned[1], turned[2]) if count == 3 else turned[1]
        main_ref[pl.ds(r, 76, stride=16), :] = main
        tail_ref[pl.ds(r, 76, stride=16), :] = tail


def matrix(main_ref, tail_ref, octant):
    rows = slice(COEF * octant, COEF * octant + COEF)
    return jnp.concatenate([main_ref[rows], tail_ref[rows, 0:TAIL]], axis=1)


def mix(first, second):
    left = iota(first.shape, 1) % 128 < CAP
    even = jnp.where(left, first, pltpu.roll(second, CAP, 1))
    odd = jnp.where(left, pltpu.roll(first, CAP, 1), second)
    return even, odd


def every_peer(own, top, act):
    tops = [lax.rem(top + step, TOP) for step in range(TOP)]
    for step in range(1, TOP):
        act(own, tops[step])

    def body(step, carry):
        place = lax.rem(own + step, OWNERS)
        for column in tops:
            act(place, column)
        return carry

    lax.fori_loop(1, OWNERS, body, 0)


def trade(own, top, source_ref, target_ref, sems):
    me = TOP * own + top

    def push(place, column):
        pltpu.make_async_remote_copy(
            src_ref=source_ref.at[TOP * place + column],
            dst_ref=target_ref.at[me],
            send_sem=sems.at[0],
            recv_sem=sems.at[1],
            device_id={"pts": place, "top": column},
            device_id_type=MESH,
        ).start()

    every_peer(own, top, push)
    target_ref[me] = source_ref[me]
    return pltpu.make_async_remote_copy(
        src_ref=source_ref.at[pl.ds(0, DEVS - 1)],
        dst_ref=target_ref.at[pl.ds(0, DEVS - 1)],
        send_sem=sems.at[0],
        recv_sem=sems.at[1],
        device_id={"pts": lax.rem(own + 1, OWNERS), "top": top},
        device_id_type=MESH,
    )


def row_of(tab_ref, index, start):
    rows = [tab_ref[index, pl.ds(start + q, 1), :] for q in range(CHUNK // 128)]
    return jnp.concatenate(rows, axis=1)


def green(tab_ref, edge_ref, surf_ref, start):
    squares = []
    for dim in range(3):
        gap = edge_ref[:, 0:1] - row_of(tab_ref, dim, start)
        squares.append(gap * gap)
    squares = jnp.concatenate(squares, axis=0)
    hi = squares.astype(BF16).astype(F32)
    rest = squares - hi
    mid = rest.astype(BF16).astype(F32)
    pieces = jnp.concatenate([hi, mid, rest - mid, jnp.zeros((8, CHUNK), F32)], axis=0)
    return lax.rsqrt(dot_nn(surf_ref[...], pieces.astype(BF16)))


FACTOR = 1.0 / (4.0 * math.pi)


def fmm_kernel(
    pos_hbm,
    dens_hbm,
    slot_hbm,
    leaf_hbm,
    m2m_hbm,
    l2l_hbm,
    uc2e_hbm,
    dc2e_hbm,
    lattice_hbm,
    edge_hbm,
    surf_hbm,
    shift_hbm,
    flat_hbm,
    out_ref,
    pos_ref,
    dens_ref,
    slot_ref,
    leaf_ref,
    m2m_ref,
    l2l_ref,
    uc2e_ref,
    dc2e_ref,
    lattice_ref,
    edge_ref,
    surf_ref,
    shift_ref,
    in_sem,
    spots_ref,
    picks_ref,
    load_ref,
    send_ref,
    recv_ref,
    leaves_ref,
    main_ref,
    tail_ref,
    up_ref,
    down_ref,
    single_ref,
    stage_ref,
    wide_ref,
    stage_sem,
    tab_ref,
    green_ref,
    sums_ref,
    order_ref,
    pad_ref,
    tmp_ref,
    gath_ref,
    roots_ref,
    src_ref,
    acc_ref,
    check_ref,
    box_ref,
    low_ref,
    fall_ref,
    leaf_mat_ref,
    pot_ref,
    rows_ref,
    reply_ref,
    back_ref,
    points_sems,
    push_sem,
    pull_sem,
    send_sem,
    recv_sem,
    pass_sem,
    take_sem,
    root_sems,
    reply_sems,
):
    own = lax.axis_index("pts")
    top = lax.axis_index("top")
    x, y, core = own // 8, (own // 2) % 4, own % 2
    partner = own + 1 - 2 * core

    def other(step, sign, side):
        across = lax.rem(x + sign * (step // 4) + 4, 4)
        along = lax.rem(y + sign * (step % 4) + 4, 4)
        return across * 8 + along * 2 + side

    moves = [
        (pos_hbm, pos_ref),
        (dens_hbm, dens_ref),
        (slot_hbm, slot_ref),
        (leaf_hbm, leaf_ref),
        (m2m_hbm, m2m_ref),
        (l2l_hbm, l2l_ref),
        (uc2e_hbm, uc2e_ref),
        (dc2e_hbm, dc2e_ref),
        (lattice_hbm, lattice_ref),
        (edge_hbm, edge_ref),
        (surf_hbm, surf_ref),
        (shift_hbm, shift_ref),
    ]
    loads = [
        pltpu.make_async_copy(source, target, in_sem.at[index])
        for index, (source, target) in enumerate(moves)
    ]
    for load in loads:
        load.start()

    def fetch(index, size):
        return pltpu.make_async_copy(
            flat_hbm.at[pl.ds(index * PIECE, size)],
            stage_ref.at[index % DEPTH, pl.ds(0, size)],
            stage_sem.at[index % DEPTH],
        )

    last = GROUPS * CHUNKS - (PIECES - 1) * PIECE
    for index in range(DEPTH):
        fetch(index, PIECE).start()
    barrier = pltpu.get_barrier_semaphore()

    def greet(place, column):
        pl.semaphore_signal(
            barrier, inc=1, device_id={"pts": place, "top": column}, device_id_type=MESH
        )

    every_peer(own, top, greet)

    for load in loads[:4]:
        load.wait()
    slot = slot_ref[...]
    owner = slot >> 12
    member = jnp.where(iota((OWNERS, PTS), 0) == owner, 1.0, 0.0)
    before = onehot(iota((PTS, PTS), 0) < iota((PTS, PTS), 1))
    prefix = dot_nn(member.astype(BF16), before)
    rank = jnp.sum(member * prefix, axis=0, keepdims=True)
    position = owner * CAP + rank.astype(jnp.int32)
    load_ref[...] = jnp.zeros_like(load_ref)
    load_ref[0:1] = pos_ref[0:1]
    load_ref[1:2] = pos_ref[2:3]
    load_ref[8:9] = pos_ref[1:2]
    load_ref[9:10] = ((slot & (OWN - 1)) + 1).astype(F32)
    for pair in range(4):
        load_ref[2 + pair : 3 + pair] = dens_ref[2 * pair : 2 * pair + 1]
        load_ref[10 + pair : 11 + pair] = dens_ref[2 * pair + 1 : 2 * pair + 2]
    payload = jnp.concatenate(split3(load_ref[...]), axis=0)
    for block in range(8):
        pick = rows_equal(256, position, 256 * block)
        spots_ref[256 * block : 256 * block + 256] = pick
        res = dot_nt(payload, pick)
        value = res[0:16] + res[16:32] + res[32:48]
        for pair in range(2):
            lanes = slice(128 * pair, 128 * pair + 128)
            tiles = mix(value[0:8, lanes], value[8:16, lanes])
            for part, tile in enumerate(tiles):
                target = 4 * block + 2 * pair + part
                for column in range(TOP):
                    send_ref[TOP * target + column, 0:2, :] = tile[0:2]
                    send_ref[TOP * target + column, 2:3, :] = tile[2 + column : 3 + column]
    pl.semaphore_wait(barrier, DEVS - 1)
    points = trade(own, top, send_ref, recv_ref, points_sems)

    def share(step, place):
        return pltpu.make_async_remote_copy(
            src_ref=leaf_ref,
            dst_ref=leaves_ref.at[place],
            send_sem=push_sem.at[step],
            recv_sem=pull_sem.at[step],
            device_id={"top": lax.rem(top + step, TOP)},
            device_id_type=MESH,
        )

    for step in range(1, TOP):
        share(step, top).start()
    leaves_ref[top] = leaf_ref[...]

    for load in loads[4:]:
        load.wait()

    def prepare(flat_ref, split_ref):
        matrices(flat_ref, main_ref, tail_ref)
        for octant in range(8):
            hi, lo = split2(matrix(main_ref, tail_ref, octant))
            split_ref[octant, 0] = hi
            split_ref[octant, 1] = lo

    prepare(m2m_ref, up_ref)
    for index, ref in enumerate((uc2e_ref, dc2e_ref, lattice_ref)):
        hi, lo = split2(ref[...])
        single_ref[index, 0] = hi
        single_ref[index, 1] = lo
    wide_ref[PIECES * PIECE : WIDE] = jnp.zeros((WIDE - PIECES * PIECE, 128), F32)
    src_ref[0:128] = jnp.zeros((128, 256), BF16)
    src_ref[128 + BROWS : 384 + BROWS] = jnp.zeros((256, 256), BF16)

    def widen(index, carry):
        @pl.when(index < PIECES - 1)
        def _():
            fetch(index, PIECE).wait()

        @pl.when(index == PIECES - 1)
        def _():
            fetch(index, last).wait()

        wide_ref[pl.ds(pl.multiple_of(index * PIECE, 32), PIECE)] = stage_ref[
            index % DEPTH
        ].astype(F32)

        @pl.when(index + DEPTH < PIECES - 1)
        def _():
            fetch(index + DEPTH, PIECE).start()

        @pl.when(index + DEPTH == PIECES - 1)
        def _():
            fetch(index + DEPTH, last).start()

        return carry

    lax.fori_loop(0, PIECES, widen, 0)
    sums_ref[...] = jnp.zeros_like(sums_ref)
    pad_ref[...] = jnp.zeros_like(pad_ref)

    for step in range(1, TOP):
        share(step, lax.rem(top + TOP - step, TOP)).wait_recv()
        share(step, top).wait_send()
    points.wait_recv()

    for pair in range(3):
        tmp_ref[...] = recv_ref[:, pair, :]
        tiles = mix(tmp_ref[pl.ds(0, 64, stride=2), :], tmp_ref[pl.ds(1, 64, stride=2), :])
        tab_ref[2 * pair] = tiles[0]
        tab_ref[2 * pair + 1] = tiles[1]
    window = leaves_ref[0, 0:1, 0:1] >> 3
    table = (leaves_ref[...].reshape(32, 128) - 8 * window).astype(F32).astype(BF16)
    row = iota((BOXES, 128), 0)
    box_ref[...] = ((row & 7) << 6) + (row & 56) + (row >> 6)

    def gather(index, carry):
        cols = pl.ds(pl.multiple_of(index * CHUNK, CHUNK), CHUNK)
        start = index * (CHUNK // 128)
        place = row_of(tab_ref, 3, start).astype(jnp.int32) - 1
        rows = dot_nn(table, onehot(iota((128, CHUNK), 0) == (place & 127)))
        leaf = jnp.sum(
            jnp.where(iota((32, CHUNK), 0) == (place >> 7), rows, 0.0), axis=0, keepdims=True
        ).astype(jnp.int32)
        code = (leaf & 7) * WIN + (leaf >> 3)
        pick = rows_equal(256, code)
        picks_ref[:, cols] = pick
        kernel = green(tab_ref, edge_ref, surf_ref, start)
        green_ref[:, cols] = kernel
        weighted = []
        for dens in range(2):
            value = kernel * (row_of(tab_ref, 4 + dens, start) * FACTOR)
            high = value.astype(BF16).astype(F32)
            weighted += [high, value - high]
        sums_ref[...] += dot_nt(jnp.concatenate(weighted, axis=0).astype(BF16), pick)
        return carry

    lax.fori_loop(0, COLS // CHUNK, gather, 0)
    eye = onehot(iota((256, 256), 0) == iota((256, 256), 1))
    for dens in range(2):
        base = 2 * COEF * dens
        total = sums_ref[base : base + COEF] + sums_ref[base + COEF : base + 2 * COEF]
        hi, mid, rest = split3(total)
        turned = dot_nt(eye, hi) + dot_nt(eye, mid) + dot_nt(eye, rest)
        order_ref[:, dens] = turned.reshape(8, WIN, COEF)
    leaf_mult = nt3(order_ref[...].reshape(2 * 256, COEF), single_ref.at[0])
    part = nt3(leaf_mult[0:64], up_ref.at[0])
    for octant in range(1, 8):
        part = part + nt3(leaf_mult[64 * octant : 64 * octant + 64], up_ref.at[octant])
    pad_ref[:, 0:COEF] = part
    lane = iota((16, 128), 1)
    tail = jnp.where(
        lane == 96,
        (window >> 3).astype(F32),
        jnp.where(lane == 97, (window & 7).astype(F32), 0.0),
    )
    for group in range(4):
        piece = pad_ref[16 * group : 16 * group + 16, 128:256]
        tail = tail + (pltpu.roll(piece, TAIL * group, 1) if group else piece)
    gath_ref[own, 0:64] = pad_ref[:, 0:128].astype(BF16)
    gath_ref[own, 64:80] = tail.astype(BF16)

    def copy(place, sems, index, target):
        return pltpu.make_async_remote_copy(
            src_ref=gath_ref.at[place],
            dst_ref=gath_ref.at[place],
            send_sem=sems[0].at[index],
            recv_sem=sems[1].at[index],
            device_id={"pts": target},
            device_id_type=MESH,
        )

    far = (send_sem, recv_sem)
    near = (pass_sem, take_sem)
    copy(own, near, 0, partner).start()
    for step in range(1, 16):
        copy(own, far, step, other(step, 1, core)).start()

    row64 = iota((64, 1), 0)
    target = (window + (row64 & 31)) & (BOXES - 1)
    digits = [target & 7, (target >> 3) & 7, target >> 6]
    rise = part.astype(BF16).astype(F32)
    for digit in digits:
        total = None
        for o in range(8):
            term = nt3(jnp.where(digit == o, rise, 0.0), up_ref.at[o])
            total = term if total is None else total + term
        rise = total
    pad_ref[:, 0:COEF] = rise
    for dens in range(2):
        total = jnp.sum(pad_ref[WIN * dens : WIN * dens + WIN], axis=0, keepdims=True)
        roots_ref[own, dens : dens + 1, :] = total[:, 0:128]
        roots_ref[own, 2 + dens : 3 + dens, :] = total[:, 128:256]

    def tell(step, carry):
        pltpu.make_async_remote_copy(
            src_ref=roots_ref.at[own],
            dst_ref=roots_ref.at[own],
            send_sem=root_sems.at[0],
            recv_sem=root_sems.at[1],
            device_id={"pts": lax.rem(own + step, OWNERS)},
            device_id_type=MESH,
        ).start()
        return carry

    lax.fori_loop(1, OWNERS, tell, 0)
    prepare(l2l_ref, down_ref)
    for step in range(1, 16):
        place = other(step, -1, core)
        copy(place, far, step, partner).wait_recv()
        copy(place, near, step, partner).start()
    told = pltpu.make_async_remote_copy(
        src_ref=roots_ref.at[pl.ds(0, OWNERS - 1)],
        dst_ref=roots_ref.at[pl.ds(0, OWNERS - 1)],
        send_sem=root_sems.at[0],
        recv_sem=root_sems.at[1],
        device_id={"pts": partner},
        device_id_type=MESH,
    )
    told.wait_recv()
    root = jnp.sum(roots_ref[...], axis=0)
    root = jnp.concatenate([root[0:2], root[2:4, 0:TAIL]], axis=1)
    fall = jnp.where(row64 < WIN, root[0:1], root[1:2])
    fall = nt3(fall, single_ref.at[2])
    for digit in digits[::-1]:
        total = None
        for o in range(8):
            term = nt3(jnp.where(digit == o, fall, 0.0), down_ref.at[o])
            total = term if total is None else total + term
        fall = total
    copy(partner, near, 0, partner).wait_recv()
    for step in range(1, 16):
        copy(other(step, -1, 1 - core), near, step, partner).wait_recv()

    eye = onehot(iota((COEF, COEF), 0) == iota((COEF, COEF), 1))
    codes = gath_ref[:, 64, :].astype(F32)
    lane = iota((OWNERS, 128), 1)
    first = jnp.sum(
        jnp.where(lane == 96, 8.0 * codes, jnp.where(lane == 97, codes, 0.0)),
        axis=1,
        keepdims=True,
    )
    spread = jnp.where(iota((OWNERS, 512), 0) == (iota((OWNERS, 512), 1) >> 4), first, 0.0)
    start = jnp.sum(spread, axis=0, keepdims=True).astype(jnp.int32)
    start = start + (iota((1, 512), 1) & 15)

    def boxes(width):
        return jnp.concatenate([box_ref[...]] * (width // 128), axis=1)

    halves = []
    for half in range(2):
        place = onehot(boxes(512) == start + 16 * half)
        pieces = [
            gath_ref[:, 32 * dens + 16 * half : 32 * dens + 16 * half + 16, :].reshape(512, 128)
            for dens in range(2)
        ]
        pieces.append(gath_ref[:, 64:80, :].reshape(512, 128))
        halves.append(dot_nn(place, jnp.concatenate(pieces, axis=1)))
    low = []
    for dens in range(2):
        main = slice(128 * dens, 128 * dens + 128)
        tail = 256 + 2 * TAIL * dens
        value = jnp.concatenate(
            [
                halves[0][:, main] + halves[1][:, main],
                halves[0][:, tail : tail + TAIL] + halves[1][:, tail + TAIL : tail + 2 * TAIL],
            ],
            axis=1,
        )
        low.append(dot_nt(eye, value.astype(BF16)))
    low_ref[...] = jnp.concatenate(low, axis=0).astype(BF16)
    fall_ref[...] = fall

    spot = (window + (iota((1, 256), 1) & 31)) & (BOXES - 1)
    masks = (0o444, 0o222, 0o111)
    based = [spot | (-1 - mask) for mask in masks]

    def build(index, carry):
        lines = []
        for part in range(2):
            shifts = shift_ref[2 * index + part]
            nbr = shifts[3:4]
            for dim in range(3):
                nbr = nbr | ((based[dim] + shifts[dim : dim + 1]) & masks[dim])
            lines.append(nbr)
        pick = onehot(boxes(512) == jnp.concatenate(lines, axis=1))
        found = dot_nn(low_ref[...], pick)
        tiles = []
        for part in range(4):
            lanes = slice(128 * part, 128 * part + 128)
            tiles.append(jnp.concatenate([found[0:COEF, lanes], found[COEF:, lanes]], axis=1))
        both = jnp.concatenate(tiles, axis=0).astype(BF16)
        src_ref[pl.ds(pl.multiple_of(128 + index * 608, 16), 608)] = both
        return carry

    lax.fori_loop(0, CLASS // 4, build, 0)

    acc_ref[...] = jnp.zeros_like(acc_ref)

    def mult(index, carry):
        for r in range(4):
            lhs = []
            for m in range(4):
                chunk = 375 * r + 95 * m + index * 8
                lhs.append(
                    jnp.concatenate(
                        [wide_ref[pl.ds(chunk + q, GPAD, stride=CHUNKS), :] for q in range(8)],
                        axis=1,
                    )
                )
            begin = pl.multiple_of(128 - 32 * r + index * 1024, 32)
            acc_ref[r] += dot_nn(
                jnp.concatenate(lhs, axis=0).astype(BF16), src_ref[pl.ds(begin, 1024)]
            )
        return carry

    lax.fori_loop(0, 12, mult, 0)
    block = (iota((1, 256), 1) >> 5) & 3
    for r in range(4):
        value = None
        for m in range(4):
            term = jnp.where(block == m, acc_ref[r, GPAD * m : GPAD * m + GROUPS], 0.0)
            value = term if value is None else value + term
        for half in range(2):
            lanes = slice(128 * half, 128 * half + 128)
            check_ref[half, pl.ds(r, GROUPS, stride=4), :] = value[:, lanes]
    lane = iota((64, 256), 1)
    row64 = iota((64, 1), 0)
    eye = onehot(iota((COEF, COEF), 0) == iota((COEF, COEF), 1))
    fold = onehot(((lane & 31) == (row64 & 31)) & ((lane >> 7) == (row64 >> 5)))
    hi, mid, rest = split3(jnp.concatenate([check_ref[0], check_ref[1]], axis=1))
    checks = dot_nt(fold, hi) + dot_nt(fold, mid) + dot_nt(fold, rest)
    local = nt3(checks, single_ref.at[1]) + fall_ref[...]
    leaves = [nt3(local, down_ref.at[o]) for o in range(8)]
    found = []
    for dens in range(2):
        value = jnp.concatenate([leaf[WIN * dens : WIN * dens + WIN] for leaf in leaves], axis=0)
        found.append(dot_nt(eye, (value * FACTOR).astype(BF16)))
    leaf_mat_ref[...] = jnp.concatenate(found, axis=0).astype(BF16)

    def spread_out(index, carry):
        cols = pl.ds(pl.multiple_of(index * CHUNK, CHUNK), CHUNK)
        start = index * (CHUNK // 128)
        pick = picks_ref[:, cols]
        kernel = green_ref[:, cols]
        found = dot_nn(leaf_mat_ref[...], pick)
        for dens in range(2):
            value = found[COEF * dens : COEF * dens + COEF]
            line = jnp.sum(kernel * value, axis=0, keepdims=True)
            for q in range(CHUNK // 128):
                pot_ref[dens, pl.ds(start + q, 1), :] = line[:, 128 * q : 128 * q + 128]
        return carry

    lax.fori_loop(0, COLS // CHUNK, spread_out, 0)
    even, odd = mix(pot_ref[0], pot_ref[1])
    tmp_ref[pl.ds(0, 64, stride=2), :] = even
    tmp_ref[pl.ds(1, 64, stride=2), :] = odd
    reply_ref[...] = tmp_ref[...].reshape(DEVS, 1, 128)
    replies = trade(own, top, reply_ref, back_ref, reply_sems)
    replies.wait_recv()
    tmp_ref[...] = back_ref[...].reshape(DEVS, 128)
    for column in range(TOP):
        tiles = mix(
            tmp_ref[pl.ds(column, 16, stride=8), :],
            tmp_ref[pl.ds(TOP + column, 16, stride=8), :],
        )
        for dens in range(2):
            rows_ref[pl.ds(2 * column + dens, 16, stride=8), :] = tiles[dens]
    value = jnp.concatenate([rows_ref[8 * j : 8 * j + 8] for j in range(16)], axis=1)
    hi = value.astype(BF16).astype(F32)
    mid = (value - hi).astype(BF16).astype(F32)
    pieces = jnp.concatenate([hi, mid, value - hi - mid], axis=0).astype(BF16)
    total = None
    for block in range(8):
        pick = spots_ref[256 * block : 256 * block + 256]
        term = dot_nn(pieces[:, 256 * block : 256 * block + 256], pick)
        total = term if total is None else total + term
    out_ref[...] = total

    points.wait_send()
    copy(own, near, 0, partner).wait_send()
    for step in range(1, 16):
        copy(own, far, step, partner).wait_send()
        copy(other(step, -1, core), near, step, partner).wait_send()
    told.wait_send()
    replies.wait_send()


def per_device(
    local_pos, densities, morton_slot, slot_leaf, uc2e, m2m, m2l_ops, dc2e, lattice, l2l
):
    vmem, sem = pltpu.VMEM, pltpu.SemaphoreType.DMA
    pieces = pl.pallas_call(
        fmm_kernel,
        out_shape=jax.ShapeDtypeStruct((24, PTS), F32),
        in_specs=[pl.BlockSpec(memory_space=pl.ANY)] * 13,
        out_specs=pl.BlockSpec(memory_space=VM),
        scratch_shapes=[
            vmem((3, PTS), F32),
            vmem((8, PTS), F32),
            vmem((1, PTS), jnp.int32),
            vmem((8, 128), jnp.int32),
            vmem((1444, 128), F32),
            vmem((1444, 128), F32),
            vmem((COEF, COEF), F32),
            vmem((COEF, COEF), F32),
            vmem((COEF, COEF), F32),
            vmem((8, 128), F32),
            vmem((COEF, 80), BF16),
            vmem((CLASS // 2, 4, 256), jnp.int32),
            sem((12,)),
            vmem((OWNERS * CAP, PTS), BF16),
            vmem((256, COLS), BF16),
            vmem((16, PTS), F32),
            vmem((DEVS, 3, 128), F32),
            vmem((DEVS, 3, 128), F32),
            vmem((TOP, 8, 128), jnp.int32),
            vmem((1216, 128), F32),
            vmem((1216, 128), F32),
            vmem((8, 2, COEF, COEF), BF16),
            vmem((8, 2, COEF, COEF), BF16),
            vmem((3, 2, COEF, COEF), BF16),
            vmem((DEPTH, PIECE, 128), BF16),
            vmem((WIDE, 128), F32),
            sem((DEPTH,)),
            vmem((6, 64, 128), F32),
            vmem((COEF, COLS), F32),
            vmem((4 * COEF, 256), F32),
            vmem((8, 2, WIN, COEF), F32),
            vmem((2 * WIN, 256), F32),
            vmem((128, 128), F32),
            vmem((OWNERS, 80, 128), BF16),
            vmem((OWNERS, 4, 128), F32),
            vmem((BROWS + 384, 256), BF16),
            vmem((4, 4 * GPAD, 256), F32),
            vmem((2, COEF, 128), F32),
            vmem((BOXES, 128), jnp.int32),
            vmem((2 * COEF, BOXES), BF16),
            vmem((2 * WIN, COEF), F32),
            vmem((2 * COEF, 256), BF16),
            vmem((2, 64, 128), F32),
            vmem((128, 128), F32),
            vmem((DEVS, 1, 128), F32),
            vmem((DEVS, 1, 128), F32),
            sem((2,)),
            sem((TOP,)),
            sem((TOP,)),
            sem((16,)),
            sem((16,)),
            sem((16,)),
            sem((16,)),
            sem((2,)),
            sem((2,)),
        ],
        compiler_params=pltpu.CompilerParams(
            vmem_limit_bytes=67_000_000, collective_id=0, has_side_effects=True
        ),
        name="fmm",
    )(
        local_pos,
        densities,
        morton_slot.reshape(1, PTS),
        slot_leaf.reshape(8, 128),
        m2m.reshape(1444, 128),
        l2l.reshape(1444, 128),
        uc2e,
        dc2e,
        lattice,
        edge_values(),
        surface_picks(),
        shift_rows(),
        m2l_ops.reshape(GROUPS * CHUNKS, 128),
    )
    return pieces[0:8] + pieces[8:16] + pieces[16:24]


def solution(mesh):
    placed = (
        P(None, ("pts", "top")),
        P(None, ("pts", "top")),
        P(("pts", "top")),
        P(("pts", "top")),
        P(),
        P(),
        P(),
        P(),
        P(),
        P(),
    )
    return jax.shard_map(
        per_device, mesh=mesh, in_specs=placed, out_specs=P(None, ("pts", "top")), check_vma=False
    )
```

```python
import functools
import math

import jax
import jax.numpy as jnp
import numpy as np
from jax import lax
from jax.experimental import pallas as pl
from jax.experimental.pallas import tpu as pltpu
from jax.sharding import PartitionSpec as P

LEVEL = 3
EDGE = 6
COEF = 152
OFFSETS = 316
PTS = 1024
OWN = 4096
CAP = 64
OWNERS = 32
TOP = 4
DEVS = 128
COLS = DEVS * CAP
BOXES = 512
WIN = 32
GROUPS = 38
CHUNKS = 1501
GPAD = 40
WIDE = 60048
PIECE = 1440
PIECES = 40
DEPTH = 5
TAIL = COEF - 128
CLASS = 80
BROWS = CLASS * COEF
CHUNK = 1024

F32 = jnp.float32
BF16 = jnp.bfloat16
VM = pltpu.MemorySpace.VMEM
MESH = pl.DeviceIdType.MESH


def surface_table():
    grid_vals = np.linspace(-1.0, 1.0, EDGE)
    points_list = []
    for a in range(EDGE):
        for b in range(EDGE):
            for c in range(EDGE):
                if min(a, b, c) == 0 or max(a, b, c) == EDGE - 1:
                    points_list.append([grid_vals[a], grid_vals[b], grid_vals[c]])
    return np.array(points_list, dtype=np.float32).T


def surface_picks():
    table = np.zeros((COEF, 80), np.float32)
    steps = np.rint((surface_table().T + 1.0) * (EDGE - 1) / 2.0).astype(int)
    for piece in range(3):
        for dim in range(3):
            table[np.arange(COEF), 24 * piece + 8 * dim + steps[:, dim]] = 1.0
    return jnp.asarray(table).astype(BF16)


def edge_values():
    table = np.zeros((8, 128), np.float32)
    table[:EDGE] = (np.float32(1.25) * np.linspace(-1.0, 1.0, EDGE).astype(np.float32))[:, None]
    return jnp.asarray(table)


def offset_table():
    points_list = []
    for dx in range(-3, 4):
        for dy in range(-3, 4):
            for dz in range(-3, 4):
                if max(abs(dx), abs(dy), abs(dz)) >= 2:
                    points_list.append([dx, dy, dz])
    return np.array(points_list, dtype=np.int32)


def dilate(value):
    return sum(((value >> bit) & 1) << (3 * bit) for bit in range(LEVEL))


def shift_rows():
    rows = np.zeros((CLASS // 2, 4, 256), np.int32)
    table = offset_table()
    lane = np.arange(256)
    for pair in range(CLASS // 2):
        offset = CLASS * ((lane >> 5) & 3) + 2 * pair + (lane >> 7)
        known = offset < OFFSETS
        steps = table[np.minimum(offset, OFFSETS - 1)] % 8
        for dim in range(3):
            rows[pair, dim] = [dilate(int(v)) << (2 - dim) for v in steps[:, dim]]
        rows[pair, 3] = np.where(known, 0, -1)
    return jnp.asarray(rows)


def split2(x):
    hi = x.astype(BF16)
    lo = (x - hi.astype(F32)).astype(BF16)
    return hi, lo


def split3(x):
    hi = x.astype(BF16)
    rest = x - hi.astype(F32)
    mid = rest.astype(BF16)
    lo = (rest - mid.astype(F32)).astype(BF16)
    return hi, mid, lo


def dot_nn(a, b):
    return lax.dot_general(a, b, (((1,), (0,)), ((), ())), preferred_element_type=F32)


def dot_nt(a, b):
    return lax.dot_general(a, b, (((1,), (1,)), ((), ())), preferred_element_type=F32)


def nt3(x, w):
    rows = x.shape[0]
    xh, xl = split2(x)
    both = dot_nt(jnp.concatenate([xh, xl], axis=0), w[0])
    return both[:rows] + both[rows:] + dot_nt(xh, w[1])


def iota(shape, dim):
    return lax.broadcasted_iota(jnp.int32, shape, dim)


def onehot(mask):
    return jnp.where(mask, 1.0, 0.0).astype(BF16)


def equal(left, right):
    shape = jnp.broadcast_shapes(left.shape, right.shape)
    same = jnp.broadcast_to(left, shape) == jnp.broadcast_to(right, shape)
    return jnp.where(same, jnp.bfloat16(1), jnp.bfloat16(0))


def rows_equal(count, line, shift=0):
    line = (line - shift).astype(jnp.int16)
    return equal(iota((count, line.shape[1]), 0).astype(jnp.int16), line)


def matrices(flat_ref, main_ref, tail_ref):
    lane = iota((76, 128), 1)
    for r in range(16):
        chunk, shift = divmod(COEF * r, 128)
        count = 3 if shift + COEF > 256 else 2
        turned = []
        for c in range(count):
            value = flat_ref[pl.ds(chunk + c, 76, stride=19), :]
            turned.append(pltpu.roll(value, 128 - shift, 1) if shift else value)
        keep = lane < 128 - shift
        main = jnp.where(keep, turned[0], turned[1])
        tail = jnp.where(keep, turned[1], turned[2]) if count == 3 else turned[1]
        main_ref[pl.ds(r, 76, stride=16), :] = main
        tail_ref[pl.ds(r, 76, stride=16), :] = tail


def matrix(main_ref, tail_ref, octant):
    rows = slice(COEF * octant, COEF * octant + COEF)
    return jnp.concatenate([main_ref[rows], tail_ref[rows, 0:TAIL]], axis=1)


def mix(first, second):
    left = iota(first.shape, 1) % 128 < CAP
    even = jnp.where(left, first, pltpu.roll(second, CAP, 1))
    odd = jnp.where(left, pltpu.roll(first, CAP, 1), second)
    return even, odd


def every_peer(own, top, act):
    tops = [lax.rem(top + step, TOP) for step in range(TOP)]
    for step in range(1, TOP):
        act(own, tops[step])

    def body(step, carry):
        place = lax.rem(own + step, OWNERS)
        for column in tops:
            act(place, column)
        return carry

    lax.fori_loop(1, OWNERS, body, 0)


def trade(own, top, source_ref, target_ref, send_sem, recv_sem):
    me = TOP * own + top

    def push(place, column):
        pltpu.make_async_remote_copy(
            src_ref=source_ref.at[TOP * place + column],
            dst_ref=target_ref.at[me],
            send_sem=send_sem,
            recv_sem=recv_sem,
            device_id={"pts": place, "top": column},
            device_id_type=MESH,
        ).start()

    every_peer(own, top, push)
    target_ref[me] = source_ref[me]
    return pltpu.make_async_remote_copy(
        src_ref=source_ref.at[pl.ds(0, DEVS - 1)],
        dst_ref=target_ref.at[pl.ds(0, DEVS - 1)],
        send_sem=send_sem,
        recv_sem=recv_sem,
        device_id={"pts": lax.rem(own + 1, OWNERS), "top": top},
        device_id_type=MESH,
    )


def row_of(tab_ref, index, start):
    rows = [tab_ref[index, pl.ds(start + q, 1), :] for q in range(CHUNK // 128)]
    return jnp.concatenate(rows, axis=1)


def green(tab_ref, edge_ref, surf_ref, start):
    squares = []
    for dim in range(3):
        gap = edge_ref[:, 0:1] - row_of(tab_ref, dim, start)
        squares.append(gap * gap)
    squares = jnp.concatenate(squares, axis=0)
    hi = squares.astype(BF16).astype(F32)
    rest = squares - hi
    mid = rest.astype(BF16).astype(F32)
    pieces = jnp.concatenate([hi, mid, rest - mid, jnp.zeros((8, CHUNK), F32)], axis=0)
    return lax.rsqrt(dot_nn(surf_ref[...], pieces.astype(BF16)))


FACTOR = 1.0 / (4.0 * math.pi)


def fmm_kernel(
    pos_hbm,
    dens_hbm,
    slot_hbm,
    leaf_hbm,
    m2m_hbm,
    l2l_hbm,
    uc2e_hbm,
    dc2e_hbm,
    lattice_hbm,
    edge_hbm,
    surf_hbm,
    shift_hbm,
    flat_hbm,
    out_ref,
    pos_ref,
    dens_ref,
    slot_ref,
    leaf_ref,
    m2m_ref,
    l2l_ref,
    uc2e_ref,
    dc2e_ref,
    lattice_ref,
    edge_ref,
    surf_ref,
    shift_ref,
    in_sem,
    where_ref,
    picks_ref,
    load_ref,
    send_ref,
    recv_ref,
    leaves_ref,
    main_ref,
    tail_ref,
    up_ref,
    down_ref,
    single_ref,
    stage_ref,
    wide_ref,
    stage_sem,
    tab_ref,
    batch_ref,
    green_ref,
    sums_ref,
    order_ref,
    pad_ref,
    tmp_ref,
    gath_ref,
    roots_ref,
    src_ref,
    acc_ref,
    check_ref,
    box_ref,
    low_ref,
    fall_ref,
    leaf_mat_ref,
    pot_ref,
    rows_ref,
    reply_ref,
    back_ref,
    points_sem,
    group_sems,
    push_sem,
    pull_sem,
    send_sem,
    recv_sem,
    pass_sem,
    take_sem,
    root_sems,
    reply_sems,
):
    own = lax.axis_index("pts")
    top = lax.axis_index("top")
    x, y, core = own // 8, (own // 2) % 4, own % 2
    partner = own + 1 - 2 * core

    def other(step, sign, side):
        across = lax.rem(x + sign * (step // 4) + 4, 4)
        along = lax.rem(y + sign * (step % 4) + 4, 4)
        return across * 8 + along * 2 + side

    barrier = pltpu.get_barrier_semaphore()

    def greet(place, column):
        pl.semaphore_signal(
            barrier, inc=1, device_id={"pts": place, "top": column}, device_id_type=MESH
        )

    every_peer(own, top, greet)

    moves = [
        (pos_hbm, pos_ref),
        (dens_hbm, dens_ref),
        (slot_hbm, slot_ref),
        (leaf_hbm, leaf_ref),
        (m2m_hbm, m2m_ref),
        (l2l_hbm, l2l_ref),
        (uc2e_hbm, uc2e_ref),
        (dc2e_hbm, dc2e_ref),
        (lattice_hbm, lattice_ref),
        (edge_hbm, edge_ref),
        (surf_hbm, surf_ref),
        (shift_hbm, shift_ref),
    ]
    loads = [
        pltpu.make_async_copy(source, target, in_sem.at[index])
        for index, (source, target) in enumerate(moves)
    ]
    for load in loads:
        load.start()

    def fetch(index, size):
        return pltpu.make_async_copy(
            flat_hbm.at[pl.ds(index * PIECE, size)],
            stage_ref.at[index % DEPTH, pl.ds(0, size)],
            stage_sem.at[index % DEPTH],
        )

    last = GROUPS * CHUNKS - (PIECES - 1) * PIECE
    for index in range(DEPTH):
        fetch(index, PIECE).start()

    for load in loads[:4]:
        load.wait()
    slot = slot_ref[...]
    owner = slot >> 12
    member = jnp.where(iota((OWNERS, PTS), 0) == owner, 1.0, 0.0)
    before = onehot(iota((PTS, PTS), 0) < iota((PTS, PTS), 1))
    prefix = dot_nn(member.astype(BF16), before)
    rank = jnp.sum(member * prefix, axis=0, keepdims=True)
    position = owner * CAP + rank.astype(jnp.int32)
    where_ref[...] = position
    load_ref[...] = jnp.zeros_like(load_ref)
    load_ref[0:1] = pos_ref[0:1]
    load_ref[1:2] = pos_ref[2:3]
    load_ref[8:9] = pos_ref[1:2]
    load_ref[9:10] = ((slot & (OWN - 1)) + 1).astype(F32)
    for pair in range(4):
        load_ref[2 + pair : 3 + pair] = dens_ref[2 * pair : 2 * pair + 1]
        load_ref[10 + pair : 11 + pair] = dens_ref[2 * pair + 1 : 2 * pair + 2]
    payload = jnp.concatenate(split3(load_ref[...]), axis=0)
    for block in range(8):
        pick = rows_equal(256, position, 256 * block)
        res = dot_nt(payload, pick)
        value = res[0:16] + res[16:32] + res[32:48]
        for pair in range(2):
            lanes = slice(128 * pair, 128 * pair + 128)
            tiles = mix(value[0:8, lanes], value[8:16, lanes])
            for part, tile in enumerate(tiles):
                target = 4 * block + 2 * pair + part
                for column in range(TOP):
                    send_ref[TOP * target + column, 0:2, :] = tile[0:2]
                    send_ref[TOP * target + column, 2:3, :] = tile[2 + column : 3 + column]
    pl.semaphore_wait(barrier, DEVS - 1)
    points = trade(
        own, top, send_ref, recv_ref, points_sem, group_sems.at[own // 4]
    )

    def share(step, place):
        return pltpu.make_async_remote_copy(
            src_ref=leaf_ref,
            dst_ref=leaves_ref.at[place],
            send_sem=push_sem.at[step],
            recv_sem=pull_sem.at[step],
            device_id={"top": lax.rem(top + step, TOP)},
            device_id_type=MESH,
        )

    for step in range(1, TOP):
        share(step, top).start()
    leaves_ref[top] = leaf_ref[...]

    for load in loads[4:]:
        load.wait()

    def prepare(flat_ref, split_ref):
        matrices(flat_ref, main_ref, tail_ref)
        for octant in range(8):
            hi, lo = split2(matrix(main_ref, tail_ref, octant))
            split_ref[octant, 0] = hi
            split_ref[octant, 1] = lo

    prepare(m2m_ref, up_ref)
    for index, ref in enumerate((uc2e_ref, dc2e_ref, lattice_ref)):
        hi, lo = split2(ref[...])
        single_ref[index, 0] = hi
        single_ref[index, 1] = lo
    wide_ref[PIECES * PIECE : WIDE] = jnp.zeros((WIDE - PIECES * PIECE, 128), F32)
    src_ref[0:128] = jnp.zeros((128, 256), BF16)
    src_ref[128 + BROWS : 384 + BROWS] = jnp.zeros((256, 256), BF16)

    def widen(index, carry):
        @pl.when(index < PIECES - 1)
        def _():
            fetch(index, PIECE).wait()

        @pl.when(index == PIECES - 1)
        def _():
            fetch(index, last).wait()

        wide_ref[pl.ds(pl.multiple_of(index * PIECE, 32), PIECE)] = stage_ref[
            index % DEPTH
        ].astype(F32)

        @pl.when(index + DEPTH < PIECES - 1)
        def _():
            fetch(index + DEPTH, PIECE).start()

        @pl.when(index + DEPTH == PIECES - 1)
        def _():
            fetch(index + DEPTH, last).start()

        return carry

    sums_ref[...] = jnp.zeros_like(sums_ref)
    pad_ref[...] = jnp.zeros_like(pad_ref)

    for step in range(1, TOP):
        share(step, lax.rem(top + TOP - step, TOP)).wait_recv()
        share(step, top).wait_send()
    window = leaves_ref[0, 0:1, 0:1] >> 3
    table = (leaves_ref[...].reshape(32, 128) - 8 * window).astype(F32).astype(BF16)
    row = iota((BOXES, 128), 0)
    box_ref[...] = ((row & 7) << 6) + (row & 56) + (row >> 6)

    def arrived(group, count):
        pltpu.make_async_remote_copy(
            src_ref=send_ref.at[pl.ds(0, count)],
            dst_ref=recv_ref.at[pl.ds(0, count)],
            send_sem=points_sem,
            recv_sem=group_sems.at[group],
            device_id={"pts": partner, "top": top},
            device_id_type=MESH,
        ).wait_recv()

    def gather(step, carry):
        lax.fori_loop(5 * step, 5 * step + 5, widen, 0)
        far_half = step // 2
        across = lax.rem(x + far_half + far_half // 2 - 2 * (far_half // 3), 4)
        index = 2 * across + lax.rem(y // 2 + step, 2)

        @pl.when(step == 0)
        def _():
            arrived(index, 15)

        @pl.when(step > 0)
        def _():
            arrived(index, 16)

        cols = pl.ds(pl.multiple_of(index * CHUNK, CHUNK), CHUNK)
        start = index * (CHUNK // 128)
        for pair in range(3):
            batch_ref[...] = recv_ref[pl.ds(16 * index, 16), pair, :]
            tiles = mix(batch_ref[pl.ds(0, 8, stride=2), :], batch_ref[pl.ds(1, 8, stride=2), :])
            rows = pl.ds(pl.multiple_of(8 * index, 8), 8)
            tab_ref[2 * pair, rows] = tiles[0]
            tab_ref[2 * pair + 1, rows] = tiles[1]
        place = row_of(tab_ref, 3, start).astype(jnp.int32) - 1
        rows = dot_nn(table, onehot(iota((128, CHUNK), 0) == (place & 127)))
        leaf = jnp.sum(
            jnp.where(iota((32, CHUNK), 0) == (place >> 7), rows, 0.0), axis=0, keepdims=True
        ).astype(jnp.int32)
        code = (leaf & 7) * WIN + (leaf >> 3)
        pick = rows_equal(256, code)
        picks_ref[:, cols] = pick
        kernel = green(tab_ref, edge_ref, surf_ref, start)
        green_ref[:, cols] = kernel
        weighted = []
        for dens in range(2):
            value = kernel * (row_of(tab_ref, 4 + dens, start) * FACTOR)
            high = value.astype(BF16).astype(F32)
            weighted += [high, value - high]
        sums_ref[...] += dot_nt(jnp.concatenate(weighted, axis=0).astype(BF16), pick)
        return carry

    lax.fori_loop(0, COLS // CHUNK, gather, 0)
    eye = onehot(iota((256, 256), 0) == iota((256, 256), 1))
    for dens in range(2):
        base = 2 * COEF * dens
        total = sums_ref[base : base + COEF] + sums_ref[base + COEF : base + 2 * COEF]
        hi, mid, rest = split3(total)
        turned = dot_nt(eye, hi) + dot_nt(eye, mid) + dot_nt(eye, rest)
        order_ref[:, dens] = turned.reshape(8, WIN, COEF)
    leaf_mult = nt3(order_ref[...].reshape(2 * 256, COEF), single_ref.at[0])
    part = nt3(leaf_mult[0:64], up_ref.at[0])
    for octant in range(1, 8):
        part = part + nt3(leaf_mult[64 * octant : 64 * octant + 64], up_ref.at[octant])
    pad_ref[:, 0:COEF] = part
    lane = iota((16, 128), 1)
    tail = jnp.where(
        lane == 96,
        (window >> 3).astype(F32),
        jnp.where(lane == 97, (window & 7).astype(F32), 0.0),
    )
    for group in range(4):
        piece = pad_ref[16 * group : 16 * group + 16, 128:256]
        tail = tail + (pltpu.roll(piece, TAIL * group, 1) if group else piece)
    gath_ref[own, 0:64] = pad_ref[:, 0:128].astype(BF16)
    gath_ref[own, 64:80] = tail.astype(BF16)

    def copy(place, sems, index, target):
        return pltpu.make_async_remote_copy(
            src_ref=gath_ref.at[place],
            dst_ref=gath_ref.at[place],
            send_sem=sems[0].at[index],
            recv_sem=sems[1].at[index],
            device_id={"pts": target},
            device_id_type=MESH,
        )

    far = (send_sem, recv_sem)
    near = (pass_sem, take_sem)
    copy(own, near, 0, partner).start()
    for step in range(1, 16):
        copy(own, far, step, other(step, 1, core)).start()

    row64 = iota((64, 1), 0)
    target = (window + (row64 & 31)) & (BOXES - 1)
    digits = [target & 7, (target >> 3) & 7, target >> 6]
    rise = part.astype(BF16).astype(F32)
    for digit in digits:
        total = None
        for o in range(8):
            term = nt3(jnp.where(digit == o, rise, 0.0), up_ref.at[o])
            total = term if total is None else total + term
        rise = total
    pad_ref[:, 0:COEF] = rise
    for dens in range(2):
        total = jnp.sum(pad_ref[WIN * dens : WIN * dens + WIN], axis=0, keepdims=True)
        roots_ref[own, dens : dens + 1, :] = total[:, 0:128]
        roots_ref[own, 2 + dens : 3 + dens, :] = total[:, 128:256]

    def tell(step, carry):
        pltpu.make_async_remote_copy(
            src_ref=roots_ref.at[own],
            dst_ref=roots_ref.at[own],
            send_sem=root_sems.at[0],
            recv_sem=root_sems.at[1],
            device_id={"pts": lax.rem(own + step, OWNERS)},
            device_id_type=MESH,
        ).start()
        return carry

    lax.fori_loop(1, OWNERS, tell, 0)
    prepare(l2l_ref, down_ref)
    for step in range(1, 16):
        place = other(step, -1, core)
        copy(place, far, step, partner).wait_recv()
        copy(place, near, step, partner).start()
    told = pltpu.make_async_remote_copy(
        src_ref=roots_ref.at[pl.ds(0, OWNERS - 1)],
        dst_ref=roots_ref.at[pl.ds(0, OWNERS - 1)],
        send_sem=root_sems.at[0],
        recv_sem=root_sems.at[1],
        device_id={"pts": partner},
        device_id_type=MESH,
    )
    told.wait_recv()
    root = jnp.sum(roots_ref[...], axis=0)
    root = jnp.concatenate([root[0:2], root[2:4, 0:TAIL]], axis=1)
    fall = jnp.where(row64 < WIN, root[0:1], root[1:2])
    fall = nt3(fall, single_ref.at[2])
    for digit in digits[::-1]:
        total = None
        for o in range(8):
            term = nt3(jnp.where(digit == o, fall, 0.0), down_ref.at[o])
            total = term if total is None else total + term
        fall = total
    copy(partner, near, 0, partner).wait_recv()
    for step in range(1, 16):
        copy(other(step, -1, 1 - core), near, step, partner).wait_recv()

    eye = onehot(iota((COEF, COEF), 0) == iota((COEF, COEF), 1))
    codes = gath_ref[:, 64, :].astype(F32)
    lane = iota((OWNERS, 128), 1)
    first = jnp.sum(
        jnp.where(lane == 96, 8.0 * codes, jnp.where(lane == 97, codes, 0.0)),
        axis=1,
        keepdims=True,
    )
    spread = jnp.where(iota((OWNERS, 512), 0) == (iota((OWNERS, 512), 1) >> 4), first, 0.0)
    start = jnp.sum(spread, axis=0, keepdims=True).astype(jnp.int32)
    start = start + (iota((1, 512), 1) & 15)

    def boxes(width):
        return jnp.concatenate([box_ref[...]] * (width // 128), axis=1)

    halves = []
    for half in range(2):
        place = onehot(boxes(512) == start + 16 * half)
        pieces = [
            gath_ref[:, 32 * dens + 16 * half : 32 * dens + 16 * half + 16, :].reshape(512, 128)
            for dens in range(2)
        ]
        pieces.append(gath_ref[:, 64:80, :].reshape(512, 128))
        halves.append(dot_nn(place, jnp.concatenate(pieces, axis=1)))
    low = []
    for dens in range(2):
        main = slice(128 * dens, 128 * dens + 128)
        tail = 256 + 2 * TAIL * dens
        value = jnp.concatenate(
            [
                halves[0][:, main] + halves[1][:, main],
                halves[0][:, tail : tail + TAIL] + halves[1][:, tail + TAIL : tail + 2 * TAIL],
            ],
            axis=1,
        )
        low.append(dot_nt(eye, value.astype(BF16)))
    low_ref[...] = jnp.concatenate(low, axis=0).astype(BF16)
    fall_ref[...] = fall

    spot = (window + (iota((1, 256), 1) & 31)) & (BOXES - 1)
    masks = (0o444, 0o222, 0o111)
    based = [spot | (-1 - mask) for mask in masks]

    def build(index, carry):
        lines = []
        for part in range(2):
            shifts = shift_ref[2 * index + part]
            nbr = shifts[3:4]
            for dim in range(3):
                nbr = nbr | ((based[dim] + shifts[dim : dim + 1]) & masks[dim])
            lines.append(nbr)
        pick = onehot(boxes(512) == jnp.concatenate(lines, axis=1))
        found = dot_nn(low_ref[...], pick)
        tiles = []
        for part in range(4):
            lanes = slice(128 * part, 128 * part + 128)
            tiles.append(jnp.concatenate([found[0:COEF, lanes], found[COEF:, lanes]], axis=1))
        both = jnp.concatenate(tiles, axis=0).astype(BF16)
        src_ref[pl.ds(pl.multiple_of(128 + index * 608, 16), 608)] = both
        return carry

    lax.fori_loop(0, CLASS // 4, build, 0)

    acc_ref[...] = jnp.zeros_like(acc_ref)

    def mult(index, carry):
        for r in range(4):
            lhs = []
            for m in range(4):
                chunk = 375 * r + 95 * m + index * 8
                lhs.append(
                    jnp.concatenate(
                        [wide_ref[pl.ds(chunk + q, GPAD, stride=CHUNKS), :] for q in range(8)],
                        axis=1,
                    )
                )
            begin = pl.multiple_of(128 - 32 * r + index * 1024, 32)
            acc_ref[r] += dot_nn(
                jnp.concatenate(lhs, axis=0).astype(BF16), src_ref[pl.ds(begin, 1024)]
            )
        return carry

    lax.fori_loop(0, 12, mult, 0)
    block = (iota((1, 256), 1) >> 5) & 3
    for r in range(4):
        value = None
        for m in range(4):
            term = jnp.where(block == m, acc_ref[r, GPAD * m : GPAD * m + GROUPS], 0.0)
            value = term if value is None else value + term
        for half in range(2):
            lanes = slice(128 * half, 128 * half + 128)
            check_ref[half, pl.ds(r, GROUPS, stride=4), :] = value[:, lanes]
    lane = iota((64, 256), 1)
    row64 = iota((64, 1), 0)
    eye = onehot(iota((COEF, COEF), 0) == iota((COEF, COEF), 1))
    fold = onehot(((lane & 31) == (row64 & 31)) & ((lane >> 7) == (row64 >> 5)))
    hi, mid, rest = split3(jnp.concatenate([check_ref[0], check_ref[1]], axis=1))
    checks = dot_nt(fold, hi) + dot_nt(fold, mid) + dot_nt(fold, rest)
    local = nt3(checks, single_ref.at[1]) + fall_ref[...]
    leaves = [nt3(local, down_ref.at[o]) for o in range(8)]
    found = []
    for dens in range(2):
        value = jnp.concatenate([leaf[WIN * dens : WIN * dens + WIN] for leaf in leaves], axis=0)
        found.append(dot_nt(eye, (value * FACTOR).astype(BF16)))
    leaf_mat_ref[...] = jnp.concatenate(found, axis=0).astype(BF16)

    def spread_out(index, carry):
        cols = pl.ds(pl.multiple_of(index * CHUNK, CHUNK), CHUNK)
        start = index * (CHUNK // 128)
        pick = picks_ref[:, cols]
        kernel = green_ref[:, cols]
        found = dot_nn(leaf_mat_ref[...], pick)
        for dens in range(2):
            value = found[COEF * dens : COEF * dens + COEF]
            line = jnp.sum(kernel * value, axis=0, keepdims=True)
            for q in range(CHUNK // 128):
                pot_ref[dens, pl.ds(start + q, 1), :] = line[:, 128 * q : 128 * q + 128]
        return carry

    lax.fori_loop(0, COLS // CHUNK, spread_out, 0)
    even, odd = mix(pot_ref[0], pot_ref[1])
    tmp_ref[pl.ds(0, 64, stride=2), :] = even
    tmp_ref[pl.ds(1, 64, stride=2), :] = odd
    reply_ref[...] = tmp_ref[...].reshape(DEVS, 1, 128)
    replies = trade(own, top, reply_ref, back_ref, reply_sems.at[0], reply_sems.at[1])
    points.wait_send()
    copy(own, near, 0, partner).wait_send()
    for step in range(1, 16):
        copy(own, far, step, partner).wait_send()
        copy(other(step, -1, core), near, step, partner).wait_send()
    told.wait_send()
    replies.wait_recv()
    tmp_ref[...] = back_ref[...].reshape(DEVS, 128)
    for column in range(TOP):
        tiles = mix(
            tmp_ref[pl.ds(column, 16, stride=8), :],
            tmp_ref[pl.ds(TOP + column, 16, stride=8), :],
        )
        for dens in range(2):
            rows_ref[pl.ds(2 * column + dens, 16, stride=8), :] = tiles[dens]
    value = jnp.concatenate([rows_ref[8 * j : 8 * j + 8] for j in range(16)], axis=1)
    hi = value.astype(BF16).astype(F32)
    mid = (value - hi).astype(BF16).astype(F32)
    pieces = jnp.concatenate([hi, mid, value - hi - mid], axis=0).astype(BF16)
    total = None
    for block in range(8):
        pick = rows_equal(256, where_ref[...], 256 * block)
        term = dot_nn(pieces[:, 256 * block : 256 * block + 256], pick)
        total = term if total is None else total + term
    out_ref[...] = total

    replies.wait_send()


def per_device(
    local_pos, densities, morton_slot, slot_leaf, uc2e, m2m, m2l_ops, dc2e, lattice, l2l
):
    vmem, sem = pltpu.VMEM, pltpu.SemaphoreType.DMA
    pieces = pl.pallas_call(
        fmm_kernel,
        out_shape=jax.ShapeDtypeStruct((24, PTS), F32),
        in_specs=[pl.BlockSpec(memory_space=pl.ANY)] * 13,
        out_specs=pl.BlockSpec(memory_space=VM),
        scratch_shapes=[
            vmem((3, PTS), F32),
            vmem((8, PTS), F32),
            vmem((1, PTS), jnp.int32),
            vmem((8, 128), jnp.int32),
            vmem((1444, 128), F32),
            vmem((1444, 128), F32),
            vmem((COEF, COEF), F32),
            vmem((COEF, COEF), F32),
            vmem((COEF, COEF), F32),
            vmem((8, 128), F32),
            vmem((COEF, 80), BF16),
            vmem((CLASS // 2, 4, 256), jnp.int32),
            sem((12,)),
            vmem((1, PTS), jnp.int32),
            vmem((256, COLS), BF16),
            vmem((16, PTS), F32),
            vmem((DEVS, 3, 128), F32),
            vmem((DEVS, 3, 128), F32),
            vmem((TOP, 8, 128), jnp.int32),
            vmem((1216, 128), F32),
            vmem((1216, 128), F32),
            vmem((8, 2, COEF, COEF), BF16),
            vmem((8, 2, COEF, COEF), BF16),
            vmem((3, 2, COEF, COEF), BF16),
            vmem((DEPTH, PIECE, 128), BF16),
            vmem((WIDE, 128), F32),
            sem((DEPTH,)),
            vmem((6, 64, 128), F32),
            vmem((16, 128), F32),
            vmem((COEF, COLS), F32),
            vmem((4 * COEF, 256), F32),
            vmem((8, 2, WIN, COEF), F32),
            vmem((2 * WIN, 256), F32),
            vmem((128, 128), F32),
            vmem((OWNERS, 80, 128), BF16),
            vmem((OWNERS, 4, 128), F32),
            vmem((BROWS + 384, 256), BF16),
            vmem((4, 4 * GPAD, 256), F32),
            vmem((2, COEF, 128), F32),
            vmem((BOXES, 128), jnp.int32),
            vmem((2 * COEF, BOXES), BF16),
            vmem((2 * WIN, COEF), F32),
            vmem((2 * COEF, 256), BF16),
            vmem((2, 64, 128), F32),
            vmem((128, 128), F32),
            vmem((DEVS, 1, 128), F32),
            vmem((DEVS, 1, 128), F32),
            sem,
            sem((8,)),
            sem((TOP,)),
            sem((TOP,)),
            sem((16,)),
            sem((16,)),
            sem((16,)),
            sem((16,)),
            sem((2,)),
            sem((2,)),
        ],
        compiler_params=pltpu.CompilerParams(
            vmem_limit_bytes=67_000_000, collective_id=0, has_side_effects=True
        ),
        name="fmm",
    )(
        local_pos,
        densities,
        morton_slot.reshape(1, PTS),
        slot_leaf.reshape(8, 128),
        m2m.reshape(1444, 128),
        l2l.reshape(1444, 128),
        uc2e,
        dc2e,
        lattice,
        edge_values(),
        surface_picks(),
        shift_rows(),
        m2l_ops.reshape(GROUPS * CHUNKS, 128),
    )
    return pieces[0:8] + pieces[8:16] + pieces[16:24]


def solution(mesh):
    placed = (
        P(None, ("pts", "top")),
        P(None, ("pts", "top")),
        P(("pts", "top")),
        P(("pts", "top")),
        P(),
        P(),
        P(),
        P(),
        P(),
        P(),
    )
    return jax.shard_map(
        per_device, mesh=mesh, in_specs=placed, out_specs=P(None, ("pts", "top")), check_vma=False
    )
```

```python
import functools
import math

import jax
import jax.numpy as jnp
import numpy as np
from jax import lax
from jax.experimental import pallas as pl
from jax.experimental.pallas import tpu as pltpu
from jax.sharding import PartitionSpec as P

LEVEL = 3
EDGE = 6
COEF = 152
OFFSETS = 316
PTS = 1024
OWN = 4096
CAP = 64
OWNERS = 32
TOP = 4
DEVS = 128
COLS = DEVS * CAP
BOXES = 512
WIN = 32
GROUPS = 38
CHUNKS = 1501
GPAD = 40
WIDE = 60048
PIECE = 1440
PIECES = 40
DEPTH = 5
TAIL = COEF - 128
CLASS = 80
BROWS = CLASS * COEF
CHUNK = 1024

F32 = jnp.float32
BF16 = jnp.bfloat16
VM = pltpu.MemorySpace.VMEM
MESH = pl.DeviceIdType.MESH


def surface_table():
    grid_vals = np.linspace(-1.0, 1.0, EDGE)
    points_list = []
    for a in range(EDGE):
        for b in range(EDGE):
            for c in range(EDGE):
                if min(a, b, c) == 0 or max(a, b, c) == EDGE - 1:
                    points_list.append([grid_vals[a], grid_vals[b], grid_vals[c]])
    return np.array(points_list, dtype=np.float32).T


def surface_picks():
    table = np.zeros((COEF, 80), np.float32)
    steps = np.rint((surface_table().T + 1.0) * (EDGE - 1) / 2.0).astype(int)
    for piece in range(3):
        for dim in range(3):
            table[np.arange(COEF), 24 * piece + 8 * dim + steps[:, dim]] = 1.0
    return jnp.asarray(table).astype(BF16)


def edge_values():
    table = np.zeros((8, 128), np.float32)
    table[:EDGE] = (np.float32(1.25) * np.linspace(-1.0, 1.0, EDGE).astype(np.float32))[:, None]
    return jnp.asarray(table)


def offset_table():
    points_list = []
    for dx in range(-3, 4):
        for dy in range(-3, 4):
            for dz in range(-3, 4):
                if max(abs(dx), abs(dy), abs(dz)) >= 2:
                    points_list.append([dx, dy, dz])
    return np.array(points_list, dtype=np.int32)


def dilate(value):
    return sum(((value >> bit) & 1) << (3 * bit) for bit in range(LEVEL))


def shift_rows():
    rows = np.zeros((CLASS // 2, 4, 256), np.int32)
    table = offset_table()
    lane = np.arange(256)
    for pair in range(CLASS // 2):
        offset = CLASS * ((lane >> 5) & 3) + 2 * pair + (lane >> 7)
        known = offset < OFFSETS
        steps = table[np.minimum(offset, OFFSETS - 1)] % 8
        for dim in range(3):
            rows[pair, dim] = [dilate(int(v)) << (2 - dim) for v in steps[:, dim]]
        rows[pair, 3] = np.where(known, 0, -1)
    return jnp.asarray(rows)


def split2(x):
    hi = x.astype(BF16)
    lo = (x - hi.astype(F32)).astype(BF16)
    return hi, lo


def split3(x):
    hi = x.astype(BF16)
    rest = x - hi.astype(F32)
    mid = rest.astype(BF16)
    lo = (rest - mid.astype(F32)).astype(BF16)
    return hi, mid, lo


def dot_nn(a, b):
    return lax.dot_general(a, b, (((1,), (0,)), ((), ())), preferred_element_type=F32)


def dot_nt(a, b):
    return lax.dot_general(a, b, (((1,), (1,)), ((), ())), preferred_element_type=F32)


def nt3(x, w):
    rows = x.shape[0]
    xh, xl = split2(x)
    both = dot_nt(jnp.concatenate([xh, xl], axis=0), w[0])
    return both[:rows] + both[rows:] + dot_nt(xh, w[1])


def iota(shape, dim):
    return lax.broadcasted_iota(jnp.int32, shape, dim)


def onehot(mask):
    return jnp.where(mask, 1.0, 0.0).astype(BF16)


def equal(left, right):
    shape = jnp.broadcast_shapes(left.shape, right.shape)
    same = jnp.broadcast_to(left, shape) == jnp.broadcast_to(right, shape)
    return jnp.where(same, jnp.bfloat16(1), jnp.bfloat16(0))


def rows_equal(count, line, shift=0):
    line = (line - shift).astype(jnp.int16)
    return equal(iota((count, line.shape[1]), 0).astype(jnp.int16), line)


def matrices(flat_ref, main_ref, tail_ref):
    lane = iota((76, 128), 1)
    for r in range(16):
        chunk, shift = divmod(COEF * r, 128)
        count = 3 if shift + COEF > 256 else 2
        turned = []
        for c in range(count):
            value = flat_ref[pl.ds(chunk + c, 76, stride=19), :]
            turned.append(pltpu.roll(value, 128 - shift, 1) if shift else value)
        keep = lane < 128 - shift
        main = jnp.where(keep, turned[0], turned[1])
        tail = jnp.where(keep, turned[1], turned[2]) if count == 3 else turned[1]
        main_ref[pl.ds(r, 76, stride=16), :] = main
        tail_ref[pl.ds(r, 76, stride=16), :] = tail


def matrix(main_ref, tail_ref, octant):
    rows = slice(COEF * octant, COEF * octant + COEF)
    return jnp.concatenate([main_ref[rows], tail_ref[rows, 0:TAIL]], axis=1)


def mix(first, second):
    left = iota(first.shape, 1) % 128 < CAP
    even = jnp.where(left, first, pltpu.roll(second, CAP, 1))
    odd = jnp.where(left, pltpu.roll(first, CAP, 1), second)
    return even, odd


def every_peer(own, top, act):
    tops = [lax.rem(top + step, TOP) for step in range(TOP)]
    for step in range(1, TOP):
        act(own, tops[step])

    def body(step, carry):
        place = lax.rem(own + step, OWNERS)
        for column in tops:
            act(place, column)
        return carry

    lax.fori_loop(1, OWNERS, body, 0)


def trade(own, top, source_ref, target_ref, send_sem, recv_sem):
    me = TOP * own + top

    def push(place, column):
        pltpu.make_async_remote_copy(
            src_ref=source_ref.at[TOP * place + column],
            dst_ref=target_ref.at[me],
            send_sem=send_sem,
            recv_sem=recv_sem,
            device_id={"pts": place, "top": column},
            device_id_type=MESH,
        ).start()

    every_peer(own, top, push)
    target_ref[me] = source_ref[me]
    return pltpu.make_async_remote_copy(
        src_ref=source_ref.at[pl.ds(0, DEVS - 1)],
        dst_ref=target_ref.at[pl.ds(0, DEVS - 1)],
        send_sem=send_sem,
        recv_sem=recv_sem,
        device_id={"pts": lax.rem(own + 1, OWNERS), "top": top},
        device_id_type=MESH,
    )


def row_of(tab_ref, index, start):
    rows = [tab_ref[index, pl.ds(start + q, 1), :] for q in range(CHUNK // 128)]
    return jnp.concatenate(rows, axis=1)


def green(tab_ref, edge_ref, surf_ref, start):
    squares = []
    for dim in range(3):
        gap = edge_ref[:, 0:1] - row_of(tab_ref, dim, start)
        squares.append(gap * gap)
    squares = jnp.concatenate(squares, axis=0)
    hi = squares.astype(BF16).astype(F32)
    rest = squares - hi
    mid = rest.astype(BF16).astype(F32)
    pieces = jnp.concatenate([hi, mid, rest - mid, jnp.zeros((8, CHUNK), F32)], axis=0)
    return lax.rsqrt(dot_nn(surf_ref[...], pieces.astype(BF16)))


FACTOR = 1.0 / (4.0 * math.pi)


def fmm_kernel(
    pos_hbm,
    dens_hbm,
    slot_hbm,
    leaf_hbm,
    m2m_hbm,
    l2l_hbm,
    uc2e_hbm,
    dc2e_hbm,
    lattice_hbm,
    edge_hbm,
    surf_hbm,
    shift_hbm,
    flat_hbm,
    out_ref,
    pos_ref,
    dens_ref,
    slot_ref,
    leaf_ref,
    m2m_ref,
    l2l_ref,
    uc2e_ref,
    dc2e_ref,
    lattice_ref,
    edge_ref,
    surf_ref,
    shift_ref,
    in_sem,
    where_ref,
    picks_ref,
    load_ref,
    send_ref,
    recv_ref,
    leaves_ref,
    main_ref,
    tail_ref,
    up_ref,
    down_ref,
    single_ref,
    stage_ref,
    wide_ref,
    stage_sem,
    tab_ref,
    batch_ref,
    green_ref,
    sums_ref,
    order_ref,
    pad_ref,
    tmp_ref,
    gath_ref,
    roots_ref,
    src_ref,
    acc_ref,
    check_ref,
    box_ref,
    low_ref,
    fall_ref,
    leaf_mat_ref,
    pot_ref,
    rows_ref,
    reply_ref,
    back_ref,
    points_sem,
    group_sems,
    push_sem,
    pull_sem,
    send_sem,
    recv_sem,
    pass_sem,
    take_sem,
    root_sems,
    reply_sems,
):
    own = lax.axis_index("pts")
    top = lax.axis_index("top")
    x, y, core = own // 8, (own // 2) % 4, own % 2
    partner = own + 1 - 2 * core

    def other(step, sign, side):
        across = lax.rem(x + sign * (step // 4) + 4, 4)
        along = lax.rem(y + sign * (step % 4) + 4, 4)
        return across * 8 + along * 2 + side

    barrier = pltpu.get_barrier_semaphore()

    def greet(place, column):
        pl.semaphore_signal(
            barrier, inc=1, device_id={"pts": place, "top": column}, device_id_type=MESH
        )

    every_peer(own, top, greet)

    moves = [
        (pos_hbm, pos_ref),
        (dens_hbm, dens_ref),
        (slot_hbm, slot_ref),
        (leaf_hbm, leaf_ref),
        (m2m_hbm, m2m_ref),
        (l2l_hbm, l2l_ref),
        (uc2e_hbm, uc2e_ref),
        (dc2e_hbm, dc2e_ref),
        (lattice_hbm, lattice_ref),
        (edge_hbm, edge_ref),
        (surf_hbm, surf_ref),
        (shift_hbm, shift_ref),
    ]
    loads = [
        pltpu.make_async_copy(source, target, in_sem.at[index])
        for index, (source, target) in enumerate(moves)
    ]
    for load in loads:
        load.start()

    def fetch(index, size):
        return pltpu.make_async_copy(
            flat_hbm.at[pl.ds(index * PIECE, size)],
            stage_ref.at[index % DEPTH, pl.ds(0, size)],
            stage_sem.at[index % DEPTH],
        )

    last = GROUPS * CHUNKS - (PIECES - 1) * PIECE
    for index in range(DEPTH):
        fetch(index, PIECE).start()

    for load in loads[:4]:
        load.wait()
    slot = slot_ref[...]
    owner = slot >> 12
    member = jnp.where(iota((OWNERS, PTS), 0) == owner, 1.0, 0.0)
    before = onehot(iota((PTS, PTS), 0) < iota((PTS, PTS), 1))
    prefix = dot_nn(member.astype(BF16), before)
    rank = jnp.sum(member * prefix, axis=0, keepdims=True)
    position = owner * CAP + rank.astype(jnp.int32)
    where_ref[...] = position
    load_ref[...] = jnp.zeros_like(load_ref)
    load_ref[0:1] = pos_ref[0:1]
    load_ref[1:2] = pos_ref[2:3]
    load_ref[8:9] = pos_ref[1:2]
    load_ref[9:10] = ((slot & (OWN - 1)) + 1).astype(F32)
    for pair in range(4):
        load_ref[2 + pair : 3 + pair] = dens_ref[2 * pair : 2 * pair + 1]
        load_ref[10 + pair : 11 + pair] = dens_ref[2 * pair + 1 : 2 * pair + 2]
    payload = jnp.concatenate(split3(load_ref[...]), axis=0)
    for block in range(8):
        pick = rows_equal(256, position, 256 * block)
        res = dot_nt(payload, pick)
        value = res[0:16] + res[16:32] + res[32:48]
        for pair in range(2):
            lanes = slice(128 * pair, 128 * pair + 128)
            tiles = mix(value[0:8, lanes], value[8:16, lanes])
            for part, tile in enumerate(tiles):
                target = 4 * block + 2 * pair + part
                for column in range(TOP):
                    send_ref[TOP * target + column, 0:2, :] = tile[0:2]
                    send_ref[TOP * target + column, 2:3, :] = tile[2 + column : 3 + column]
    pl.semaphore_wait(barrier, DEVS - 1)
    points = trade(
        own, top, send_ref, recv_ref, points_sem, group_sems.at[own // 4]
    )

    def share(step, place):
        return pltpu.make_async_remote_copy(
            src_ref=leaf_ref,
            dst_ref=leaves_ref.at[place],
            send_sem=push_sem.at[step],
            recv_sem=pull_sem.at[step],
            device_id={"top": lax.rem(top + step, TOP)},
            device_id_type=MESH,
        )

    for step in range(1, TOP):
        share(step, top).start()
    leaves_ref[top] = leaf_ref[...]

    for load in loads[4:]:
        load.wait()

    def prepare(flat_ref, split_ref):
        matrices(flat_ref, main_ref, tail_ref)
        for octant in range(8):
            hi, lo = split2(matrix(main_ref, tail_ref, octant))
            split_ref[octant, 0] = hi
            split_ref[octant, 1] = lo

    prepare(m2m_ref, up_ref)
    for index, ref in enumerate((uc2e_ref, dc2e_ref, lattice_ref)):
        hi, lo = split2(ref[...])
        single_ref[index, 0] = hi
        single_ref[index, 1] = lo
    wide_ref[PIECES * PIECE : WIDE] = jnp.zeros((WIDE - PIECES * PIECE, 128), F32)
    src_ref[0:128] = jnp.zeros((128, 256), BF16)
    src_ref[128 + BROWS : 384 + BROWS] = jnp.zeros((256, 256), BF16)

    def widen(index, carry):
        @pl.when(index < PIECES - 1)
        def _():
            fetch(index, PIECE).wait()

        @pl.when(index == PIECES - 1)
        def _():
            fetch(index, last).wait()

        wide_ref[pl.ds(pl.multiple_of(index * PIECE, 32), PIECE)] = stage_ref[
            index % DEPTH
        ].astype(F32)

        @pl.when(index + DEPTH < PIECES - 1)
        def _():
            fetch(index + DEPTH, PIECE).start()

        @pl.when(index + DEPTH == PIECES - 1)
        def _():
            fetch(index + DEPTH, last).start()

        return carry

    sums_ref[...] = jnp.zeros_like(sums_ref)
    pad_ref[...] = jnp.zeros_like(pad_ref)

    for step in range(1, TOP):
        share(step, lax.rem(top + TOP - step, TOP)).wait_recv()
        share(step, top).wait_send()
    window = leaves_ref[0, 0:1, 0:1] >> 3
    table = (leaves_ref[...].reshape(32, 128) - 8 * window).astype(F32).astype(BF16)
    row = iota((BOXES, 128), 0)
    box_ref[...] = ((row & 7) << 6) + (row & 56) + (row >> 6)

    def arrived(group, count):
        pltpu.make_async_remote_copy(
            src_ref=send_ref.at[pl.ds(0, count)],
            dst_ref=recv_ref.at[pl.ds(0, count)],
            send_sem=points_sem,
            recv_sem=group_sems.at[group],
            device_id={"pts": partner, "top": top},
            device_id_type=MESH,
        ).wait_recv()

    def gather(step, carry):
        lax.fori_loop(5 * step, 5 * step + 5, widen, 0)
        far_half = step // 2
        across = lax.rem(x + far_half + far_half // 2 - 2 * (far_half // 3), 4)
        index = 2 * across + lax.rem(y // 2 + step, 2)

        @pl.when(step == 0)
        def _():
            arrived(index, 15)

        @pl.when(step > 0)
        def _():
            arrived(index, 16)

        cols = pl.ds(pl.multiple_of(index * CHUNK, CHUNK), CHUNK)
        start = index * (CHUNK // 128)
        for pair in range(3):
            batch_ref[...] = recv_ref[pl.ds(16 * index, 16), pair, :]
            tiles = mix(batch_ref[pl.ds(0, 8, stride=2), :], batch_ref[pl.ds(1, 8, stride=2), :])
            rows = pl.ds(pl.multiple_of(8 * index, 8), 8)
            tab_ref[2 * pair, rows] = tiles[0]
            tab_ref[2 * pair + 1, rows] = tiles[1]
        place = row_of(tab_ref, 3, start).astype(jnp.int32) - 1
        rows = dot_nn(table, onehot(iota((128, CHUNK), 0) == (place & 127)))
        leaf = jnp.sum(
            jnp.where(iota((32, CHUNK), 0) == (place >> 7), rows, 0.0), axis=0, keepdims=True
        ).astype(jnp.int32)
        code = (leaf & 7) * WIN + (leaf >> 3)
        pick = rows_equal(256, code)
        picks_ref[:, cols] = pick
        kernel = green(tab_ref, edge_ref, surf_ref, start)
        green_ref[:, cols] = kernel
        weighted = []
        for dens in range(2):
            value = kernel * (row_of(tab_ref, 4 + dens, start) * FACTOR)
            high = value.astype(BF16).astype(F32)
            weighted += [high, value - high]
        sums_ref[...] += dot_nt(jnp.concatenate(weighted, axis=0).astype(BF16), pick)
        return carry

    lax.fori_loop(0, COLS // CHUNK, gather, 0)
    eye = onehot(iota((256, 256), 0) == iota((256, 256), 1))
    for dens in range(2):
        base = 2 * COEF * dens
        total = sums_ref[base : base + COEF] + sums_ref[base + COEF : base + 2 * COEF]
        hi, mid, rest = split3(total)
        turned = dot_nt(eye, hi) + dot_nt(eye, mid) + dot_nt(eye, rest)
        order_ref[:, dens] = turned.reshape(8, WIN, COEF)
    leaf_mult = nt3(order_ref[...].reshape(2 * 256, COEF), single_ref.at[0])
    part = nt3(leaf_mult[0:64], up_ref.at[0])
    for octant in range(1, 8):
        part = part + nt3(leaf_mult[64 * octant : 64 * octant + 64], up_ref.at[octant])
    pad_ref[:, 0:COEF] = part
    lane = iota((16, 128), 1)
    tail = jnp.where(
        lane == 96,
        (window >> 3).astype(F32),
        jnp.where(lane == 97, (window & 7).astype(F32), 0.0),
    )
    for group in range(4):
        piece = pad_ref[16 * group : 16 * group + 16, 128:256]
        tail = tail + (pltpu.roll(piece, TAIL * group, 1) if group else piece)
    gath_ref[own, 0:64] = pad_ref[:, 0:128].astype(BF16)
    gath_ref[own, 64:80] = tail.astype(BF16)

    def copy(place, sems, index, target):
        return pltpu.make_async_remote_copy(
            src_ref=gath_ref.at[place],
            dst_ref=gath_ref.at[place],
            send_sem=sems[0].at[index],
            recv_sem=sems[1].at[index],
            device_id={"pts": target},
            device_id_type=MESH,
        )

    far = (send_sem, recv_sem)
    near = (pass_sem, take_sem)
    copy(own, near, 0, partner).start()
    for step in range(1, 16):
        copy(own, far, step, other(step, 1, core)).start()

    row64 = iota((64, 1), 0)
    target = (window + (row64 & 31)) & (BOXES - 1)
    digits = [target & 7, (target >> 3) & 7, target >> 6]
    rise = part.astype(BF16).astype(F32)
    for digit in digits:
        total = None
        for o in range(8):
            term = nt3(jnp.where(digit == o, rise, 0.0), up_ref.at[o])
            total = term if total is None else total + term
        rise = total
    pad_ref[:, 0:COEF] = rise
    for dens in range(2):
        total = jnp.sum(pad_ref[WIN * dens : WIN * dens + WIN], axis=0, keepdims=True)
        roots_ref[own, dens : dens + 1, :] = total[:, 0:128]
        roots_ref[own, 2 + dens : 3 + dens, :] = total[:, 128:256]

    def tell(step, carry):
        pltpu.make_async_remote_copy(
            src_ref=roots_ref.at[own],
            dst_ref=roots_ref.at[own],
            send_sem=root_sems.at[0],
            recv_sem=root_sems.at[1],
            device_id={"pts": lax.rem(own + step, OWNERS)},
            device_id_type=MESH,
        ).start()
        return carry

    lax.fori_loop(1, OWNERS, tell, 0)
    prepare(l2l_ref, down_ref)
    for step in range(1, 16):
        place = other(step, -1, core)
        copy(place, far, step, partner).wait_recv()
        copy(place, near, step, partner).start()
    told = pltpu.make_async_remote_copy(
        src_ref=roots_ref.at[pl.ds(0, OWNERS - 1)],
        dst_ref=roots_ref.at[pl.ds(0, OWNERS - 1)],
        send_sem=root_sems.at[0],
        recv_sem=root_sems.at[1],
        device_id={"pts": partner},
        device_id_type=MESH,
    )
    told.wait_recv()
    root = jnp.sum(roots_ref[...], axis=0)
    root = jnp.concatenate([root[0:2], root[2:4, 0:TAIL]], axis=1)
    fall = jnp.where(row64 < WIN, root[0:1], root[1:2])
    fall = nt3(fall, single_ref.at[2])
    for digit in digits[::-1]:
        total = None
        for o in range(8):
            term = nt3(jnp.where(digit == o, fall, 0.0), down_ref.at[o])
            total = term if total is None else total + term
        fall = total
    copy(partner, near, 0, partner).wait_recv()
    for step in range(1, 16):
        copy(other(step, -1, 1 - core), near, step, partner).wait_recv()

    eye = onehot(iota((COEF, COEF), 0) == iota((COEF, COEF), 1))
    codes = gath_ref[:, 64, :].astype(F32)
    lane = iota((OWNERS, 128), 1)
    first = jnp.sum(
        jnp.where(lane == 96, 8.0 * codes, jnp.where(lane == 97, codes, 0.0)),
        axis=1,
        keepdims=True,
    )
    spread = jnp.where(iota((OWNERS, 512), 0) == (iota((OWNERS, 512), 1) >> 4), first, 0.0)
    start = jnp.sum(spread, axis=0, keepdims=True).astype(jnp.int32)
    start = start + (iota((1, 512), 1) & 15)

    def boxes(width):
        return jnp.concatenate([box_ref[...]] * (width // 128), axis=1)

    halves = []
    for half in range(2):
        place = onehot(boxes(512) == start + 16 * half)
        pieces = [
            gath_ref[:, 32 * dens + 16 * half : 32 * dens + 16 * half + 16, :].reshape(512, 128)
            for dens in range(2)
        ]
        pieces.append(gath_ref[:, 64:80, :].reshape(512, 128))
        halves.append(dot_nn(place, jnp.concatenate(pieces, axis=1)))
    low = []
    for dens in range(2):
        main = slice(128 * dens, 128 * dens + 128)
        tail = 256 + 2 * TAIL * dens
        value = jnp.concatenate(
            [
                halves[0][:, main] + halves[1][:, main],
                halves[0][:, tail : tail + TAIL] + halves[1][:, tail + TAIL : tail + 2 * TAIL],
            ],
            axis=1,
        )
        low.append(dot_nt(eye, value.astype(BF16)))
    low_ref[...] = jnp.concatenate(low, axis=0).astype(BF16)
    fall_ref[...] = fall

    spot = (window + (iota((1, 256), 1) & 31)) & (BOXES - 1)
    masks = (0o444, 0o222, 0o111)
    based = [spot | (-1 - mask) for mask in masks]

    def build(index, carry):
        lines = []
        for part in range(2):
            shifts = shift_ref[2 * index + part]
            nbr = shifts[3:4]
            for dim in range(3):
                nbr = nbr | ((based[dim] + shifts[dim : dim + 1]) & masks[dim])
            lines.append(nbr)
        pick = onehot(boxes(512) == jnp.concatenate(lines, axis=1))
        found = dot_nn(low_ref[...], pick)
        tiles = []
        for part in range(4):
            lanes = slice(128 * part, 128 * part + 128)
            tiles.append(jnp.concatenate([found[0:COEF, lanes], found[COEF:, lanes]], axis=1))
        both = jnp.concatenate(tiles, axis=0).astype(BF16)
        src_ref[pl.ds(pl.multiple_of(128 + index * 608, 16), 608)] = both
        return carry

    lax.fori_loop(0, CLASS // 4, build, 0)

    acc_ref[...] = jnp.zeros_like(acc_ref)

    def mult(index, carry):
        for r in range(4):
            lhs = []
            for m in range(4):
                chunk = 375 * r + 95 * m + index * 8
                lhs.append(
                    jnp.concatenate(
                        [wide_ref[pl.ds(chunk + q, GPAD, stride=CHUNKS), :] for q in range(8)],
                        axis=1,
                    )
                )
            begin = pl.multiple_of(128 - 32 * r + index * 1024, 32)
            acc_ref[r] += dot_nn(
                jnp.concatenate(lhs, axis=0).astype(BF16), src_ref[pl.ds(begin, 1024)]
            )
        return carry

    lax.fori_loop(0, 12, mult, 0)
    block = (iota((1, 256), 1) >> 5) & 3
    for r in range(4):
        value = None
        for m in range(4):
            term = jnp.where(block == m, acc_ref[r, GPAD * m : GPAD * m + GROUPS], 0.0)
            value = term if value is None else value + term
        for half in range(2):
            lanes = slice(128 * half, 128 * half + 128)
            check_ref[half, pl.ds(r, GROUPS, stride=4), :] = value[:, lanes]
    lane = iota((64, 256), 1)
    row64 = iota((64, 1), 0)
    eye = onehot(iota((COEF, COEF), 0) == iota((COEF, COEF), 1))
    fold = onehot(((lane & 31) == (row64 & 31)) & ((lane >> 7) == (row64 >> 5)))
    hi, mid, rest = split3(jnp.concatenate([check_ref[0], check_ref[1]], axis=1))
    checks = dot_nt(fold, hi) + dot_nt(fold, mid) + dot_nt(fold, rest)
    local = nt3(checks, single_ref.at[1]) + fall_ref[...]
    leaves = [nt3(local, down_ref.at[o]) for o in range(8)]
    found = []
    for dens in range(2):
        value = jnp.concatenate([leaf[WIN * dens : WIN * dens + WIN] for leaf in leaves], axis=0)
        found.append(dot_nt(eye, (value * FACTOR).astype(BF16)))
    leaf_mat_ref[...] = jnp.concatenate(found, axis=0).astype(BF16)

    def spread_out(index, home):
        cols = pl.ds(pl.multiple_of(index * CHUNK, CHUNK), CHUNK)
        kernel = green_ref[:, cols]
        found = dot_nn(leaf_mat_ref[...], picks_ref[:, cols])
        for dens in range(2):
            value = found[COEF * dens : COEF * dens + COEF]
            line = jnp.sum(kernel * value, axis=0, keepdims=True)
            for q in range(CHUNK // 128):
                pot_ref[dens, q : q + 1, :] = line[:, 128 * q : 128 * q + 128]
        even, odd = mix(pot_ref[0], pot_ref[1])
        batch_ref[pl.ds(0, 8, stride=2), :] = even
        batch_ref[pl.ds(1, 8, stride=2), :] = odd
        reply_ref[pl.ds(16 * index, 16)] = batch_ref[...].reshape(16, 1, 128)
        for place in range(4):
            for column in range(TOP):
                block = 16 * index + TOP * place + column
                send = pltpu.make_async_remote_copy(
                    src_ref=reply_ref.at[block],
                    dst_ref=back_ref.at[me],
                    send_sem=reply_sems.at[0],
                    recv_sem=reply_sems.at[1],
                    device_id={"pts": 4 * index + place, "top": column},
                    device_id_type=MESH,
                )
                if home:
                    pl.when(block != me)(send.start)
                else:
                    send.start()

    def answer(step, carry):
        turned = 7 - step
        far_half = turned // 2
        across = lax.rem(x + far_half + far_half // 2 - 2 * (far_half // 3), 4)
        spread_out(2 * across + lax.rem(y // 2 + turned, 2), False)
        return carry

    me = TOP * own + top
    lax.fori_loop(0, 7, answer, 0)
    spread_out(own // 4, True)
    back_ref[me] = reply_ref[me]
    replies = pltpu.make_async_remote_copy(
        src_ref=reply_ref.at[pl.ds(0, DEVS - 1)],
        dst_ref=back_ref.at[pl.ds(0, DEVS - 1)],
        send_sem=reply_sems.at[0],
        recv_sem=reply_sems.at[1],
        device_id={"pts": partner, "top": top},
        device_id_type=MESH,
    )
    points.wait_send()
    copy(own, near, 0, partner).wait_send()
    for step in range(1, 16):
        copy(own, far, step, partner).wait_send()
        copy(other(step, -1, core), near, step, partner).wait_send()
    told.wait_send()
    replies.wait_recv()
    tmp_ref[...] = back_ref[...].reshape(DEVS, 128)
    for column in range(TOP):
        tiles = mix(
            tmp_ref[pl.ds(column, 16, stride=8), :],
            tmp_ref[pl.ds(TOP + column, 16, stride=8), :],
        )
        for dens in range(2):
            rows_ref[pl.ds(2 * column + dens, 16, stride=8), :] = tiles[dens]
    value = jnp.concatenate([rows_ref[8 * j : 8 * j + 8] for j in range(16)], axis=1)
    hi = value.astype(BF16).astype(F32)
    mid = (value - hi).astype(BF16).astype(F32)
    pieces = jnp.concatenate([hi, mid, value - hi - mid], axis=0).astype(BF16)
    total = None
    for block in range(8):
        pick = rows_equal(256, where_ref[...], 256 * block)
        term = dot_nn(pieces[:, 256 * block : 256 * block + 256], pick)
        total = term if total is None else total + term
    out_ref[...] = total

    replies.wait_send()


def per_device(
    local_pos, densities, morton_slot, slot_leaf, uc2e, m2m, m2l_ops, dc2e, lattice, l2l
):
    vmem, sem = pltpu.VMEM, pltpu.SemaphoreType.DMA
    pieces = pl.pallas_call(
        fmm_kernel,
        out_shape=jax.ShapeDtypeStruct((24, PTS), F32),
        in_specs=[pl.BlockSpec(memory_space=pl.ANY)] * 13,
        out_specs=pl.BlockSpec(memory_space=VM),
        scratch_shapes=[
            vmem((3, PTS), F32),
            vmem((8, PTS), F32),
            vmem((1, PTS), jnp.int32),
            vmem((8, 128), jnp.int32),
            vmem((1444, 128), F32),
            vmem((1444, 128), F32),
            vmem((COEF, COEF), F32),
            vmem((COEF, COEF), F32),
            vmem((COEF, COEF), F32),
            vmem((8, 128), F32),
            vmem((COEF, 80), BF16),
            vmem((CLASS // 2, 4, 256), jnp.int32),
            sem((12,)),
            vmem((1, PTS), jnp.int32),
            vmem((256, COLS), BF16),
            vmem((16, PTS), F32),
            vmem((DEVS, 3, 128), F32),
            vmem((DEVS, 3, 128), F32),
            vmem((TOP, 8, 128), jnp.int32),
            vmem((1216, 128), F32),
            vmem((1216, 128), F32),
            vmem((8, 2, COEF, COEF), BF16),
            vmem((8, 2, COEF, COEF), BF16),
            vmem((3, 2, COEF, COEF), BF16),
            vmem((DEPTH, PIECE, 128), BF16),
            vmem((WIDE, 128), F32),
            sem((DEPTH,)),
            vmem((6, 64, 128), F32),
            vmem((16, 128), F32),
            vmem((COEF, COLS), F32),
            vmem((4 * COEF, 256), F32),
            vmem((8, 2, WIN, COEF), F32),
            vmem((2 * WIN, 256), F32),
            vmem((128, 128), F32),
            vmem((OWNERS, 80, 128), BF16),
            vmem((OWNERS, 4, 128), F32),
            vmem((BROWS + 384, 256), BF16),
            vmem((4, 4 * GPAD, 256), F32),
            vmem((2, COEF, 128), F32),
            vmem((BOXES, 128), jnp.int32),
            vmem((2 * COEF, BOXES), BF16),
            vmem((2 * WIN, COEF), F32),
            vmem((2 * COEF, 256), BF16),
            vmem((2, 8, 128), F32),
            vmem((128, 128), F32),
            vmem((DEVS, 1, 128), F32),
            vmem((DEVS, 1, 128), F32),
            sem,
            sem((8,)),
            sem((TOP,)),
            sem((TOP,)),
            sem((16,)),
            sem((16,)),
            sem((16,)),
            sem((16,)),
            sem((2,)),
            sem((2,)),
        ],
        compiler_params=pltpu.CompilerParams(
            vmem_limit_bytes=67_000_000, collective_id=0, has_side_effects=True
        ),
        name="fmm",
    )(
        local_pos,
        densities,
        morton_slot.reshape(1, PTS),
        slot_leaf.reshape(8, 128),
        m2m.reshape(1444, 128),
        l2l.reshape(1444, 128),
        uc2e,
        dc2e,
        lattice,
        edge_values(),
        surface_picks(),
        shift_rows(),
        m2l_ops.reshape(GROUPS * CHUNKS, 128),
    )
    return pieces[0:8] + pieces[8:16] + pieces[16:24]


def solution(mesh):
    placed = (
        P(None, ("pts", "top")),
        P(None, ("pts", "top")),
        P(("pts", "top")),
        P(("pts", "top")),
        P(),
        P(),
        P(),
        P(),
        P(),
        P(),
    )
    return jax.shard_map(
        per_device, mesh=mesh, in_specs=placed, out_specs=P(None, ("pts", "top")), check_vma=False
    )
```
